32 devices in a mesh: cls: 4 (over x, core), draw: 8 (over z, y).
Axes of the slice: x: 2, y: 2, z: 4, core: 2. Of those that a mesh axis runs over, the one named last changes fastest.
Arguments:
- features: bfloat16 [128, 1024], replicated, may hold values from -128 to 128
- mean_head: bfloat16 [1024, 21888], P('draw', 'cls'), may hold values from -1 to 1
- scale_head: bfloat16 [1024, 21888], P('draw', 'cls'), may hold values from -1 to 1
- factor: bfloat16 [21888, 50], P('cls'), may hold values from -0.875 to 0.875
- noise: bfloat16 [16, 128, 50], P('draw'), may hold values from -5 to 5
- labels: float32 [128, 21888], P(None, 'cls'), may hold values from 0 to 1, as said below
Outputs:
- mean_grad: float32 [1024, 21888], P('draw', 'cls')
- scale_grad: float32 [1024, 21888], P('draw', 'cls')
- feature_grad: float32 [128, 1024], P(None, 'draw')
The draws below stay inside these ranges and needn't reach their ends.
Inputs may be any that keep to these rules, and one draw needn't show every extreme that they name: `labels`: each row is nonnegative, sums to one, and is zero on the last 45 classes.
All inputs are finite; a program needn't handle non-finite values.
Results may differ from the reference program's by a relative error of at most 0.0028.
Values may be sent and summed in bfloat16 or wider, within the bound.
A program may use at most 320 MiB of HBM per device.

```python
import math
import jax
import jax.numpy as jnp
from jax import lax

B = 128
D = 1024
C = 21888
R = 50
CREAL = 21843
S = 16


def head_pair(key):
    norm_scale = 1.0 / math.sqrt(D)
    mean_weight = jax.random.truncated_normal(jax.random.fold_in(key, 11), -6.0, 6.0, (D, C), jnp.float32) * norm_scale
    scale_weight = jax.random.truncated_normal(jax.random.fold_in(key, 12), -6.0, 6.0, (D, C), jnp.float32) * norm_scale
    return (mean_weight.astype(jnp.bfloat16), scale_weight.astype(jnp.bfloat16))


def draw_mean_head(key, part):
    return head_pair(key)[0]


def draw_scale_head(key, part):
    return head_pair(key)[1]


def draw_features(key, part):
    return jax.random.truncated_normal(jax.random.fold_in(key, 20), -6.0, 6.0, (B, D), jnp.float32).astype(jnp.bfloat16)


def draw_labels(key, part):
    logits = 2.0 * jax.random.normal(key, (B, C), jnp.float32)
    valid = jnp.arange(C) < CREAL
    weights = jnp.where(valid[None, :], jnp.exp(logits - jnp.max(logits, axis=1, keepdims=True)), 0.0)
    return (weights / jnp.sum(weights, axis=1, keepdims=True)).astype(jnp.float32)


def levels(rng, extent, cuts, smallest, high):
    gain, own = 1.0, jax.random.fold_in(rng, 6)
    for position, blocks in cuts:
        heights = jnp.exp(jax.random.uniform(jax.random.fold_in(own, position), (blocks,), jnp.float32, smallest / len(cuts), high / len(cuts)))
        gain = gain * jnp.repeat(heights, extent[position] // blocks).reshape([-1 if axis == position else 1 for axis in range(len(extent))])
    return gain


def scatter_about(stream_key, dims, scale, bound, cuts=(), held_as=jnp.bfloat16):
    entries = scale * jax.random.normal(stream_key, dims, jnp.float32)
    if cuts:
        entries = entries * levels(stream_key, dims, cuts, -0.22, 0.18)
    return jnp.clip(entries, -bound, bound).astype(held_as)


def setup_inputs(seed: int = 0) -> dict:
    arg_keys = jax.random.split(jax.random.key(seed), 7)
    features = draw_features(jax.random.fold_in(arg_keys[6], 71), 0)
    mean_head = draw_mean_head(jax.random.fold_in(arg_keys[6], 71), 0)
    scale_head = draw_scale_head(jax.random.fold_in(arg_keys[6], 71), 0)
    factor = scatter_about(arg_keys[3], (C, R), R ** -0.5, 0.875, ((0, 4),))
    noise = scatter_about(arg_keys[4], (S, B, R), 1.0, 5.0, ((0, 8),))
    labels = draw_labels(jax.random.fold_in(arg_keys[6], 71), 0)
    return dict(features=features, mean_head=mean_head, scale_head=scale_head, factor=factor, noise=noise, labels=labels)


def reference(features, mean_head, scale_head, factor, noise, labels):
    mean_logit = jnp.dot(features.astype(jnp.float32), mean_head.astype(jnp.float32), preferred_element_type=jnp.float32)
    scale_pre = jnp.dot(features.astype(jnp.float32), scale_head.astype(jnp.float32), preferred_element_type=jnp.float32)
    spread = jax.nn.softplus(scale_pre)
    class_ids = jnp.arange(C, dtype=jnp.int32)
    shift = jnp.where(class_ids >= CREAL, 30000.0, 0.0).astype(jnp.float32)
    factor_t = factor.T

    def noisy(sample):
        lowrank = jnp.dot(sample.astype(jnp.float32), factor_t.astype(jnp.float32), preferred_element_type=jnp.float32)
        return (lowrank, mean_logit + spread * lowrank - shift[None, :])

    def logprob(sample):
        lowrank, logits = noisy(sample)
        row_max = jnp.max(logits, axis=1)
        total = jnp.sum(jnp.exp(logits - row_max[:, None]), axis=1)
        return (lowrank, logits - (row_max + jnp.log(total))[:, None])

    def first_pass(carry, sample):
        best, summed = carry
        lowrank, logp = logprob(sample)
        top = jnp.maximum(best, logp)
        summed = summed * jnp.exp(best - top) + jnp.exp(logp - top)
        return ((top, summed), None)
    start = (jnp.full((B, C), -jnp.inf, jnp.float32), jnp.zeros((B, C), jnp.float32))
    (best, summed), _ = lax.scan(first_pass, start, noise)
    mix = best + jnp.log(summed)

    def second_pass(carry, sample):
        dmean, dspread = carry
        lowrank, logp = logprob(sample)
        ratio = jnp.exp(logp - mix)
        dots = jnp.sum(labels * ratio, axis=1)
        dz = (jnp.exp(logp) * dots[:, None] - labels * ratio) / B
        return ((dmean + dz, dspread + dz * lowrank), None)
    zeros = jnp.zeros((B, C), jnp.float32)
    (dmean, dspread), _ = lax.scan(second_pass, (zeros, zeros), noise)
    mean_cot = dmean.astype(jnp.bfloat16)
    scale_cot = (dspread * jax.nn.sigmoid(scale_pre)).astype(jnp.bfloat16)
    mean_grad = jnp.dot(features.T.astype(jnp.float32), mean_cot.astype(jnp.float32), preferred_element_type=jnp.float32)
    scale_grad = jnp.dot(features.T.astype(jnp.float32), scale_cot.astype(jnp.float32), preferred_element_type=jnp.float32)
    feature_grad = jnp.dot(mean_cot.astype(jnp.float32), mean_head.T.astype(jnp.float32), preferred_element_type=jnp.float32) + jnp.dot(scale_cot.astype(jnp.float32), scale_head.T.astype(jnp.float32), preferred_element_type=jnp.float32)
    return (mean_grad, scale_grad, feature_grad)
```

```python
import functools
import jax
import jax.numpy as jnp
from jax import lax
from jax.experimental import pallas as pl
from jax.experimental.pallas import tpu as pltpu
from jax.sharding import PartitionSpec as P

CREAL = 21843
UNIT = 16
MESH = pl.DeviceIdType.MESH
ANY = pl.BlockSpec(memory_space=pl.ANY)
VMEM = pl.BlockSpec(memory_space=pltpu.VMEM)


def start_of(owner, n, units):
    return lax.div(owner * units, n)


def at_width(owner, n, units, run):
    base = units // n
    wide = start_of(owner + 1, n, units) - start_of(owner, n, units) > base
    pl.when(wide)(functools.partial(run, (base + 1) * UNIT))
    pl.when(jnp.logical_not(wide))(functools.partial(run, base * UNIT))


def exchange_kernel(
    n, units, feat, mean, scale, noise, logits, noise_out, held, part_out, part_in,
    send, recv, part_send, part_recv, nsend, nrecv, local, nlocal,
):
    me, cls = lax.axis_index("draw"), lax.axis_index("cls")
    half, rows = n // 2, mean.shape[1]
    mirror = lax.rem(me + half, n)
    base, spot = lax.div(me, half) * half, lax.rem(me, half)
    barrier = pltpu.get_barrier_semaphore()
    for k in range(1, n):
        pl.semaphore_signal(barrier, inc=1, device_id=(cls, lax.rem(me + k, n)), device_id_type=MESH)
    pl.semaphore_wait(barrier, n - 1)

    def remote(source, target, send_sem, recv_sem, device):
        return pltpu.make_async_remote_copy(
            source, target, send_sem, recv_sem, device_id=(cls, device), device_id_type=MESH
        )

    def noise_copy(slot, k, device):
        return remote(noise, noise_out.at[slot], nsend.at[k], nrecv.at[slot], device)

    def block(head, owner, width):
        start = pl.multiple_of(start_of(owner, n, units) * UNIT, UNIT)
        return (mean, scale)[head].at[pl.ds(start, width)]

    def block_copy(far, head, owner, k, source, device, act):
        at_width(
            owner, n, units,
            lambda w: act(
                remote(
                    block(head, owner, w), held.at[far, head, source, pl.ds(0, w)],
                    send.at[far, head, k], recv.at[far, head, source], device,
                )
            ),
        )

    def own_copy(far, head, act):
        owner = mirror if far else me
        at_width(
            owner, n, units,
            lambda w: act(
                pltpu.make_async_copy(
                    block(head, owner, w), held.at[far, head, spot, pl.ds(0, w)], local.at[far, head]
                )
            ),
        )

    def sends(far, head, act):
        for k in range(1, half):
            peer = base + lax.rem(spot + k, half)
            block_copy(far, head, lax.rem(peer + half, n) if far else peer, k, spot, peer, act)

    def columns_of(source):
        if rows % 128:
            return feat[source]
        return feat[:, pl.ds(pl.multiple_of(source * rows, rows), rows)]

    def arrive(far, head):
        owner = mirror if far else me
        for k in range(1, half):
            source = lax.rem(spot + half - k, half)
            block_copy(far, head, owner, k, source, base + source, lambda c: c.wait_recv())
        own_copy(far, head, lambda c: c.wait())
        total = None
        for source in range(half):
            term = lax.dot_general(
                held[far, head, source], columns_of(base + source), (((1,), (1,)), ((), ())),
                preferred_element_type=jnp.float32,
            )
            total = term if total is None else total + term
        return total

    def part_copy(head):
        return remote(part_out.at[head], part_in.at[head], part_send.at[head], part_recv.at[head], mirror)

    own_noise = pltpu.make_async_copy(noise, noise_out.at[me], nlocal)
    stages = [(1, 0), (1, 1), (0, 0), (0, 1)]
    sends(1, 0, lambda c: c.start())
    for k in range(1, n):
        noise_copy(me, k, lax.rem(me + k, n)).start()
    for far, head in stages[1:]:
        sends(far, head, lambda c: c.start())
    for far, head in stages:
        own_copy(far, head, lambda c: c.start())
    own_noise.start()
    for head in range(2):
        part_out[head] = arrive(1, head)
        part_copy(head).start()
    for head in range(2):
        logits[head] = arrive(0, head)
    for k in range(1, n):
        source = lax.rem(me + n - k, n)
        noise_copy(source, k, source).wait_recv()
    own_noise.wait()
    for head in range(2):
        part_copy(head).wait_recv()
        logits[head] = logits[head] + part_in[head]
    for far, head in stages:
        sends(far, head, lambda c: c.wait_send())
    for k in range(1, n):
        noise_copy(me, k, lax.rem(me + k, n)).wait_send()
    for head in range(2):
        part_copy(head).wait_send()


def gather_kernel(n, units, cot, out, send, recv, local):
    me, cls = lax.axis_index("draw"), lax.axis_index("cls")
    half = n // 2
    group, side = lax.div(me, 2), lax.rem(me, 2)
    partner = group * 2 + 1 - side
    split = units // n // 2 * UNIT
    pieces = [(head, part) for head in range(2) for part in range(2)]
    barrier = pltpu.get_barrier_semaphore()
    peers = [partner] + [lax.rem(group + k, half) * 2 + side for k in range(1, half)]
    for peer in peers:
        pl.semaphore_signal(barrier, inc=1, device_id=(cls, peer), device_id_type=MESH)
    pl.semaphore_wait(barrier, half)

    def source(piece, width):
        head, part = pieces[piece]
        return cot.at[head, pl.ds(split, width - split) if part else pl.ds(0, split)]

    def place(piece, owner, width):
        head, part = pieces[piece]
        start = start_of(owner, n, units) * UNIT + part * split
        return out.at[head, pl.ds(pl.multiple_of(start, UNIT), width - split if part else split)]

    def send_own(piece, owner, slot, device, act):
        at_width(
            owner, n, units,
            lambda w: act(
                pltpu.make_async_remote_copy(
                    source(piece, w), place(piece, owner, w), send.at[slot, piece], recv.at[owner, piece],
                    device_id=(cls, device), device_id_type=MESH,
                )
            ),
        )

    def forward(piece, owner, slot, act):
        at_width(
            owner, n, units,
            lambda w: act(
                pltpu.make_async_remote_copy(
                    place(piece, owner, w), place(piece, owner, w), send.at[slot, piece], recv.at[owner, piece],
                    device_id=(cls, partner), device_id_type=MESH,
                )
            ),
        )

    def own(piece, act):
        at_width(
            me, n, units,
            lambda w: act(pltpu.make_async_copy(source(piece, w), place(piece, me, w), local.at[piece])),
        )

    count = len(pieces)
    for piece in range(count):
        for k in range(1, half):
            send_own(piece, me, k, peers[k], lambda c: c.start())
        send_own(piece, me, 0, partner, lambda c: c.start())
    for piece in range(count):
        own(piece, lambda c: c.start())
    order = sorted(range(1, half), key=lambda k: min(k, half - k))
    for piece in range(count):
        for k in order:
            send_own(piece, peers[k], k, peers[k], lambda c: c.wait_recv())
            forward(piece, peers[k], half + k, lambda c: c.start())
    for piece in range(count):
        send_own(piece, partner, 0, partner, lambda c: c.wait_recv())
        for k in range(1, half):
            owner = lax.rem(group + k, half) * 2 + 1 - side
            forward(piece, owner, half + k, lambda c: c.wait_recv())
    for piece in range(count):
        for k in range(half):
            send_own(piece, me, k, peers[k], lambda c: c.wait_send())
        for k in range(1, half):
            forward(piece, peers[k], half + k, lambda c: c.wait_send())
        own(piece, lambda c: c.wait())


def merge(slots, count, softmax):
    if not softmax:
        total = slots[0]
        for i in range(1, count):
            total = total + slots[i]
        return total
    top = slots[0, 0]
    for i in range(1, count):
        top = jnp.maximum(top, slots[i, 0])
    total = jnp.zeros_like(top)
    for i in range(count):
        total = total + slots[i, 1] * jnp.exp(slots[i, 0] - top)
    return jnp.stack((top, total))


def reduce_kernel(counts, softmax, x, out, *scratch):
    levels = len(counts)
    slots, sends, recvs = scratch[:levels], scratch[levels : 2 * levels], scratch[2 * levels :]
    cls, draw = lax.axis_index("cls"), lax.axis_index("draw")

    def device(level, index):
        return (index, draw) if level == 0 else (cls, index)

    barrier = pltpu.get_barrier_semaphore()
    for level, n in enumerate(counts):
        me = (cls, draw)[level]
        for k in range(1, n):
            pl.semaphore_signal(
                barrier, inc=1, device_id=device(level, lax.rem(me + k, n)), device_id_type=MESH
            )
    pl.semaphore_wait(barrier, sum(counts) - levels)
    value = x[...]
    for level, n in enumerate(counts):
        me = (cls, draw)[level]
        held = slots[level]
        held[me] = value

        def copy(slot, k, target):
            return pltpu.make_async_remote_copy(
                held.at[slot], held.at[slot], sends[level].at[k], recvs[level].at[slot],
                device_id=device(level, target), device_id_type=MESH,
            )

        for k in range(1, n):
            copy(me, k, lax.rem(me + k, n)).start()
        for k in range(1, n):
            source = lax.rem(me + n - k, n)
            copy(source, k, source).wait_recv()
        for k in range(1, n):
            copy(me, k, lax.rem(me + k, n)).wait_send()
        value = merge(held, n, softmax)
    if softmax:
        out[...] = value[0] + jnp.log(value[1])
    else:
        out[...] = value


def params(collective_id, grant=32):
    return pltpu.CompilerParams(
        collective_id=collective_id, has_side_effects=True, vmem_limit_bytes=grant * 2**20
    )


def reduce_over(x, counts, softmax, collective_id):
    shape = x.shape[1:] if softmax else x.shape
    return pl.pallas_call(
        functools.partial(reduce_kernel, counts, softmax),
        out_shape=jax.ShapeDtypeStruct(shape, jnp.float32),
        in_specs=[VMEM],
        out_specs=VMEM,
        scratch_shapes=[pltpu.VMEM((n,) + x.shape, jnp.float32) for n in counts]
        + [pltpu.SemaphoreType.DMA((n,)) for n in counts]
        + [pltpu.SemaphoreType.DMA((n,)) for n in counts],
        compiler_params=params(collective_id),
    )(x)


def on_device(features, mean_head, scale_head, factor, noise, labels):
    rows, columns = mean_head.shape
    batch = features.shape[0]
    n, ncls = lax.axis_size("draw"), lax.axis_size("cls")
    me = lax.axis_index("draw")
    units = columns // UNIT
    tile = -(-units // n) * UNIT
    own, rank = noise.shape[0], noise.shape[2]
    draws = own * n
    mean_rows, scale_rows = mean_head.T, scale_head.T
    half = n // 2
    feat = features.reshape(batch, n, rows).transpose(1, 0, 2) if rows % 128 else features

    heads, noise_t = pl.pallas_call(
        functools.partial(exchange_kernel, n, units),
        out_shape=(
            jax.ShapeDtypeStruct((2, tile, batch), jnp.float32),
            jax.ShapeDtypeStruct((n, own, rank, batch), jnp.bfloat16),
        ),
        in_specs=[VMEM] + [ANY] * 3,
        out_specs=(VMEM, ANY),
        scratch_shapes=[
            pltpu.VMEM((2, 2, half, tile, rows), jnp.bfloat16),
            pltpu.VMEM((2, tile, batch), jnp.float32),
            pltpu.VMEM((2, tile, batch), jnp.float32),
            pltpu.SemaphoreType.DMA((2, 2, half)),
            pltpu.SemaphoreType.DMA((2, 2, half)),
            pltpu.SemaphoreType.DMA((2,)),
            pltpu.SemaphoreType.DMA((2,)),
            pltpu.SemaphoreType.DMA((n,)),
            pltpu.SemaphoreType.DMA((n,)),
            pltpu.SemaphoreType.DMA((2, 2)),
            pltpu.SemaphoreType.DMA,
        ],
        compiler_params=params(0),
    )(feat, mean_rows, scale_rows, noise.transpose(0, 2, 1))

    first = start_of(me, n, units) * UNIT
    width = start_of(me + 1, n, units) * UNIT - first
    offsets = jnp.arange(tile, dtype=jnp.int32)[:, None]
    valid = offsets < width
    class_ids = lax.axis_index("cls") * columns + first + offsets
    shift = jnp.where(class_ids >= CREAL, 30000.0, 0.0).astype(jnp.float32)
    my_factor = lax.dynamic_slice_in_dim(factor.T, first, tile, 1)
    my_labels = jnp.where(valid, lax.dynamic_slice_in_dim(labels.T, first, tile, 0), 0.0)

    mean_logit, scale_pre = heads[0], heads[1]
    scale_pre = jnp.where(valid, scale_pre, 0.0)
    spread = jax.nn.softplus(scale_pre)
    lowrank = jnp.einsum(
        "rc,srb->scb", my_factor, noise_t.reshape(draws, rank, batch), preferred_element_type=jnp.float32
    )
    logits = mean_logit[None] + spread[None] * lowrank - shift[None]
    logits = jnp.where(valid[None], logits, -1e30)
    local_top = jnp.max(logits, axis=1)
    local_total = jnp.sum(jnp.exp(logits - local_top[:, None]), axis=1)
    lse = reduce_over(jnp.stack((local_top, local_total)), (ncls, n), True, 1)
    log_prob = logits - lse[:, None]
    best = jnp.max(log_prob, axis=0)
    risen = jnp.exp(log_prob - best[None])
    inverse = 1.0 / jnp.sum(risen, axis=0)
    weight = my_labels * inverse
    label_dot = reduce_over(jnp.sum(weight[None] * risen, axis=1), (ncls, n), False, 2)
    logit_cot = risen * ((jnp.exp(best) / batch)[None] * label_dot[:, None] - (weight / batch)[None])
    dmean = jnp.sum(logit_cot, axis=0)
    dspread = jnp.sum(logit_cot * lowrank, axis=0)
    cots = jnp.stack((dmean, dspread * jax.nn.sigmoid(scale_pre))).astype(jnp.bfloat16)

    gathered = pl.pallas_call(
        functools.partial(gather_kernel, n, units),
        out_shape=jax.ShapeDtypeStruct((2, columns, batch), jnp.bfloat16),
        in_specs=[ANY],
        out_specs=ANY,
        scratch_shapes=[
            pltpu.SemaphoreType.DMA((n, 4)),
            pltpu.SemaphoreType.DMA((n, 4)),
            pltpu.SemaphoreType.DMA((4,)),
        ],
        compiler_params=params(3),
    )(cots)
    mean_cot, scale_cot = gathered[0], gathered[1]
    my_columns = lax.dynamic_slice_in_dim(features, me * rows, rows, 1)
    over_classes = (((0,), (0,)), ((), ()))
    feature_part = lax.dot_general(
        mean_cot, mean_rows, over_classes, preferred_element_type=jnp.float32
    ) + lax.dot_general(scale_cot, scale_rows, over_classes, preferred_element_type=jnp.float32)
    mean_grad = jnp.dot(mean_cot, my_columns, preferred_element_type=jnp.float32).T
    scale_grad = jnp.dot(scale_cot, my_columns, preferred_element_type=jnp.float32).T
    feature_grad, step = feature_part, 1
    while step < ncls:
        feature_grad = feature_grad + lax.ppermute(feature_grad, "cls", [(i, i ^ step) for i in range(ncls)])
        step *= 2
    return (mean_grad, scale_grad, feature_grad)


GRAIN = 64
NEG = -1e30


def when(cond, fn):
    pl.when(cond)(fn)


class Plan:
    def __init__(self, batch, rows, columns, rank):
        self.batch, self.rows, self.columns, self.rank = batch, rows, columns, rank
        units = columns // UNIT
        edges = [q * units // 4 * UNIT for q in range(5)]
        widest = max(b - a for a, b in zip(edges, edges[1:]))
        step = 2 * GRAIN
        self.width = -(-widest // step) * step
        self.units = units
        self.extra = max(0, edges[3] + self.width - columns)
        self.starts = edges[:3] + [edges[3] - self.extra]
        self.sizes = [b - a for a, b in zip(self.starts, self.starts[1:] + [columns])]
        self.chunks = self.width // GRAIN
        self.steps = self.chunks // 2

    def start(self, q):
        return pl.multiple_of(lax.div(q * self.units, 4) * UNIT - self.extra * lax.div(q, 3), UNIT)

    def size(self, q):
        after = lax.div((q + 1) * self.units, 4) * UNIT - self.extra * (lax.div(q + 1, 3) - lax.div(q + 1, 4))
        return after - self.start(q)


def tree(fn, items):
    items = list(items)
    while len(items) > 1:
        items = [fn(*items[i : i + 2]) if i + 1 < len(items) else items[i] for i in range(0, len(items), 2)]
    return items[0]


def softmax_kernel(
    plan, draws, ahead, lag_in, lag_out, relay_in, relay_out, late,
    feat, mean, scale, factor, noise, labels, cot, part,
    wbuf, sums, arrived, zbuf, low, gate, weight, peak, fcols, fac, fq, nb, nmat, lab, top, total, lseb, dotb,
    red, far, whole, acc,
    lsem, ysend, yrecv, zsend, zrecv, nsend, nrecv, nstage, nstage_r, rsend, rrecv, fsend, frecv,
    gzs, gzr, gys, gyr, wsem, csend, crecv,
):
    me, cls = lax.axis_index("draw"), lax.axis_index("cls")
    z, y = lax.div(me, 2), lax.rem(me, 2)
    xx, core = lax.div(cls, 2), lax.rem(cls, 2)
    half = lax.div(z, 2)
    outer = (z == 0) | (z == 3)
    inner = jnp.logical_not(outer)
    edge, mid = 3 * half, 1 + half
    across = 2 - half
    batch, rows, chunks, steps = plan.batch, plan.rows, plan.chunks, plan.steps
    own_q = half * 2 + y
    start = plan.start(own_q)
    valid_rows = plan.size(own_q)
    plane = cls * 2 + y
    heads = (mean, scale)

    def at(zi, yi):
        return (cls, zi * 2 + yi)

    def in_plane(p):
        return (lax.div(p, 2), z * 2 + lax.rem(p, 2))

    barrier = pltpu.get_barrier_semaphore()
    for k in range(1, 8):
        pl.semaphore_signal(barrier, inc=1, device_id=in_plane(lax.rem(plane + k, 8)), device_id_type=MESH)
    for k in range(1, 4):
        pl.semaphore_signal(barrier, inc=1, device_id=at(lax.rem(z + k, 4), y), device_id_type=MESH)

    def remote(src, dst, s, r, device):
        return pltpu.make_async_remote_copy(src, dst, s, r, device_id=device, device_id_type=MESH)

    def local_own(e, h):
        return pltpu.make_async_copy(
            heads[h].at[pl.ds(plan.start(e * 2 + y), plan.width)],
            wbuf.at[e, h, :, pl.ds(pl.multiple_of(y * rows, rows), rows)],
            lsem.at[e * 2 + h],
        )

    feat_copy = pltpu.make_async_copy(
        feat.at[:, pl.ds(pl.multiple_of(z * 2 * rows, 2 * rows), 2 * rows)], fcols, lsem.at[4]
    )
    factor_copy = pltpu.make_async_copy(factor, fac, lsem.at[5])
    label_copy = pltpu.make_async_copy(labels.at[pl.ds(start, plan.width)], lab, lsem.at[6])
    noise_own = pltpu.make_async_copy(
        noise.at[core, pl.ds(pl.multiple_of(xx * 32, 32), 32)], nb.at[core, xx, y, z], lsem.at[7]
    )

    def y_copy(e, h, k):
        return remote(
            heads[h].at[pl.ds(plan.start(e * 2 + 1 - y) + k * GRAIN, GRAIN)],
            wbuf.at[e, h, pl.ds(pl.multiple_of(k * GRAIN, GRAIN), GRAIN), pl.ds(pl.multiple_of(y * rows, rows), rows)],
            ysend.at[k, e, h], yrecv.at[k, e, h], at(z, 1 - y),
        )

    def y_landed(e, h, k):
        return remote(
            heads[h].at[pl.ds(plan.start(e * 2 + 1 - y) + k * GRAIN, GRAIN)],
            wbuf.at[
                e, h, pl.ds(pl.multiple_of(k * GRAIN, GRAIN), GRAIN),
                pl.ds(pl.multiple_of((1 - y) * rows, rows), rows),
            ],
            ysend.at[k, e, h], yrecv.at[k, e, h], at(z, 1 - y),
        )

    def y_start(k):
        for e in range(2):
            for h in range(2):
                y_copy(e, h, k).start()

    def z_copy(e, k, target):
        return remote(sums.at[k, e], arrived.at[e, k], zsend.at[e, k], zrecv.at[e, k], at(target, y))

    def noise_copy(e, source):
        return remote(
            noise.at[core, pl.ds(pl.multiple_of(xx * 32, 32), 32)], nb.at[core, xx, y, source],
            nsend.at[e], nrecv.at[source], at(3 * e, y),
        )

    stages = [
        lambda act: act(remote(nb.at[core, xx, y], nb.at[core, xx, y], nstage.at[0], nstage_r.at[0], at(z, 1 - y))),
        lambda act: act(
            remote(nb.at[core, xx], nb.at[core, xx], nstage.at[1], nstage_r.at[1], ((1 - xx) * 2 + core, me))
        ),
        lambda act: act(remote(nb.at[core], nb.at[core], nstage.at[2], nstage_r.at[2], (xx * 2 + 1 - core, me))),
    ]
    landed = [
        lambda act: act(
            remote(nb.at[core, xx, 1 - y], nb.at[core, xx, 1 - y], nstage.at[0], nstage_r.at[0], at(z, 1 - y))
        ),
        lambda act: act(
            remote(
                nb.at[core, 1 - xx], nb.at[core, 1 - xx], nstage.at[1], nstage_r.at[1], ((1 - xx) * 2 + core, me)
            )
        ),
        lambda act: act(
            remote(nb.at[1 - core], nb.at[1 - core], nstage.at[2], nstage_r.at[2], (xx * 2 + 1 - core, me))
        ),
    ]

    feat_copy.start()
    for e in range(2):
        for h in range(2):
            local_own(e, h).start()
    if plan.rank < 64:
        fq[...] = jnp.zeros_like(fq)
    factor_copy.start()
    noise_own.start()
    pl.semaphore_wait(barrier, 10)
    for k in range(ahead):
        y_start(k)
    for e in range(2):
        when(z != 3 * e, lambda: noise_copy(e, z).start())
    label_copy.start()
    top[...] = jnp.full_like(top, NEG)
    total[...] = jnp.zeros_like(total)
    acc[...] = jnp.zeros_like(acc)
    feat_copy.wait()
    for e in range(2):
        for h in range(2):
            local_own(e, h).wait()

    def lanes(s):
        return slice(s * batch, (s + 1) * batch)

    def first_pass(k):
        @pl.when(lax.rem(k, 2) == 0)
        def _():
            low[pl.ds(pl.multiple_of(k * GRAIN, GRAIN), 2 * GRAIN)] = lax.dot_general(
                fq[:, pl.ds(pl.multiple_of(k * GRAIN, 2 * GRAIN), 2 * GRAIN)], nmat[...],
                (((0,), (0,)), ((), ())), preferred_element_type=jnp.float32,
            )
        rows_k = pl.ds(pl.multiple_of(k * GRAIN, GRAIN), GRAIN)
        logit, pre = sums[k, half, 0], sums[k, half, 1]
        offset = k * GRAIN + lax.broadcasted_iota(jnp.int32, (GRAIN, batch), 0)
        valid = offset < valid_rows
        ids = cls * plan.columns + start + offset
        shifted = logit - jnp.where(ids >= CREAL, 30000.0, 0.0)
        fade = jnp.exp(-jnp.abs(pre))
        spread = jnp.maximum(pre, 0.0) + jnp.log1p(fade)
        gate[rows_k] = jnp.where(pre >= 0, 1.0, fade) / (1.0 + fade)
        shifted = jnp.where(valid, shifted, NEG)
        spread = jnp.where(valid, spread, 0.0)
        for s in range(draws):
            value = shifted + spread * low[rows_k, lanes(s)]
            zbuf[rows_k, lanes(s)] = value
            blocks = [value[i * 8 : i * 8 + 8] for i in range(GRAIN // 8)]
            old = top[:, lanes(s)]
            new = jnp.maximum(old, tree(jnp.maximum, blocks))
            grown = tree(jnp.add, [jnp.exp(b - new) for b in blocks])
            total[:, lanes(s)] = total[:, lanes(s)] * jnp.exp(old - new) + grown
            top[:, lanes(s)] = new

    e_first, e_second = 1 - half, half

    def noise_stage(i):
        @pl.when(i == 2)
        def _():
            for k in range(4):
                when(z != k, lambda: noise_copy(half, k).wait_recv())
            noise_own.wait()
            stages[0](lambda c: c.start())

        for n in (1, 2):
            @pl.when(i == 2 + n)
            def _():
                landed[n - 1](lambda c: c.wait_recv())
                stages[n](lambda c: c.start())

        @pl.when(i == 4)
        def _():
            factor_copy.wait()
            for q in range(4):
                def pick(q=q):
                    fq[: plan.rank] = fac[:, plan.starts[q] : plan.starts[q] + plan.width]
                when(own_q == q, pick)

        @pl.when(i == 5)
        def _():
            landed[2](lambda c: c.wait_recv())
            for j in range(2):
                for yi in range(2):
                    for zi in range(4):
                        s = (j * 2 + yi) * 4 + zi
                        for h in range(2):
                            nmat[h * 32 : h * 32 + 32, lanes(s)] = nb[j, h, yi, zi]

    def forward(i, carry):
        when(i + ahead < chunks, lambda: y_start(i + ahead))
        when(outer, lambda: noise_stage(i))

        @pl.when(i < chunks)
        def _():
            for e in range(2):
                for h in range(2):
                    y_landed(e, h, i).wait_recv()
            block = pl.ds(pl.multiple_of(i * GRAIN, GRAIN), GRAIN)
            lhs = jnp.concatenate([wbuf[e, h, block] for e in range(2) for h in range(2)], axis=0)
            value = lax.dot_general(
                lhs, fcols[...], (((1,), (1,)), ((), ())), preferred_element_type=jnp.float32
            )
            sums[i] = value.reshape(2, 2, GRAIN, batch)

            @pl.when(inner)
            def _():
                z_copy(e_first, i, mid).wait_recv()
                sums[i, e_first] = sums[i, e_first] + arrived[e_first, i]
            z_copy(e_first, i, jnp.where(outer, mid, across)).start()

        k_in = i - lag_in
        @pl.when(inner & (k_in >= 0) & (k_in < chunks))
        def _():
            z_copy(e_second, k_in, mid).wait_recv()
            sums[k_in, e_second] = sums[k_in, e_second] + arrived[e_second, k_in]
            z_copy(e_second, k_in, edge).start()

        k_out = i - lag_out
        @pl.when(outer & (k_out >= 0))
        def _():
            z_copy(e_second, k_out, mid).wait_recv()
            sums[k_out, e_second] = sums[k_out, e_second] + arrived[e_second, k_out]
            first_pass(k_out)
        return carry

    lax.fori_loop(0, chunks + lag_out, forward, 0)
    whole_copies = [pltpu.make_async_copy(heads[h], whole.at[h], wsem.at[h]) for h in range(2)]
    for copy in whole_copies:
        copy.start()
    label_copy.wait()

    @pl.when(inner)
    def _():
        factor_copy.wait()
        noise_own.wait()

    def spread_values(kind):
        def copy(slot, k, device):
            return remote(red.at[kind, slot], red.at[kind, slot], rsend.at[kind, k], rrecv.at[kind, slot], device)
        for k in range(1, 8):
            copy(plane, k, in_plane(lax.rem(plane + k, 8))).start()
        for k in range(1, 8):
            source = lax.rem(plane + 8 - k, 8)
            copy(source, k, in_plane(source)).wait_recv()
        parts = [red[kind, p] for p in range(8)]
        return parts

    def far_copy(kind, slot):
        return remote(
            far.at[kind, slot], far.at[kind, slot], fsend.at[kind], frecv.at[kind], at(3 - z, y)
        )

    def log_merge(parts):
        best = tree(jnp.maximum, parts)
        return best + jnp.log(tree(jnp.add, [jnp.exp(p - best) for p in parts]))

    def fan_out(target, value):
        for s in range(draws):
            target[:, lanes(s)] = jnp.broadcast_to(value[s : s + 1], (8, batch))

    def reduce_all(kind, merge):
        far[kind, half] = merge(spread_values(kind))
        far_copy(kind, half).start()
        far_copy(kind, 1 - half).wait_recv()
        return merge([far[kind, 0], far[kind, 1]])

    @pl.when(outer)
    def _():
        for s in range(draws):
            m = top[:, lanes(s)]
            best = jnp.max(m, axis=0, keepdims=True)
            size = jnp.sum(total[:, lanes(s)] * jnp.exp(m - best), axis=0, keepdims=True)
            red[0, plane, s : s + 1, :] = best + jnp.log(size)
        fan_out(lseb, reduce_all(0, log_merge))

        def second_pass(r, sums_in):
            block = pl.ds(pl.multiple_of(r * 8, 8), 8)
            logs = [zbuf[block, lanes(s)] - lseb[:, lanes(s)] for s in range(draws)]
            best = tree(jnp.maximum, logs)
            risen = [jnp.exp(v - best) for v in logs]
            offset = r * 8 + lax.broadcasted_iota(jnp.int32, (8, batch), 0)
            share = jnp.where(offset < valid_rows, lab[block] / tree(jnp.add, risen), 0.0)
            peak[block] = jnp.exp(best) * (1.0 / batch)
            weight[block] = share * (1.0 / batch)
            for s in range(draws):
                zbuf[block, lanes(s)] = risen[s]
            return tuple(a + share * v for a, v in zip(sums_in, risen))

        dots = lax.fori_loop(
            0, plan.width // 8, second_pass, tuple(jnp.zeros((8, batch), jnp.float32) for _ in range(draws))
        )
        for s in range(draws):
            red[1, plane, s : s + 1, :] = jnp.sum(dots[s], axis=0, keepdims=True)
        fan_out(dotb, reduce_all(1, lambda parts: tree(jnp.add, parts)))

    def cot_chunk(c):
        def body(b, carry):
            means, scales = [], []
            for part in range(2):
                block = pl.ds(pl.multiple_of(c * GRAIN + b * 16 + part * 8, 8), 8)
                eb, wt = peak[block], weight[block]
                terms = [zbuf[block, lanes(s)] * (eb * dotb[:, lanes(s)] - wt) for s in range(draws)]
                means.append(tree(jnp.add, terms))
                scales.append(
                    tree(jnp.add, [t * low[block, lanes(s)] for s, t in enumerate(terms)]) * gate[block]
                )
            inside = pl.ds(pl.multiple_of(b * 16, 16), 16)
            cot[own_q, c, inside, :batch] = jnp.concatenate(means, axis=0).astype(jnp.bfloat16)
            cot[own_q, c, inside, batch:] = jnp.concatenate(scales, axis=0).astype(jnp.bfloat16)
            return carry
        lax.fori_loop(0, GRAIN // 16, body, 0)

    def gz(e, kind, k, target):
        q = e * 2 + (y if kind < 2 else 1 - y)
        c = k + steps if kind == 1 else k
        return remote(cot.at[q, c], cot.at[q, c], gzs.at[e, kind, k], gzr.at[e, kind, k], at(target, y))

    def gy(e, kind, k, side):
        q, c = e * 2 + side, k + steps * kind
        return remote(cot.at[q, c], cot.at[q, c], gys.at[e, kind, k], gyr.at[e, kind, k], at(z, 1 - y))

    def relay(e, i, target):
        @pl.when((i >= 0) & (i < steps))
        def _():
            for kind in (1, 0):
                gz(e, kind, i, mid).wait_recv()
                if target is not None:
                    gz(e, kind, i, target).start()
                if kind == 1:
                    gy(e, 1, i, y).start()
        j = i - late
        @pl.when((j >= 0) & (j < steps))
        def _():
            gz(e, 2, j, mid).wait_recv()
            if target is not None:
                gz(e, 2, j, target).start()

    def absorb(j):
        for e in range(2):
            gy(e, 1, j, 1 - y).wait_recv()
        for kind in range(2):
            c = j + kind * steps
            for h in range(2):
                lhs = jnp.concatenate([cot[q, c, :, h * batch : (h + 1) * batch] for q in range(4)], axis=0)
                rhs = jnp.concatenate(
                    [
                        whole[h, pl.ds(pl.multiple_of(plan.starts[q] + c * GRAIN, UNIT), GRAIN)]
                        for q in range(4)
                    ],
                    axis=0,
                )
                acc[...] += lax.dot_general(
                    lhs, rhs, (((0,), (0,)), ((), ())), preferred_element_type=jnp.float32
                )

    for copy in whole_copies:
        copy.wait()

    def gather(i, carry):
        @pl.when(outer)
        def _():
            @pl.when(i < steps)
            def _():
                for kind in (1, 0):
                    cot_chunk(i + kind * steps)
                    gz(half, kind, i, mid).start()
                    gy(half, kind, i, y).start()
            j = i - late
            @pl.when((j >= 0) & (j < steps))
            def _():
                gy(half, 0, j, 1 - y).wait_recv()
                gz(half, 2, j, mid).start()
            relay(1 - half, i - relay_out, None)

        @pl.when(inner)
        def _():
            relay(half, i, across)
            relay(1 - half, i - relay_in, edge)
        last = i - relay_out - late
        when(last >= 0, lambda: absorb(last))
        return carry

    lax.fori_loop(0, steps + relay_out + late, gather, 0)

    def twin(slot):
        return remote(acc, part.at[slot], csend, crecv, (xx * 2 + 1 - core, me))

    part[core] = acc[...]
    twin(core).start()
    twin(1 - core).wait_recv()

    def settle(k, carry):
        for e in range(2):
            gy(e, 1, k, y).wait_send()
        for kind in range(3):
            gz(half, kind, k, mid).wait_send()
            when(inner, lambda: gz(1 - half, kind, k, mid).wait_send())
        when(outer, lambda: gy(half, 0, k, y).wait_send())
        return carry

    lax.fori_loop(0, steps, settle, 0)

    def settle_first(k, carry):
        for e in range(2):
            for h in range(2):
                y_copy(e, h, k).wait_send()
        z_copy(e_first, k, mid).wait_send()
        when(inner, lambda: z_copy(e_second, k, mid).wait_send())
        return carry

    lax.fori_loop(0, chunks, settle_first, 0)
    twin(core).wait_send()
    for e in range(2):
        when(z != 3 * e, lambda: noise_copy(e, z).wait_send())

    @pl.when(outer)
    def _():
        for n in range(3):
            stages[n](lambda c: c.wait_send())
        for kind in range(2):
            for k in range(1, 8):
                remote(
                    red.at[kind, plane], red.at[kind, plane], rsend.at[kind, k], rrecv.at[kind, plane],
                    in_plane(lax.rem(plane + k, 8)),
                ).wait_send()
            far_copy(kind, half).wait_send()


def head_kernel(plan, cot, feat, mean_out, scale_out, stage, sems):
    batch, rows = plan.batch, plan.rows
    me = lax.axis_index("draw")
    cols = feat[:, pl.ds(pl.multiple_of(me * rows, rows), rows)]
    blank = jnp.zeros_like(cols)
    rhs = jnp.concatenate(
        [jnp.concatenate([cols, blank], axis=1), jnp.concatenate([blank, cols], axis=1)], axis=0
    )
    outs = (mean_out, scale_out)
    copies = []
    for q in range(4):
        size, first = plan.sizes[q], plan.starts[q]
        for part in range(2):
            begin = part * plan.steps * GRAIN
            count = min(plan.steps * GRAIN, size - begin)
            lhs = cot[q, part * plan.steps : (part + 1) * plan.steps].reshape(plan.steps * GRAIN, 2 * batch)
            value = jnp.dot(lhs[:count], rhs, preferred_element_type=jnp.float32)
            spot = slice(first + begin, first + begin + count)
            for h in range(2):
                stage[h, spot] = value[:, h * rows : (h + 1) * rows]
                copy = pltpu.make_async_copy(stage.at[h, spot], outs[h].at[spot], sems.at[h, q * 2 + part])
                copy.start()
                copies.append(copy)
    for copy in copies:
        copy.wait()


def ends_on_device(features, mean_head, scale_head, factor, noise, labels):
    rows, columns = mean_head.shape
    batch = features.shape[0]
    own, rank = noise.shape[0], noise.shape[2]
    draws = own * 8
    plan = Plan(batch, rows, columns, rank)
    width, chunks, steps = plan.width, plan.chunks, plan.steps
    mean_rows, scale_rows = mean_head.T, scale_head.T
    noise_t = jnp.pad(noise.transpose(0, 2, 1), ((0, 0), (0, 64 - rank), (0, 0)))
    dma = pltpu.SemaphoreType.DMA
    f32, bf16 = jnp.float32, jnp.bfloat16
    cot, part = pl.pallas_call(
        functools.partial(softmax_kernel, plan, draws, 2, 3, 8, 1, 4, 1),
        out_shape=(
            jax.ShapeDtypeStruct((4, chunks, GRAIN, 2 * batch), bf16),
            jax.ShapeDtypeStruct((2, batch, rows), f32),
        ),
        in_specs=[ANY] * 6,
        out_specs=(VMEM, VMEM),
        scratch_shapes=[
            pltpu.VMEM((2, 2, width, 2 * rows), bf16),
            pltpu.VMEM((chunks, 2, 2, GRAIN, batch), f32),
            pltpu.VMEM((2, chunks, 2, GRAIN, batch), f32),
            pltpu.VMEM((width, draws * batch), f32),
            pltpu.VMEM((width, draws * batch), f32),
            pltpu.VMEM((width, batch), f32),
            pltpu.VMEM((width, batch), f32),
            pltpu.VMEM((width, batch), f32),
            pltpu.VMEM((batch, 2 * rows), bf16),
            pltpu.VMEM((rank, columns), bf16),
            pltpu.VMEM((64, width), bf16),
            pltpu.VMEM((2, 2, 2, 4, 32, batch), bf16),
            pltpu.VMEM((64, draws * batch), bf16),
            pltpu.VMEM((width, batch), f32),
            pltpu.VMEM((8, draws * batch), f32),
            pltpu.VMEM((8, draws * batch), f32),
            pltpu.VMEM((8, draws * batch), f32),
            pltpu.VMEM((8, draws * batch), f32),
            pltpu.VMEM((2, 8, draws, batch), f32),
            pltpu.VMEM((2, 2, draws, batch), f32),
            pltpu.VMEM((2, columns, rows), bf16),
            pltpu.VMEM((batch, rows), f32),
            dma((8,)),
            dma((chunks, 2, 2)),
            dma((chunks, 2, 2)),
            dma((2, chunks)),
            dma((2, chunks)),
            dma((2,)),
            dma((4,)),
            dma((3,)),
            dma((3,)),
            dma((2, 8)),
            dma((2, 8)),
            dma((2,)),
            dma((2,)),
            dma((2, 3, steps)),
            dma((2, 3, steps)),
            dma((2, 2, steps)),
            dma((2, 2, steps)),
            dma((2,)),
            dma,
            dma,
        ],
        compiler_params=params(0, 56),
    )(features, mean_rows, scale_rows, factor.T, noise_t, labels.T)

    both = part[0] + part[1]
    other = lax.ppermute(both, "cls", [(i, i ^ 2) for i in range(4)])
    mean_grad, scale_grad = pl.pallas_call(
        functools.partial(head_kernel, plan),
        out_shape=(jax.ShapeDtypeStruct((columns, rows), f32),) * 2,
        in_specs=[VMEM, VMEM],
        out_specs=(ANY, ANY),
        scratch_shapes=[pltpu.VMEM((2, columns, rows), f32), dma((2, 8))],
        compiler_params=pltpu.CompilerParams(vmem_limit_bytes=32 * 2**20),
        cost_estimate=pl.CostEstimate(
            flops=8 * columns * batch * rows, bytes_accessed=16 * columns * rows, transcendentals=0
        ),
    )(cot, features)
    return (mean_grad.T, scale_grad.T, both + other)


def solution(mesh):
    ends = dict(mesh.shape) == {"cls": 4, "draw": 8}
    return jax.shard_map(
        ends_on_device if ends else on_device,
        mesh=mesh,
        in_specs=(
            P(),
            P("draw", "cls"),
            P("draw", "cls"),
            P("cls", None),
            P("draw", None, None),
            P(None, "cls"),
        ),
        out_specs=(P("draw", "cls"), P("draw", "cls"), P(None, "draw")),
        check_vma=False,
    )
```

```python
import functools
import jax
import jax.numpy as jnp
from jax import lax
from jax.experimental import pallas as pl
from jax.experimental.pallas import tpu as pltpu
from jax.sharding import PartitionSpec as P

CREAL = 21843
UNIT = 16
MESH = pl.DeviceIdType.MESH
ANY = pl.BlockSpec(memory_space=pl.ANY)
VMEM = pl.BlockSpec(memory_space=pltpu.VMEM)


def start_of(owner, n, units):
    return lax.div(owner * units, n)


def at_width(owner, n, units, run):
    base = units // n
    wide = start_of(owner + 1, n, units) - start_of(owner, n, units) > base
    pl.when(wide)(functools.partial(run, (base + 1) * UNIT))
    pl.when(jnp.logical_not(wide))(functools.partial(run, base * UNIT))


def exchange_kernel(
    n, units, feat, mean, scale, noise, logits, noise_out, held, part_out, part_in,
    send, recv, part_send, part_recv, nsend, nrecv, local, nlocal,
):
    me, cls = lax.axis_index("draw"), lax.axis_index("cls")
    half, rows = n // 2, mean.shape[1]
    mirror = lax.rem(me + half, n)
    base, spot = lax.div(me, half) * half, lax.rem(me, half)
    barrier = pltpu.get_barrier_semaphore()
    for k in range(1, n):
        pl.semaphore_signal(barrier, inc=1, device_id=(cls, lax.rem(me + k, n)), device_id_type=MESH)
    pl.semaphore_wait(barrier, n - 1)

    def remote(source, target, send_sem, recv_sem, device):
        return pltpu.make_async_remote_copy(
            source, target, send_sem, recv_sem, device_id=(cls, device), device_id_type=MESH
        )

    def noise_copy(slot, k, device):
        return remote(noise, noise_out.at[slot], nsend.at[k], nrecv.at[slot], device)

    def block(head, owner, width):
        start = pl.multiple_of(start_of(owner, n, units) * UNIT, UNIT)
        return (mean, scale)[head].at[pl.ds(start, width)]

    def block_copy(far, head, owner, k, source, device, act):
        at_width(
            owner, n, units,
            lambda w: act(
                remote(
                    block(head, owner, w), held.at[far, head, source, pl.ds(0, w)],
                    send.at[far, head, k], recv.at[far, head, source], device,
                )
            ),
        )

    def own_copy(far, head, act):
        owner = mirror if far else me
        at_width(
            owner, n, units,
            lambda w: act(
                pltpu.make_async_copy(
                    block(head, owner, w), held.at[far, head, spot, pl.ds(0, w)], local.at[far, head]
                )
            ),
        )

    def sends(far, head, act):
        for k in range(1, half):
            peer = base + lax.rem(spot + k, half)
            block_copy(far, head, lax.rem(peer + half, n) if far else peer, k, spot, peer, act)

    def columns_of(source):
        if rows % 128:
            return feat[source]
        return feat[:, pl.ds(pl.multiple_of(source * rows, rows), rows)]

    def arrive(far, head):
        owner = mirror if far else me
        for k in range(1, half):
            source = lax.rem(spot + half - k, half)
            block_copy(far, head, owner, k, source, base + source, lambda c: c.wait_recv())
        own_copy(far, head, lambda c: c.wait())
        total = None
        for source in range(half):
            term = lax.dot_general(
                held[far, head, source], columns_of(base + source), (((1,), (1,)), ((), ())),
                preferred_element_type=jnp.float32,
            )
            total = term if total is None else total + term
        return total

    def part_copy(head):
        return remote(part_out.at[head], part_in.at[head], part_send.at[head], part_recv.at[head], mirror)

    own_noise = pltpu.make_async_copy(noise, noise_out.at[me], nlocal)
    stages = [(1, 0), (1, 1), (0, 0), (0, 1)]
    sends(1, 0, lambda c: c.start())
    for k in range(1, n):
        noise_copy(me, k, lax.rem(me + k, n)).start()
    for far, head in stages[1:]:
        sends(far, head, lambda c: c.start())
    for far, head in stages:
        own_copy(far, head, lambda c: c.start())
    own_noise.start()
    for head in range(2):
        part_out[head] = arrive(1, head)
        part_copy(head).start()
    for head in range(2):
        logits[head] = arrive(0, head)
    for k in range(1, n):
        source = lax.rem(me + n - k, n)
        noise_copy(source, k, source).wait_recv()
    own_noise.wait()
    for head in range(2):
        part_copy(head).wait_recv()
        logits[head] = logits[head] + part_in[head]
    for far, head in stages:
        sends(far, head, lambda c: c.wait_send())
    for k in range(1, n):
        noise_copy(me, k, lax.rem(me + k, n)).wait_send()
    for head in range(2):
        part_copy(head).wait_send()


def gather_kernel(n, units, cot, out, send, recv, local):
    me, cls = lax.axis_index("draw"), lax.axis_index("cls")
    half = n // 2
    group, side = lax.div(me, 2), lax.rem(me, 2)
    partner = group * 2 + 1 - side
    split = units // n // 2 * UNIT
    pieces = [(head, part) for head in range(2) for part in range(2)]
    barrier = pltpu.get_barrier_semaphore()
    peers = [partner] + [lax.rem(group + k, half) * 2 + side for k in range(1, half)]
    for peer in peers:
        pl.semaphore_signal(barrier, inc=1, device_id=(cls, peer), device_id_type=MESH)
    pl.semaphore_wait(barrier, half)

    def source(piece, width):
        head, part = pieces[piece]
        return cot.at[head, pl.ds(split, width - split) if part else pl.ds(0, split)]

    def place(piece, owner, width):
        head, part = pieces[piece]
        start = start_of(owner, n, units) * UNIT + part * split
        return out.at[head, pl.ds(pl.multiple_of(start, UNIT), width - split if part else split)]

    def send_own(piece, owner, slot, device, act):
        at_width(
            owner, n, units,
            lambda w: act(
                pltpu.make_async_remote_copy(
                    source(piece, w), place(piece, owner, w), send.at[slot, piece], recv.at[owner, piece],
                    device_id=(cls, device), device_id_type=MESH,
                )
            ),
        )

    def forward(piece, owner, slot, act):
        at_width(
            owner, n, units,
            lambda w: act(
                pltpu.make_async_remote_copy(
                    place(piece, owner, w), place(piece, owner, w), send.at[slot, piece], recv.at[owner, piece],
                    device_id=(cls, partner), device_id_type=MESH,
                )
            ),
        )

    def own(piece, act):
        at_width(
            me, n, units,
            lambda w: act(pltpu.make_async_copy(source(piece, w), place(piece, me, w), local.at[piece])),
        )

    count = len(pieces)
    for piece in range(count):
        for k in range(1, half):
            send_own(piece, me, k, peers[k], lambda c: c.start())
        send_own(piece, me, 0, partner, lambda c: c.start())
    for piece in range(count):
        own(piece, lambda c: c.start())
    order = sorted(range(1, half), key=lambda k: min(k, half - k))
    for piece in range(count):
        for k in order:
            send_own(piece, peers[k], k, peers[k], lambda c: c.wait_recv())
            forward(piece, peers[k], half + k, lambda c: c.start())
    for piece in range(count):
        send_own(piece, partner, 0, partner, lambda c: c.wait_recv())
        for k in range(1, half):
            owner = lax.rem(group + k, half) * 2 + 1 - side
            forward(piece, owner, half + k, lambda c: c.wait_recv())
    for piece in range(count):
        for k in range(half):
            send_own(piece, me, k, peers[k], lambda c: c.wait_send())
        for k in range(1, half):
            forward(piece, peers[k], half + k, lambda c: c.wait_send())
        own(piece, lambda c: c.wait())


def merge(slots, count, softmax):
    if not softmax:
        total = slots[0]
        for i in range(1, count):
            total = total + slots[i]
        return total
    top = slots[0, 0]
    for i in range(1, count):
        top = jnp.maximum(top, slots[i, 0])
    total = jnp.zeros_like(top)
    for i in range(count):
        total = total + slots[i, 1] * jnp.exp(slots[i, 0] - top)
    return jnp.stack((top, total))


def reduce_kernel(counts, softmax, x, out, *scratch):
    levels = len(counts)
    slots, sends, recvs = scratch[:levels], scratch[levels : 2 * levels], scratch[2 * levels :]
    cls, draw = lax.axis_index("cls"), lax.axis_index("draw")

    def device(level, index):
        return (index, draw) if level == 0 else (cls, index)

    barrier = pltpu.get_barrier_semaphore()
    for level, n in enumerate(counts):
        me = (cls, draw)[level]
        for k in range(1, n):
            pl.semaphore_signal(
                barrier, inc=1, device_id=device(level, lax.rem(me + k, n)), device_id_type=MESH
            )
    pl.semaphore_wait(barrier, sum(counts) - levels)
    value = x[...]
    for level, n in enumerate(counts):
        me = (cls, draw)[level]
        held = slots[level]
        held[me] = value

        def copy(slot, k, target):
            return pltpu.make_async_remote_copy(
                held.at[slot], held.at[slot], sends[level].at[k], recvs[level].at[slot],
                device_id=device(level, target), device_id_type=MESH,
            )

        for k in range(1, n):
            copy(me, k, lax.rem(me + k, n)).start()
        for k in range(1, n):
            source = lax.rem(me + n - k, n)
            copy(source, k, source).wait_recv()
        for k in range(1, n):
            copy(me, k, lax.rem(me + k, n)).wait_send()
        value = merge(held, n, softmax)
    if softmax:
        out[...] = value[0] + jnp.log(value[1])
    else:
        out[...] = value


def params(collective_id, grant=32):
    return pltpu.CompilerParams(
        collective_id=collective_id, has_side_effects=True, vmem_limit_bytes=grant * 2**20
    )


def reduce_over(x, counts, softmax, collective_id):
    shape = x.shape[1:] if softmax else x.shape
    return pl.pallas_call(
        functools.partial(reduce_kernel, counts, softmax),
        out_shape=jax.ShapeDtypeStruct(shape, jnp.float32),
        in_specs=[VMEM],
        out_specs=VMEM,
        scratch_shapes=[pltpu.VMEM((n,) + x.shape, jnp.float32) for n in counts]
        + [pltpu.SemaphoreType.DMA((n,)) for n in counts]
        + [pltpu.SemaphoreType.DMA((n,)) for n in counts],
        compiler_params=params(collective_id),
    )(x)


def on_device(features, mean_head, scale_head, factor, noise, labels):
    rows, columns = mean_head.shape
    batch = features.shape[0]
    n, ncls = lax.axis_size("draw"), lax.axis_size("cls")
    me = lax.axis_index("draw")
    units = columns // UNIT
    tile = -(-units // n) * UNIT
    own, rank = noise.shape[0], noise.shape[2]
    draws = own * n
    mean_rows, scale_rows = mean_head.T, scale_head.T
    half = n // 2
    feat = features.reshape(batch, n, rows).transpose(1, 0, 2) if rows % 128 else features

    heads, noise_t = pl.pallas_call(
        functools.partial(exchange_kernel, n, units),
        out_shape=(
            jax.ShapeDtypeStruct((2, tile, batch), jnp.float32),
            jax.ShapeDtypeStruct((n, own, rank, batch), jnp.bfloat16),
        ),
        in_specs=[VMEM] + [ANY] * 3,
        out_specs=(VMEM, ANY),
        scratch_shapes=[
            pltpu.VMEM((2, 2, half, tile, rows), jnp.bfloat16),
            pltpu.VMEM((2, tile, batch), jnp.float32),
            pltpu.VMEM((2, tile, batch), jnp.float32),
            pltpu.SemaphoreType.DMA((2, 2, half)),
            pltpu.SemaphoreType.DMA((2, 2, half)),
            pltpu.SemaphoreType.DMA((2,)),
            pltpu.SemaphoreType.DMA((2,)),
            pltpu.SemaphoreType.DMA((n,)),
            pltpu.SemaphoreType.DMA((n,)),
            pltpu.SemaphoreType.DMA((2, 2)),
            pltpu.SemaphoreType.DMA,
        ],
        compiler_params=params(0),
    )(feat, mean_rows, scale_rows, noise.transpose(0, 2, 1))

    first = start_of(me, n, units) * UNIT
    width = start_of(me + 1, n, units) * UNIT - first
    offsets = jnp.arange(tile, dtype=jnp.int32)[:, None]
    valid = offsets < width
    class_ids = lax.axis_index("cls") * columns + first + offsets
    shift = jnp.where(class_ids >= CREAL, 30000.0, 0.0).astype(jnp.float32)
    my_factor = lax.dynamic_slice_in_dim(factor.T, first, tile, 1)
    my_labels = jnp.where(valid, lax.dynamic_slice_in_dim(labels.T, first, tile, 0), 0.0)

    mean_logit, scale_pre = heads[0], heads[1]
    scale_pre = jnp.where(valid, scale_pre, 0.0)
    spread = jax.nn.softplus(scale_pre)
    lowrank = jnp.einsum(
        "rc,srb->scb", my_factor, noise_t.reshape(draws, rank, batch), preferred_element_type=jnp.float32
    )
    logits = mean_logit[None] + spread[None] * lowrank - shift[None]
    logits = jnp.where(valid[None], logits, -1e30)
    local_top = jnp.max(logits, axis=1)
    local_total = jnp.sum(jnp.exp(logits - local_top[:, None]), axis=1)
    lse = reduce_over(jnp.stack((local_top, local_total)), (ncls, n), True, 1)
    log_prob = logits - lse[:, None]
    best = jnp.max(log_prob, axis=0)
    risen = jnp.exp(log_prob - best[None])
    inverse = 1.0 / jnp.sum(risen, axis=0)
    weight = my_labels * inverse
    label_dot = reduce_over(jnp.sum(weight[None] * risen, axis=1), (ncls, n), False, 2)
    logit_cot = risen * ((jnp.exp(best) / batch)[None] * label_dot[:, None] - (weight / batch)[None])
    dmean = jnp.sum(logit_cot, axis=0)
    dspread = jnp.sum(logit_cot * lowrank, axis=0)
    cots = jnp.stack((dmean, dspread * jax.nn.sigmoid(scale_pre))).astype(jnp.bfloat16)

    gathered = pl.pallas_call(
        functools.partial(gather_kernel, n, units),
        out_shape=jax.ShapeDtypeStruct((2, columns, batch), jnp.bfloat16),
        in_specs=[ANY],
        out_specs=ANY,
        scratch_shapes=[
            pltpu.SemaphoreType.DMA((n, 4)),
            pltpu.SemaphoreType.DMA((n, 4)),
            pltpu.SemaphoreType.DMA((4,)),
        ],
        compiler_params=params(3),
    )(cots)
    mean_cot, scale_cot = gathered[0], gathered[1]
    my_columns = lax.dynamic_slice_in_dim(features, me * rows, rows, 1)
    over_classes = (((0,), (0,)), ((), ()))
    feature_part = lax.dot_general(
        mean_cot, mean_rows, over_classes, preferred_element_type=jnp.float32
    ) + lax.dot_general(scale_cot, scale_rows, over_classes, preferred_element_type=jnp.float32)
    mean_grad = jnp.dot(mean_cot, my_columns, preferred_element_type=jnp.float32).T
    scale_grad = jnp.dot(scale_cot, my_columns, preferred_element_type=jnp.float32).T
    feature_grad, step = feature_part, 1
    while step < ncls:
        feature_grad = feature_grad + lax.ppermute(feature_grad, "cls", [(i, i ^ step) for i in range(ncls)])
        step *= 2
    return (mean_grad, scale_grad, feature_grad)


GRAIN = 64
NEG = -1e30


def when(cond, fn):
    pl.when(cond)(fn)


class Plan:
    def __init__(self, batch, rows, columns, rank):
        self.batch, self.rows, self.columns, self.rank = batch, rows, columns, rank
        units = columns // UNIT
        edges = [q * units // 4 * UNIT for q in range(5)]
        widest = max(b - a for a, b in zip(edges, edges[1:]))
        step = 2 * GRAIN
        self.width = -(-widest // step) * step
        self.units = units
        self.extra = max(0, edges[3] + self.width - columns)
        self.starts = edges[:3] + [edges[3] - self.extra]
        self.sizes = [b - a for a, b in zip(self.starts, self.starts[1:] + [columns])]
        self.chunks = self.width // GRAIN
        self.steps = self.chunks // 2

    def start(self, q):
        return pl.multiple_of(lax.div(q * self.units, 4) * UNIT - self.extra * lax.div(q, 3), UNIT)

    def size(self, q):
        after = lax.div((q + 1) * self.units, 4) * UNIT - self.extra * (lax.div(q + 1, 3) - lax.div(q + 1, 4))
        return after - self.start(q)


def tree(fn, items):
    items = list(items)
    while len(items) > 1:
        items = [fn(*items[i : i + 2]) if i + 1 < len(items) else items[i] for i in range(0, len(items), 2)]
    return items[0]


def softmax_kernel(
    plan, draws, ahead, lag_in, lag_out, relay_in, relay_out, late,
    feat, mean, scale, factor, noise, labels, cot_out, part,
    wbuf, sums, arrived, zbuf, low, gate, weight, peak, fcols, fturn, fac, fq, nb, nmat, lab, top, total, lseb, dotb,
    red, whole, acc, acc_in, cot,
    lsem, ysend, yrecv, zsend, zrecv, nsend, nrecv, nstage, nstage_r, rsend, rrecv,
    gzs, gzr, gys, gyr, wsem, csend, crecv, osem,
):
    me, cls = lax.axis_index("draw"), lax.axis_index("cls")
    z, y = lax.div(me, 2), lax.rem(me, 2)
    xx, core = lax.div(cls, 2), lax.rem(cls, 2)
    half = lax.div(z, 2)
    outer = (z == 0) | (z == 3)
    inner = jnp.logical_not(outer)
    edge, mid = 3 * half, 1 + half
    across = 2 - half
    batch, rows, chunks, steps = plan.batch, plan.rows, plan.chunks, plan.steps
    own_q = half * 2 + y
    start = plan.start(own_q)
    valid_rows = plan.size(own_q)
    plane = cls * 2 + y
    heads = (mean, scale)

    def at(zi, yi):
        return (cls, zi * 2 + yi)

    def in_plane(p):
        return (lax.div(p, 2), z * 2 + lax.rem(p, 2))

    barrier = pltpu.get_barrier_semaphore()
    for k in range(1, 8):
        pl.semaphore_signal(barrier, inc=1, device_id=in_plane(lax.rem(plane + k, 8)), device_id_type=MESH)
    for k in range(1, 4):
        pl.semaphore_signal(barrier, inc=1, device_id=at(lax.rem(z + k, 4), y), device_id_type=MESH)

    @pl.when(outer)
    def _():
        for k in range(1, 8):
            p = lax.rem(plane + k, 8)
            pl.semaphore_signal(
                barrier, inc=1, device_id=(lax.div(p, 2), (3 - z) * 2 + lax.rem(p, 2)), device_id_type=MESH
            )

    def remote(src, dst, s, r, device):
        return pltpu.make_async_remote_copy(src, dst, s, r, device_id=device, device_id_type=MESH)

    def local_own(e, h):
        return pltpu.make_async_copy(
            heads[h].at[pl.ds(plan.start(e * 2 + y), plan.width)],
            wbuf.at[e, h, :, pl.ds(pl.multiple_of(y * rows, rows), rows)],
            lsem.at[e * 2 + h],
        )

    feat_copy = pltpu.make_async_copy(
        feat.at[:, pl.ds(pl.multiple_of(z * 2 * rows, 2 * rows), 2 * rows)], fcols, lsem.at[4]
    )
    factor_copy = pltpu.make_async_copy(factor, fac, lsem.at[5])
    label_copy = pltpu.make_async_copy(labels.at[pl.ds(start, plan.width)], lab, lsem.at[6])
    noise_own = pltpu.make_async_copy(
        noise.at[core], nb.at[core, y, z], lsem.at[7]
    )

    def y_copy(e, h, k):
        return remote(
            heads[h].at[pl.ds(plan.start(e * 2 + 1 - y) + k * GRAIN, GRAIN)],
            wbuf.at[e, h, pl.ds(pl.multiple_of(k * GRAIN, GRAIN), GRAIN), pl.ds(pl.multiple_of(y * rows, rows), rows)],
            ysend, yrecv.at[k], at(z, 1 - y),
        )

    def y_landed(k):
        block = wbuf.at[
            :, :, pl.ds(pl.multiple_of(k * GRAIN, GRAIN), GRAIN), pl.ds(pl.multiple_of((1 - y) * rows, rows), rows)
        ]
        return remote(block, block, ysend, yrecv.at[k], at(z, 1 - y))

    def y_sent():
        block = wbuf.at[:, :, :, pl.ds(pl.multiple_of(y * rows, rows), rows)]
        return remote(block, block, ysend, yrecv.at[0], at(z, 1 - y))

    def y_start(k):
        for e in range(2):
            for h in range(2):
                y_copy(e, h, k).start()

    def z_copy(e, k, target):
        return remote(sums.at[k, e], arrived.at[e, k], zsend.at[e], zrecv.at[e, k], at(target, y))

    def noise_copy(e, source):
        return remote(
            noise.at[core], nb.at[core, y, source], nsend.at[e], nrecv.at[source], at(3 * e, y),
        )

    sibling = (xx * 2 + 1 - core, me)

    def stage(n, far_side):
        if n == 0:
            block = nb.at[core, 1 - y if far_side else y]
            return remote(block, block, nstage.at[0], nstage_r.at[0], at(z, 1 - y))
        block = nb.at[1 - core if far_side else core]
        return remote(block, block, nstage.at[1], nstage_r.at[1], sibling)

    feat_copy.start()
    for e in range(2):
        for h in range(2):
            local_own(e, h).start()
    if plan.rank < 64:
        fq[...] = jnp.zeros_like(fq)
        nmat[...] = jnp.zeros_like(nmat)
    factor_copy.start()
    noise_own.start()
    when(outer, lambda: pl.semaphore_wait(barrier, 17))
    when(inner, lambda: pl.semaphore_wait(barrier, 10))
    for k in range(ahead):
        y_start(k)
    for e in range(2):
        when(z != 3 * e, lambda: noise_copy(e, z).start())
    label_copy.start()
    top[...] = jnp.full_like(top, NEG)
    total[...] = jnp.zeros_like(total)
    acc[...] = jnp.zeros_like(acc)
    feat_copy.wait()
    fturn[...] = fcols[...].T
    for e in range(2):
        for h in range(2):
            local_own(e, h).wait()

    def lanes(s):
        return slice(s * batch, (s + 1) * batch)

    def first_pass(k):
        @pl.when(lax.rem(k, 128 // GRAIN) == 0)
        def _():
            low[pl.ds(pl.multiple_of(k * GRAIN, 128), 128)] = lax.dot_general(
                fq[:, pl.ds(pl.multiple_of(k * GRAIN, 128), 128)], nmat[...],
                (((0,), (0,)), ((), ())), preferred_element_type=jnp.float32,
            )
        rows_k = pl.ds(pl.multiple_of(k * GRAIN, GRAIN), GRAIN)
        logit, pre = sums[k, half, 0], sums[k, half, 1]
        offset = k * GRAIN + lax.broadcasted_iota(jnp.int32, (GRAIN, batch), 0)
        valid = offset < valid_rows
        ids = cls * plan.columns + start + offset
        shifted = logit - jnp.where(ids >= CREAL, 30000.0, 0.0)
        fade = jnp.exp(-jnp.abs(pre))
        spread = jnp.maximum(pre, 0.0) + jnp.log1p(fade)
        gate[rows_k] = jnp.where(pre >= 0, 1.0, fade) / (1.0 + fade)
        shifted = jnp.where(valid, shifted, NEG)
        spread = jnp.where(valid, spread, 0.0)
        for s in range(draws):
            value = shifted + spread * low[rows_k, lanes(s)]
            zbuf[rows_k, lanes(s)] = value
            blocks = [value[i * 8 : i * 8 + 8] for i in range(GRAIN // 8)]
            old = top[:, lanes(s)]
            new = jnp.maximum(old, tree(jnp.maximum, blocks))
            grown = tree(jnp.add, [jnp.exp(b - new) for b in blocks])
            total[:, lanes(s)] = total[:, lanes(s)] * jnp.exp(old - new) + grown
            top[:, lanes(s)] = new

    e_first, e_second = 1 - half, half

    def noise_stage(i):
        @pl.when(i == 2)
        def _():
            for k in range(4):
                when(z != k, lambda: noise_copy(half, k).wait_recv())
            noise_own.wait()
            stage(0, False).start()

        @pl.when(i == 4)
        def _():
            stage(0, True).wait_recv()
            stage(1, False).start()

        @pl.when(i == 3)
        def _():
            factor_copy.wait()
            for q in range(4):
                def pick(q=q):
                    fq[: plan.rank] = fac[:, plan.starts[q] : plan.starts[q] + plan.width]
                when(own_q == q, pick)

        @pl.when(i == 5)
        def _():
            stage(1, True).wait_recv()
            for j in range(2):
                for yi in range(2):
                    for zi in range(4):
                        nmat[: plan.rank, lanes((j * 2 + yi) * 4 + zi)] = nb[j, yi, zi]

    def own_sums(i):
        when(i + ahead < chunks, lambda: y_start(i + ahead))
        y_landed(i).wait_recv()
        block = pl.ds(pl.multiple_of(i * GRAIN, GRAIN), GRAIN)
        lhs = jnp.concatenate([wbuf[e, h, block] for e in range(2) for h in range(2)], axis=0)
        value = lax.dot_general(
            lhs, fturn[...], (((1,), (0,)), ((), ())), preferred_element_type=jnp.float32
        )
        sums[i] = value.reshape(2, 2, GRAIN, batch)

    def add_arrived(e, k):
        z_copy(e, k, mid).wait_recv()
        sums[k, e] = sums[k, e] + arrived[e, k]

    def forward_inner(i, carry):
        @pl.when(i < chunks)
        def _():
            own_sums(i)
            add_arrived(e_first, i)
            z_copy(e_first, i, across).start()
        k = i - lag_in
        @pl.when(k >= 0)
        def _():
            add_arrived(e_second, k)
            z_copy(e_second, k, edge).start()
        return carry

    def forward_outer(i, carry):
        @pl.when(i < chunks)
        def _():
            own_sums(i)
            z_copy(e_first, i, mid).start()
        noise_stage(i)
        k = i - lag_out
        @pl.when(k >= 0)
        def _():
            add_arrived(e_second, k)
            first_pass(k)
        return carry

    @pl.when(inner)
    def _():
        lax.fori_loop(0, chunks + lag_in, forward_inner, 0)

    @pl.when(outer)
    def _():
        lax.fori_loop(0, chunks + lag_out, forward_outer, 0)

    whole_copies = [pltpu.make_async_copy(heads[h], whole.at[h], wsem.at[h]) for h in range(2)]
    for copy in whole_copies:
        copy.start()
    label_copy.wait()

    @pl.when(inner)
    def _():
        factor_copy.wait()
        noise_own.wait()

    spot = half * 8 + plane

    def end_device(p):
        return (lax.div(lax.rem(p, 8), 2), lax.div(p, 8) * 6 + lax.rem(p, 2))

    def red_copy(kind, slot, k, p):
        return remote(red.at[kind, slot], red.at[kind, slot], rsend.at[kind, k], rrecv.at[kind, slot], end_device(p))

    def log_merge(parts):
        best = tree(jnp.maximum, parts)
        return best + jnp.log(tree(jnp.add, [jnp.exp(p - best) for p in parts]))

    def fan_out(target, value):
        for s in range(draws):
            target[:, lanes(s)] = jnp.broadcast_to(value[s : s + 1], (8, batch))

    def reduce_all(kind, merge):
        for k in range(8, 16):
            red_copy(kind, spot, k, lax.rem(spot + k, 16)).start()
        for k in range(1, 8):
            red_copy(kind, spot, k, lax.rem(spot + k, 16)).start()
        for k in range(1, 16):
            source = lax.rem(spot + 16 - k, 16)
            red_copy(kind, source, k, source).wait_recv()
        return merge([red[kind, p] for p in range(16)])

    @pl.when(outer)
    def _():
        for s in range(draws):
            m = top[:, lanes(s)]
            best = jnp.max(m, axis=0, keepdims=True)
            size = jnp.sum(total[:, lanes(s)] * jnp.exp(m - best), axis=0, keepdims=True)
            red[0, spot, s : s + 1, :] = best + jnp.log(size)
        fan_out(lseb, reduce_all(0, log_merge))

        def second_pass(r, sums_in):
            block = pl.ds(pl.multiple_of(r * 8, 8), 8)
            logs = [zbuf[block, lanes(s)] - lseb[:, lanes(s)] for s in range(draws)]
            best = tree(jnp.maximum, logs)
            risen = [jnp.exp(v - best) for v in logs]
            offset = r * 8 + lax.broadcasted_iota(jnp.int32, (8, batch), 0)
            share = jnp.where(offset < valid_rows, lab[block] / tree(jnp.add, risen), 0.0)
            peak[block] = jnp.exp(best) * (1.0 / batch)
            weight[block] = share * (1.0 / batch)
            for s in range(draws):
                zbuf[block, lanes(s)] = risen[s]
            return tuple(a + share * v for a, v in zip(sums_in, risen))

        dots = lax.fori_loop(
            0, plan.width // 8, second_pass, tuple(jnp.zeros((8, batch), jnp.float32) for _ in range(draws)),
            unroll=4,
        )
        for s in range(draws):
            red[1, spot, s : s + 1, :] = jnp.sum(dots[s], axis=0, keepdims=True)
        fan_out(dotb, reduce_all(1, lambda parts: tree(jnp.add, parts)))

    def cot_chunk(c):
        def body(b, carry):
            means, scales = [], []
            for part in range(2):
                block = pl.ds(pl.multiple_of(c * GRAIN + b * 16 + part * 8, 8), 8)
                eb, wt = peak[block], weight[block]
                terms = [zbuf[block, lanes(s)] * (eb * dotb[:, lanes(s)] - wt) for s in range(draws)]
                means.append(tree(jnp.add, terms))
                scales.append(
                    tree(jnp.add, [t * low[block, lanes(s)] for s, t in enumerate(terms)]) * gate[block]
                )
            inside = pl.ds(pl.multiple_of(b * 16, 16), 16)
            cot[own_q, c, inside, :batch] = jnp.concatenate(means, axis=0).astype(jnp.bfloat16)
            cot[own_q, c, inside, batch:] = jnp.concatenate(scales, axis=0).astype(jnp.bfloat16)
            return carry
        lax.fori_loop(0, GRAIN // 16, body, 0)

    def gz(e, kind, k, target):
        q = e * 2 + (y if kind < 2 else 1 - y)
        c = k + steps if kind == 1 else k
        return remote(cot.at[q, c], cot.at[q, c], gzs.at[e, kind], gzr.at[e, kind, k], at(target, y))

    def gy(e, kind, k, side):
        q, c = e * 2 + side, k + steps * kind
        return remote(cot.at[q, c], cot.at[q, c], gys.at[e, kind], gyr.at[e, kind, k], at(z, 1 - y))

    def relay(e, i, target):
        @pl.when((i >= 0) & (i < steps))
        def _():
            for kind in (1, 0):
                gz(e, kind, i, mid).wait_recv()
                if target is not None:
                    gz(e, kind, i, target).start()
                if kind == 1:
                    gy(e, 1, i, y).start()
        j = i - late
        @pl.when((j >= 0) & (j < steps))
        def _():
            gz(e, 2, j, mid).wait_recv()
            if target is not None:
                gz(e, 2, j, target).start()

    def keep(q, c):
        return pltpu.make_async_copy(cot.at[q, c], cot_out.at[q, c], osem)

    def absorb(j):
        for e in range(2):
            gy(e, 1, j, 1 - y).wait_recv()
        for q in range(4):
            for kind in range(2):
                keep(q, j + kind * steps).start()
        for kind in range(2):
            c = j + kind * steps
            for h in range(2):
                lhs = jnp.concatenate([cot[q, c, :, h * batch : (h + 1) * batch] for q in range(4)], axis=0)
                rhs = jnp.concatenate(
                    [
                        whole[h, pl.ds(pl.multiple_of(plan.starts[q] + c * GRAIN, UNIT), GRAIN)]
                        for q in range(4)
                    ],
                    axis=0,
                )
                acc[...] += lax.dot_general(
                    lhs, rhs, (((0,), (0,)), ((), ())), preferred_element_type=jnp.float32
                )

    for copy in whole_copies:
        copy.wait()

    def gather(i, carry):
        @pl.when(outer)
        def _():
            @pl.when(i < steps)
            def _():
                for kind in (1, 0):
                    cot_chunk(i + kind * steps)
                    gz(half, kind, i, mid).start()
                    gy(half, kind, i, y).start()
            j = i - late
            @pl.when((j >= 0) & (j < steps))
            def _():
                gy(half, 0, j, 1 - y).wait_recv()
                gz(half, 2, j, mid).start()
            relay(1 - half, i - relay_out, None)

        @pl.when(inner)
        def _():
            relay(half, i, across)
            relay(1 - half, i - relay_in, edge)
        last = i - relay_out - late
        when(last >= 0, lambda: absorb(last))
        return carry

    lax.fori_loop(0, steps + relay_out + late, gather, 0)

    twin = remote(acc, acc_in, csend, crecv, sibling)
    twin.start()
    twin.wait_recv()
    part[...] = acc[...] + acc_in[...]

    def relayed(e, kind):
        block = cot.at[e * 2, pl.ds(kind % 2 * steps, steps)]
        return remote(block, block, gzs.at[e, kind], gzr.at[e, kind, 0], at(mid, y))

    def crossed(e, kind):
        block = cot.at[e * 2, pl.ds(kind * steps, steps)]
        return remote(block, block, gys.at[e, kind], gyr.at[e, kind, 0], at(z, 1 - y))

    for kind in range(3):
        relayed(half, kind).wait_send()
        when(inner, lambda: relayed(1 - half, kind).wait_send())
    for e in range(2):
        crossed(e, 1).wait_send()
    when(outer, lambda: crossed(half, 0).wait_send())
    pltpu.make_async_copy(cot, cot_out, osem).wait()
    def z_sent(e):
        return remote(arrived.at[e], arrived.at[e], zsend.at[e], zrecv.at[e, 0], at(mid, y))

    y_sent().wait_send()
    z_sent(e_first).wait_send()
    when(inner, lambda: z_sent(e_second).wait_send())
    twin.wait_send()
    for e in range(2):
        when(z != 3 * e, lambda: noise_copy(e, z).wait_send())

    @pl.when(outer)
    def _():
        for n in range(2):
            stage(n, False).wait_send()
        for kind in range(2):
            for k in range(1, 16):
                red_copy(kind, spot, k, lax.rem(spot + k, 16)).wait_send()


def head_kernel(plan, cot_in, feat_in, mean_out, scale_out, cot, cols_in, stage, loads, sems):
    batch, rows = plan.batch, plan.rows
    me = lax.axis_index("draw")
    feat_copy = pltpu.make_async_copy(
        feat_in.at[:, pl.ds(pl.multiple_of(me * rows, rows), rows)], cols_in, loads.at[8]
    )

    def load(q, part):
        span = pl.ds(part * plan.steps, plan.steps)
        return pltpu.make_async_copy(cot_in.at[q, span], cot.at[q, span], loads.at[q * 2 + part])

    feat_copy.start()
    for q in range(4):
        for part in range(2):
            load(q, part).start()
    feat_copy.wait()
    cols = cols_in[...]
    blank = jnp.zeros_like(cols)
    rhs = jnp.concatenate(
        [jnp.concatenate([cols, blank], axis=1), jnp.concatenate([blank, cols], axis=1)], axis=0
    )
    outs = (mean_out, scale_out)
    copies = []
    for q in range(4):
        size, first = plan.sizes[q], plan.starts[q]
        for part in range(2):
            begin = part * plan.steps * GRAIN
            count = min(plan.steps * GRAIN, size - begin)
            load(q, part).wait()
            lhs = cot[q, part * plan.steps : (part + 1) * plan.steps].reshape(plan.steps * GRAIN, 2 * batch)
            value = jnp.dot(lhs[:count], rhs, preferred_element_type=jnp.float32)
            spot = slice(first + begin, first + begin + count)
            for h in range(2):
                stage[h, spot] = value[:, h * rows : (h + 1) * rows]
                copy = pltpu.make_async_copy(stage.at[h, spot], outs[h].at[spot], sems.at[h, q * 2 + part])
                copy.start()
                copies.append(copy)
    for copy in copies:
        copy.wait()


def ends_on_device(features, mean_head, scale_head, factor, noise, labels):
    rows, columns = mean_head.shape
    batch = features.shape[0]
    own, rank = noise.shape[0], noise.shape[2]
    draws = own * 8
    plan = Plan(batch, rows, columns, rank)
    width, chunks, steps = plan.width, plan.chunks, plan.steps
    mean_rows, scale_rows = mean_head.T, scale_head.T
    noise_t = noise.transpose(0, 2, 1)
    dma = pltpu.SemaphoreType.DMA
    f32, bf16 = jnp.float32, jnp.bfloat16
    cot, part = pl.pallas_call(
        functools.partial(softmax_kernel, plan, draws, 3, 2, 8, 2, 6, 2),
        out_shape=(
            jax.ShapeDtypeStruct((4, chunks, GRAIN, 2 * batch), bf16),
            jax.ShapeDtypeStruct((batch, rows), f32),
        ),
        in_specs=[ANY] * 6,
        out_specs=(ANY, VMEM),
        scratch_shapes=[
            pltpu.VMEM((2, 2, width, 2 * rows), bf16),
            pltpu.VMEM((chunks, 2, 2, GRAIN, batch), f32),
            pltpu.VMEM((2, chunks, 2, GRAIN, batch), f32),
            pltpu.VMEM((width, draws * batch), f32),
            pltpu.VMEM((width, draws * batch), f32),
            pltpu.VMEM((width, batch), f32),
            pltpu.VMEM((width, batch), f32),
            pltpu.VMEM((width, batch), f32),
            pltpu.VMEM((batch, 2 * rows), bf16),
            pltpu.VMEM((2 * rows, batch), bf16),
            pltpu.VMEM((rank, columns), bf16),
            pltpu.VMEM((64, width), bf16),
            pltpu.VMEM((2, 2, 4, rank, batch), bf16),
            pltpu.VMEM((64, draws * batch), bf16),
            pltpu.VMEM((width, batch), f32),
            pltpu.VMEM((8, draws * batch), f32),
            pltpu.VMEM((8, draws * batch), f32),
            pltpu.VMEM((8, draws * batch), f32),
            pltpu.VMEM((8, draws * batch), f32),
            pltpu.VMEM((2, 16, draws, batch), f32),
            pltpu.VMEM((2, columns, rows), bf16),
            pltpu.VMEM((batch, rows), f32),
            pltpu.VMEM((batch, rows), f32),
            pltpu.VMEM((4, chunks, GRAIN, 2 * batch), bf16),
            dma((8,)),
            dma,
            dma((chunks,)),
            dma((2,)),
            dma((2, chunks)),
            dma((2,)),
            dma((4,)),
            dma((2,)),
            dma((2,)),
            dma((2, 16)),
            dma((2, 16)),
            dma((2, 3)),
            dma((2, 3, steps)),
            dma((2, 2)),
            dma((2, 2, steps)),
            dma((2,)),
            dma,
            dma,
            dma,
        ],
        compiler_params=params(0, 56),
    )(features, mean_rows, scale_rows, factor.T, noise_t, labels.T)

    other = lax.ppermute(part, "cls", [(i, i ^ 2) for i in range(4)])
    mean_grad, scale_grad = pl.pallas_call(
        functools.partial(head_kernel, plan),
        out_shape=(jax.ShapeDtypeStruct((columns, rows), f32),) * 2,
        in_specs=[ANY, ANY],
        out_specs=(ANY, ANY),
        scratch_shapes=[
            pltpu.VMEM((4, chunks, GRAIN, 2 * batch), bf16),
            pltpu.VMEM((batch, rows), bf16),
            pltpu.VMEM((2, columns, rows), f32),
            dma((9,)),
            dma((2, 8)),
        ],
        compiler_params=pltpu.CompilerParams(vmem_limit_bytes=60 * 2**20),
        cost_estimate=pl.CostEstimate(
            flops=8 * columns * batch * rows, bytes_accessed=16 * columns * rows, transcendentals=0
        ),
    )(cot, features)
    return (mean_grad.T, scale_grad.T, part + other)


def solution(mesh):
    ends = dict(mesh.shape) == {"cls": 4, "draw": 8}
    return jax.shard_map(
        ends_on_device if ends else on_device,
        mesh=mesh,
        in_specs=(
            P(),
            P("draw", "cls"),
            P("draw", "cls"),
            P("cls", None),
            P("draw", None, None),
            P(None, "cls"),
        ),
        out_specs=(P("draw", "cls"), P("draw", "cls"), P(None, "draw")),
        check_vma=False,
    )
```

```python
import functools
import jax
import jax.numpy as jnp
from jax import lax
from jax.experimental import pallas as pl
from jax.experimental.pallas import tpu as pltpu
from jax.sharding import PartitionSpec as P

CREAL = 21843
UNIT = 16
MESH = pl.DeviceIdType.MESH
ANY = pl.BlockSpec(memory_space=pl.ANY)
VMEM = pl.BlockSpec(memory_space=pltpu.VMEM)
HBM = pl.BlockSpec(memory_space=pltpu.HBM)


def start_of(owner, n, units):
    return lax.div(owner * units, n)


def at_width(owner, n, units, run):
    base = units // n
    wide = start_of(owner + 1, n, units) - start_of(owner, n, units) > base
    pl.when(wide)(functools.partial(run, (base + 1) * UNIT))
    pl.when(jnp.logical_not(wide))(functools.partial(run, base * UNIT))


def exchange_kernel(
    n, units, feat, mean, scale, noise, logits, noise_out, held, part_out, part_in,
    send, recv, part_send, part_recv, nsend, nrecv, local, nlocal,
):
    me, cls = lax.axis_index("draw"), lax.axis_index("cls")
    half, rows = n // 2, mean.shape[1]
    mirror = lax.rem(me + half, n)
    base, spot = lax.div(me, half) * half, lax.rem(me, half)
    barrier = pltpu.get_barrier_semaphore()
    for k in range(1, n):
        pl.semaphore_signal(barrier, inc=1, device_id=(cls, lax.rem(me + k, n)), device_id_type=MESH)
    pl.semaphore_wait(barrier, n - 1)

    def remote(source, target, send_sem, recv_sem, device):
        return pltpu.make_async_remote_copy(
            source, target, send_sem, recv_sem, device_id=(cls, device), device_id_type=MESH
        )

    def noise_copy(slot, k, device):
        return remote(noise, noise_out.at[slot], nsend.at[k], nrecv.at[slot], device)

    def block(head, owner, width):
        start = pl.multiple_of(start_of(owner, n, units) * UNIT, UNIT)
        return (mean, scale)[head].at[pl.ds(start, width)]

    def block_copy(far, head, owner, k, source, device, act):
        at_width(
            owner, n, units,
            lambda w: act(
                remote(
                    block(head, owner, w), held.at[far, head, source, pl.ds(0, w)],
                    send.at[far, head, k], recv.at[far, head, source], device,
                )
            ),
        )

    def own_copy(far, head, act):
        owner = mirror if far else me
        at_width(
            owner, n, units,
            lambda w: act(
                pltpu.make_async_copy(
                    block(head, owner, w), held.at[far, head, spot, pl.ds(0, w)], local.at[far, head]
                )
            ),
        )

    def sends(far, head, act):
        for k in range(1, half):
            peer = base + lax.rem(spot + k, half)
            block_copy(far, head, lax.rem(peer + half, n) if far else peer, k, spot, peer, act)

    def columns_of(source):
        if rows % 128:
            return feat[source]
        return feat[:, pl.ds(pl.multiple_of(source * rows, rows), rows)]

    def arrive(far, head):
        owner = mirror if far else me
        for k in range(1, half):
            source = lax.rem(spot + half - k, half)
            block_copy(far, head, owner, k, source, base + source, lambda c: c.wait_recv())
        own_copy(far, head, lambda c: c.wait())
        total = None
        for source in range(half):
            term = lax.dot_general(
                held[far, head, source], columns_of(base + source), (((1,), (1,)), ((), ())),
                preferred_element_type=jnp.float32,
            )
            total = term if total is None else total + term
        return total

    def part_copy(head):
        return remote(part_out.at[head], part_in.at[head], part_send.at[head], part_recv.at[head], mirror)

    own_noise = pltpu.make_async_copy(noise, noise_out.at[me], nlocal)
    stages = [(1, 0), (1, 1), (0, 0), (0, 1)]
    sends(1, 0, lambda c: c.start())
    for k in range(1, n):
        noise_copy(me, k, lax.rem(me + k, n)).start()
    for far, head in stages[1:]:
        sends(far, head, lambda c: c.start())
    for far, head in stages:
        own_copy(far, head, lambda c: c.start())
    own_noise.start()
    for head in range(2):
        part_out[head] = arrive(1, head)
        part_copy(head).start()
    for head in range(2):
        logits[head] = arrive(0, head)
    for k in range(1, n):
        source = lax.rem(me + n - k, n)
        noise_copy(source, k, source).wait_recv()
    own_noise.wait()
    for head in range(2):
        part_copy(head).wait_recv()
        logits[head] = logits[head] + part_in[head]
    for far, head in stages:
        sends(far, head, lambda c: c.wait_send())
    for k in range(1, n):
        noise_copy(me, k, lax.rem(me + k, n)).wait_send()
    for head in range(2):
        part_copy(head).wait_send()


def gather_kernel(n, units, cot, out, send, recv, local):
    me, cls = lax.axis_index("draw"), lax.axis_index("cls")
    half = n // 2
    group, side = lax.div(me, 2), lax.rem(me, 2)
    partner = group * 2 + 1 - side
    split = units // n // 2 * UNIT
    pieces = [(head, part) for head in range(2) for part in range(2)]
    barrier = pltpu.get_barrier_semaphore()
    peers = [partner] + [lax.rem(group + k, half) * 2 + side for k in range(1, half)]
    for peer in peers:
        pl.semaphore_signal(barrier, inc=1, device_id=(cls, peer), device_id_type=MESH)
    pl.semaphore_wait(barrier, half)

    def source(piece, width):
        head, part = pieces[piece]
        return cot.at[head, pl.ds(split, width - split) if part else pl.ds(0, split)]

    def place(piece, owner, width):
        head, part = pieces[piece]
        start = start_of(owner, n, units) * UNIT + part * split
        return out.at[head, pl.ds(pl.multiple_of(start, UNIT), width - split if part else split)]

    def send_own(piece, owner, slot, device, act):
        at_width(
            owner, n, units,
            lambda w: act(
                pltpu.make_async_remote_copy(
                    source(piece, w), place(piece, owner, w), send.at[slot, piece], recv.at[owner, piece],
                    device_id=(cls, device), device_id_type=MESH,
                )
            ),
        )

    def forward(piece, owner, slot, act):
        at_width(
            owner, n, units,
            lambda w: act(
                pltpu.make_async_remote_copy(
                    place(piece, owner, w), place(piece, owner, w), send.at[slot, piece], recv.at[owner, piece],
                    device_id=(cls, partner), device_id_type=MESH,
                )
            ),
        )

    def own(piece, act):
        at_width(
            me, n, units,
            lambda w: act(pltpu.make_async_copy(source(piece, w), place(piece, me, w), local.at[piece])),
        )

    count = len(pieces)
    for piece in range(count):
        for k in range(1, half):
            send_own(piece, me, k, peers[k], lambda c: c.start())
        send_own(piece, me, 0, partner, lambda c: c.start())
    for piece in range(count):
        own(piece, lambda c: c.start())
    order = sorted(range(1, half), key=lambda k: min(k, half - k))
    for piece in range(count):
        for k in order:
            send_own(piece, peers[k], k, peers[k], lambda c: c.wait_recv())
            forward(piece, peers[k], half + k, lambda c: c.start())
    for piece in range(count):
        send_own(piece, partner, 0, partner, lambda c: c.wait_recv())
        for k in range(1, half):
            owner = lax.rem(group + k, half) * 2 + 1 - side
            forward(piece, owner, half + k, lambda c: c.wait_recv())
    for piece in range(count):
        for k in range(half):
            send_own(piece, me, k, peers[k], lambda c: c.wait_send())
        for k in range(1, half):
            forward(piece, peers[k], half + k, lambda c: c.wait_send())
        own(piece, lambda c: c.wait())


def merge(slots, count, softmax):
    if not softmax:
        total = slots[0]
        for i in range(1, count):
            total = total + slots[i]
        return total
    top = slots[0, 0]
    for i in range(1, count):
        top = jnp.maximum(top, slots[i, 0])
    total = jnp.zeros_like(top)
    for i in range(count):
        total = total + slots[i, 1] * jnp.exp(slots[i, 0] - top)
    return jnp.stack((top, total))


def reduce_kernel(counts, softmax, x, out, *scratch):
    levels = len(counts)
    slots, sends, recvs = scratch[:levels], scratch[levels : 2 * levels], scratch[2 * levels :]
    cls, draw = lax.axis_index("cls"), lax.axis_index("draw")

    def device(level, index):
        return (index, draw) if level == 0 else (cls, index)

    barrier = pltpu.get_barrier_semaphore()
    for level, n in enumerate(counts):
        me = (cls, draw)[level]
        for k in range(1, n):
            pl.semaphore_signal(
                barrier, inc=1, device_id=device(level, lax.rem(me + k, n)), device_id_type=MESH
            )
    pl.semaphore_wait(barrier, sum(counts) - levels)
    value = x[...]
    for level, n in enumerate(counts):
        me = (cls, draw)[level]
        held = slots[level]
        held[me] = value

        def copy(slot, k, target):
            return pltpu.make_async_remote_copy(
                held.at[slot], held.at[slot], sends[level].at[k], recvs[level].at[slot],
                device_id=device(level, target), device_id_type=MESH,
            )

        for k in range(1, n):
            copy(me, k, lax.rem(me + k, n)).start()
        for k in range(1, n):
            source = lax.rem(me + n - k, n)
            copy(source, k, source).wait_recv()
        for k in range(1, n):
            copy(me, k, lax.rem(me + k, n)).wait_send()
        value = merge(held, n, softmax)
    if softmax:
        out[...] = value[0] + jnp.log(value[1])
    else:
        out[...] = value


def params(collective_id, grant=32):
    return pltpu.CompilerParams(
        collective_id=collective_id, has_side_effects=True, vmem_limit_bytes=grant * 2**20
    )


def reduce_over(x, counts, softmax, collective_id):
    shape = x.shape[1:] if softmax else x.shape
    return pl.pallas_call(
        functools.partial(reduce_kernel, counts, softmax),
        out_shape=jax.ShapeDtypeStruct(shape, jnp.float32),
        in_specs=[VMEM],
        out_specs=VMEM,
        scratch_shapes=[pltpu.VMEM((n,) + x.shape, jnp.float32) for n in counts]
        + [pltpu.SemaphoreType.DMA((n,)) for n in counts]
        + [pltpu.SemaphoreType.DMA((n,)) for n in counts],
        compiler_params=params(collective_id),
    )(x)


def on_device(features, mean_head, scale_head, factor, noise, labels):
    rows, columns = mean_head.shape
    batch = features.shape[0]
    n, ncls = lax.axis_size("draw"), lax.axis_size("cls")
    me = lax.axis_index("draw")
    units = columns // UNIT
    tile = -(-units // n) * UNIT
    own, rank = noise.shape[0], noise.shape[2]
    draws = own * n
    mean_rows, scale_rows = mean_head.T, scale_head.T
    half = n // 2
    feat = features.reshape(batch, n, rows).transpose(1, 0, 2) if rows % 128 else features

    heads, noise_t = pl.pallas_call(
        functools.partial(exchange_kernel, n, units),
        out_shape=(
            jax.ShapeDtypeStruct((2, tile, batch), jnp.float32),
            jax.ShapeDtypeStruct((n, own, rank, batch), jnp.bfloat16),
        ),
        in_specs=[VMEM] + [ANY] * 3,
        out_specs=(VMEM, ANY),
        scratch_shapes=[
            pltpu.VMEM((2, 2, half, tile, rows), jnp.bfloat16),
            pltpu.VMEM((2, tile, batch), jnp.float32),
            pltpu.VMEM((2, tile, batch), jnp.float32),
            pltpu.SemaphoreType.DMA((2, 2, half)),
            pltpu.SemaphoreType.DMA((2, 2, half)),
            pltpu.SemaphoreType.DMA((2,)),
            pltpu.SemaphoreType.DMA((2,)),
            pltpu.SemaphoreType.DMA((n,)),
            pltpu.SemaphoreType.DMA((n,)),
            pltpu.SemaphoreType.DMA((2, 2)),
            pltpu.SemaphoreType.DMA,
        ],
        compiler_params=params(0),
    )(feat, mean_rows, scale_rows, noise.transpose(0, 2, 1))

    first = start_of(me, n, units) * UNIT
    width = start_of(me + 1, n, units) * UNIT - first
    offsets = jnp.arange(tile, dtype=jnp.int32)[:, None]
    valid = offsets < width
    class_ids = lax.axis_index("cls") * columns + first + offsets
    shift = jnp.where(class_ids >= CREAL, 30000.0, 0.0).astype(jnp.float32)
    my_factor = lax.dynamic_slice_in_dim(factor.T, first, tile, 1)
    my_labels = jnp.where(valid, lax.dynamic_slice_in_dim(labels.T, first, tile, 0), 0.0)

    mean_logit, scale_pre = heads[0], heads[1]
    scale_pre = jnp.where(valid, scale_pre, 0.0)
    spread = jax.nn.softplus(scale_pre)
    lowrank = jnp.einsum(
        "rc,srb->scb", my_factor, noise_t.reshape(draws, rank, batch), preferred_element_type=jnp.float32
    )
    logits = mean_logit[None] + spread[None] * lowrank - shift[None]
    logits = jnp.where(valid[None], logits, -1e30)
    local_top = jnp.max(logits, axis=1)
    local_total = jnp.sum(jnp.exp(logits - local_top[:, None]), axis=1)
    lse = reduce_over(jnp.stack((local_top, local_total)), (ncls, n), True, 1)
    log_prob = logits - lse[:, None]
    best = jnp.max(log_prob, axis=0)
    risen = jnp.exp(log_prob - best[None])
    inverse = 1.0 / jnp.sum(risen, axis=0)
    weight = my_labels * inverse
    label_dot = reduce_over(jnp.sum(weight[None] * risen, axis=1), (ncls, n), False, 2)
    logit_cot = risen * ((jnp.exp(best) / batch)[None] * label_dot[:, None] - (weight / batch)[None])
    dmean = jnp.sum(logit_cot, axis=0)
    dspread = jnp.sum(logit_cot * lowrank, axis=0)
    cots = jnp.stack((dmean, dspread * jax.nn.sigmoid(scale_pre))).astype(jnp.bfloat16)

    gathered = pl.pallas_call(
        functools.partial(gather_kernel, n, units),
        out_shape=jax.ShapeDtypeStruct((2, columns, batch), jnp.bfloat16),
        in_specs=[ANY],
        out_specs=ANY,
        scratch_shapes=[
            pltpu.SemaphoreType.DMA((n, 4)),
            pltpu.SemaphoreType.DMA((n, 4)),
            pltpu.SemaphoreType.DMA((4,)),
        ],
        compiler_params=params(3),
    )(cots)
    mean_cot, scale_cot = gathered[0], gathered[1]
    my_columns = lax.dynamic_slice_in_dim(features, me * rows, rows, 1)
    over_classes = (((0,), (0,)), ((), ()))
    feature_part = lax.dot_general(
        mean_cot, mean_rows, over_classes, preferred_element_type=jnp.float32
    ) + lax.dot_general(scale_cot, scale_rows, over_classes, preferred_element_type=jnp.float32)
    mean_grad = jnp.dot(mean_cot, my_columns, preferred_element_type=jnp.float32).T
    scale_grad = jnp.dot(scale_cot, my_columns, preferred_element_type=jnp.float32).T
    feature_grad, step = feature_part, 1
    while step < ncls:
        feature_grad = feature_grad + lax.ppermute(feature_grad, "cls", [(i, i ^ step) for i in range(ncls)])
        step *= 2
    return (mean_grad, scale_grad, feature_grad)


GRAIN = 64
SMALL = 32
NEG = -1e30


def when(cond, fn):
    pl.when(cond)(fn)


class Plan:
    def __init__(self, batch, rows, columns, rank):
        self.batch, self.rows, self.columns, self.rank = batch, rows, columns, rank
        units = columns // UNIT
        edges = [q * units // 4 * UNIT for q in range(5)]
        widest = max(b - a for a, b in zip(edges, edges[1:]))
        self.width = -(-widest // SMALL) * SMALL
        self.padded = -(-self.width // 128) * 128
        self.full = self.width // GRAIN - 1
        self.chunks = self.full + (self.width - self.full * GRAIN) // SMALL
        self.side = self.width // 2
        self.side_full = self.side // GRAIN
        self.rest = self.side - self.side_full * GRAIN
        self.steps = self.side_full + (self.rest > 0)
        self.units = units
        self.extra = max(0, edges[3] + self.width - columns)
        self.starts = edges[:3] + [edges[3] - self.extra]
        self.sizes = [b - a for a, b in zip(self.starts, self.starts[1:] + [columns])]

    def start(self, q):
        return pl.multiple_of(lax.div(q * self.units, 4) * UNIT - self.extra * lax.div(q, 3), UNIT)

    def chunk(self, k, run):
        def tail():
            run(SMALL, pl.multiple_of(self.full * GRAIN + (k - self.full) * SMALL, SMALL))
        when(k < self.full, lambda: run(GRAIN, pl.multiple_of(k * GRAIN, GRAIN)))
        when(k >= self.full, tail)

    def step(self, k, run):
        when(k < self.side_full, lambda: run(GRAIN, pl.multiple_of(k * GRAIN, GRAIN)))
        if self.rest:
            when(k >= self.side_full, lambda: run(self.rest, self.side_full * GRAIN))

    def size(self, q):
        after = lax.div((q + 1) * self.units, 4) * UNIT - self.extra * (lax.div(q + 1, 3) - lax.div(q + 1, 4))
        return after - self.start(q)


def tree(fn, items):
    items = list(items)
    while len(items) > 1:
        items = [fn(*items[i : i + 2]) if i + 1 < len(items) else items[i] for i in range(0, len(items), 2)]
    return items[0]


def softmax_kernel(
    plan, draws, ahead, lag_in, lag_out, relay_in, relay_out,
    feat, mean, scale, factor, noise, labels, cot, part,
    wbuf, sums, arrived, zbuf, low, gate, weight, peak, fcols, fturn, fac, fq, nb, nmat, lab, top, total, lseb, dotb,
    red, whole, acc, acc_in,
    lsem, ysend, yrecv, zsend, zrecv, nsend, nrecv, nstage, nstage_r, rsend, rrecv,
    gzs, gzr, gys, gyr, wsem, csend, crecv,
):
    me, cls = lax.axis_index("draw"), lax.axis_index("cls")
    z, y = lax.div(me, 2), lax.rem(me, 2)
    xx, core = lax.div(cls, 2), lax.rem(cls, 2)
    half = lax.div(z, 2)
    outer = (z == 0) | (z == 3)
    inner = jnp.logical_not(outer)
    edge, mid = 3 * half, 1 + half
    across = 2 - half
    batch, rows, chunks, steps = plan.batch, plan.rows, plan.chunks, plan.steps
    own_q = half * 2 + y
    start = plan.start(own_q)
    valid_rows = plan.size(own_q)
    plane = cls * 2 + y
    heads = (mean, scale)

    def at(zi, yi):
        return (cls, zi * 2 + yi)

    def in_plane(p):
        return (lax.div(p, 2), z * 2 + lax.rem(p, 2))

    barrier = pltpu.get_barrier_semaphore()
    for k in range(1, 8):
        pl.semaphore_signal(barrier, inc=1, device_id=in_plane(lax.rem(plane + k, 8)), device_id_type=MESH)
    for k in range(1, 4):
        pl.semaphore_signal(barrier, inc=1, device_id=at(lax.rem(z + k, 4), y), device_id_type=MESH)

    @pl.when(outer)
    def _():
        for k in range(1, 8):
            p = lax.rem(plane + k, 8)
            pl.semaphore_signal(
                barrier, inc=1, device_id=(lax.div(p, 2), (3 - z) * 2 + lax.rem(p, 2)), device_id_type=MESH
            )

    def remote(src, dst, s, r, device):
        return pltpu.make_async_remote_copy(src, dst, s, r, device_id=device, device_id_type=MESH)

    def local_own(e, h):
        return pltpu.make_async_copy(
            heads[h].at[pl.ds(plan.start(e * 2 + y), plan.width)],
            wbuf.at[e, h, :, pl.ds(pl.multiple_of(y * rows, rows), rows)],
            lsem.at[e * 2 + h],
        )

    feat_copy = pltpu.make_async_copy(
        feat.at[:, pl.ds(pl.multiple_of(z * 2 * rows, 2 * rows), 2 * rows)], fcols, lsem.at[4]
    )
    factor_copy = pltpu.make_async_copy(factor, fac, lsem.at[5])
    label_copy = pltpu.make_async_copy(labels.at[pl.ds(start, plan.width)], lab, lsem.at[6])
    noise_own = pltpu.make_async_copy(
        noise.at[core], nb.at[core, y, z], lsem.at[7]
    )

    def y_copy(e, h, k, grain, row):
        return remote(
            heads[h].at[pl.ds(plan.start(e * 2 + 1 - y) + row, grain)],
            wbuf.at[e, h, pl.ds(row, grain), pl.ds(pl.multiple_of(y * rows, rows), rows)],
            ysend, yrecv.at[k], at(z, 1 - y),
        )

    def y_landed(k, grain, row):
        block = wbuf.at[:, :, pl.ds(row, grain), pl.ds(pl.multiple_of((1 - y) * rows, rows), rows)]
        return remote(block, block, ysend, yrecv.at[k], at(z, 1 - y))

    def y_sent():
        block = wbuf.at[:, :, :, pl.ds(pl.multiple_of(y * rows, rows), rows)]
        return remote(block, block, ysend, yrecv.at[0], at(z, 1 - y))

    def y_start(k):
        def run(grain, row):
            for e in range(2):
                for h in range(2):
                    y_copy(e, h, k, grain, row).start()
        plan.chunk(k, run)

    def z_copy(e, k, grain, row, target):
        block = pl.ds(row, grain)
        return remote(
            sums.at[e, :, block], arrived.at[e, :, block], zsend.at[e], zrecv.at[e, k], at(target, y)
        )

    def noise_copy(e, source):
        return remote(
            noise.at[core], nb.at[core, y, source], nsend.at[e], nrecv.at[source], at(3 * e, y),
        )

    sibling = (xx * 2 + 1 - core, me)

    def stage(n, far_side):
        if n == 0:
            block = nb.at[core, 1 - y if far_side else y]
            return remote(block, block, nstage.at[0], nstage_r.at[0], at(z, 1 - y))
        block = nb.at[1 - core if far_side else core]
        return remote(block, block, nstage.at[1], nstage_r.at[1], sibling)

    feat_copy.start()
    for e in range(2):
        for h in range(2):
            local_own(e, h).start()
    if plan.rank < 64:
        fq[...] = jnp.zeros_like(fq)
        nmat[...] = jnp.zeros_like(nmat)
    factor_copy.start()
    noise_own.start()
    when(outer, lambda: pl.semaphore_wait(barrier, 17))
    when(inner, lambda: pl.semaphore_wait(barrier, 10))
    for k in range(ahead):
        y_start(k)
    for e in range(2):
        when(z != 3 * e, lambda: noise_copy(e, z).start())
    label_copy.start()
    top[...] = jnp.full_like(top, NEG)
    total[...] = jnp.zeros_like(total)
    acc[...] = jnp.zeros_like(acc)
    feat_copy.wait()
    fturn[...] = fcols[...].T
    for e in range(2):
        for h in range(2):
            local_own(e, h).wait()

    def lanes(s):
        return slice(s * batch, (s + 1) * batch)

    def first_pass(grain, row):
        @pl.when(lax.rem(row, 128) == 0)
        def _():
            span = pl.ds(pl.multiple_of(row, 128), 128)
            low[span] = lax.dot_general(
                fq[:, span], nmat[...], (((0,), (0,)), ((), ())), preferred_element_type=jnp.float32
            )
        rows_k = pl.ds(row, grain)
        logit, pre = sums[half, 0, rows_k], sums[half, 1, rows_k]
        offset = row + lax.broadcasted_iota(jnp.int32, (grain, batch), 0)
        valid = offset < valid_rows
        ids = cls * plan.columns + start + offset
        shifted = logit - jnp.where(ids >= CREAL, 30000.0, 0.0)
        fade = jnp.exp(-jnp.abs(pre))
        spread = jnp.maximum(pre, 0.0) + jnp.log1p(fade)
        gate[rows_k] = jnp.where(pre >= 0, 1.0, fade) / (1.0 + fade)
        shifted = jnp.where(valid, shifted, NEG)
        spread = jnp.where(valid, spread, 0.0)
        for s in range(draws):
            value = shifted + spread * low[rows_k, lanes(s)]
            zbuf[rows_k, lanes(s)] = value
            blocks = [value[i * 8 : i * 8 + 8] for i in range(grain // 8)]
            old = top[:, lanes(s)]
            new = jnp.maximum(old, tree(jnp.maximum, blocks))
            grown = tree(jnp.add, [jnp.exp(b - new) for b in blocks])
            total[:, lanes(s)] = total[:, lanes(s)] * jnp.exp(old - new) + grown
            top[:, lanes(s)] = new

    e_first, e_second = 1 - half, half

    def noise_stage(i):
        @pl.when(i == 2)
        def _():
            for k in range(4):
                when(z != k, lambda: noise_copy(half, k).wait_recv())
            noise_own.wait()
            stage(0, False).start()

        @pl.when(i == 4)
        def _():
            stage(0, True).wait_recv()
            stage(1, False).start()

        @pl.when(i == 3)
        def _():
            factor_copy.wait()
            for q in range(4):
                def pick(q=q):
                    fq[: plan.rank, : plan.width] = fac[:, plan.starts[q] : plan.starts[q] + plan.width]
                when(own_q == q, pick)

        @pl.when(i == 5)
        def _():
            stage(1, True).wait_recv()
            for j in range(2):
                for yi in range(2):
                    for zi in range(4):
                        nmat[: plan.rank, lanes((j * 2 + yi) * 4 + zi)] = nb[j, yi, zi]

    def own_sums(i, grain, row):
        when(i + ahead < chunks, lambda: y_start(i + ahead))
        y_landed(i, grain, row).wait_recv()
        block = pl.ds(row, grain)
        lhs = jnp.concatenate([wbuf[e, h, block] for e in range(2) for h in range(2)], axis=0)
        value = lax.dot_general(
            lhs, fturn[...], (((1,), (0,)), ((), ())), preferred_element_type=jnp.float32
        )
        sums[:, :, block] = value.reshape(2, 2, grain, batch)

    def add_arrived(e, k, grain, row):
        z_copy(e, k, grain, row, mid).wait_recv()
        block = pl.ds(row, grain)
        sums[e, :, block] = sums[e, :, block] + arrived[e, :, block]

    def forward_inner(i, carry):
        def first(grain, row):
            own_sums(i, grain, row)
            add_arrived(e_first, i, grain, row)
            z_copy(e_first, i, grain, row, across).start()

        def second(grain, row):
            add_arrived(e_second, i - lag_in, grain, row)
            z_copy(e_second, i - lag_in, grain, row, edge).start()

        when(i < chunks, lambda: plan.chunk(i, first))
        when(i >= lag_in, lambda: plan.chunk(i - lag_in, second))
        return carry

    def forward_outer(i, carry):
        def first(grain, row):
            own_sums(i, grain, row)
            z_copy(e_first, i, grain, row, mid).start()

        def second(grain, row):
            add_arrived(e_second, i - lag_out, grain, row)
            first_pass(grain, row)

        when(i < chunks, lambda: plan.chunk(i, first))
        noise_stage(i)
        when(i >= lag_out, lambda: plan.chunk(i - lag_out, second))
        return carry

    @pl.when(inner)
    def _():
        lax.fori_loop(0, chunks + lag_in, forward_inner, 0)

    @pl.when(outer)
    def _():
        lax.fori_loop(0, chunks + lag_out, forward_outer, 0)

    whole_copies = [pltpu.make_async_copy(heads[h], whole.at[h], wsem.at[h]) for h in range(2)]
    for copy in whole_copies:
        copy.start()
    label_copy.wait()

    @pl.when(inner)
    def _():
        factor_copy.wait()
        noise_own.wait()

    spot = half * 8 + plane

    def end_device(p):
        return (lax.div(lax.rem(p, 8), 2), lax.div(p, 8) * 6 + lax.rem(p, 2))

    def red_copy(kind, slot, k, p):
        return remote(red.at[kind, slot], red.at[kind, slot], rsend.at[kind, k], rrecv.at[kind, slot], end_device(p))

    def log_merge(parts):
        best = tree(jnp.maximum, parts)
        return best + jnp.log(tree(jnp.add, [jnp.exp(p - best) for p in parts]))

    def fan_out(target, value):
        for s in range(draws):
            target[:, lanes(s)] = jnp.broadcast_to(value[s : s + 1], (8, batch))

    def reduce_all(kind, merge):
        for k in range(8, 16):
            red_copy(kind, spot, k, lax.rem(spot + k, 16)).start()
        for k in range(1, 8):
            red_copy(kind, spot, k, lax.rem(spot + k, 16)).start()
        for k in range(1, 16):
            source = lax.rem(spot + 16 - k, 16)
            red_copy(kind, source, k, source).wait_recv()
        return merge([red[kind, p] for p in range(16)])

    @pl.when(outer)
    def _():
        for s in range(draws):
            m = top[:, lanes(s)]
            best = jnp.max(m, axis=0, keepdims=True)
            size = jnp.sum(total[:, lanes(s)] * jnp.exp(m - best), axis=0, keepdims=True)
            red[0, spot, s : s + 1, :] = best + jnp.log(size)
        fan_out(lseb, reduce_all(0, log_merge))

        def second_pass(r, sums_in):
            block = pl.ds(pl.multiple_of(r * 8, 8), 8)
            logs = [zbuf[block, lanes(s)] - lseb[:, lanes(s)] for s in range(draws)]
            best = tree(jnp.maximum, logs)
            risen = [jnp.exp(v - best) for v in logs]
            offset = r * 8 + lax.broadcasted_iota(jnp.int32, (8, batch), 0)
            share = jnp.where(offset < valid_rows, lab[block] / tree(jnp.add, risen), 0.0)
            peak[block] = jnp.exp(best) * (1.0 / batch)
            weight[block] = share * (1.0 / batch)
            for s in range(draws):
                zbuf[block, lanes(s)] = risen[s]
            return tuple(a + share * v for a, v in zip(sums_in, risen))

        dots = lax.fori_loop(
            0, plan.width // 8, second_pass, tuple(jnp.zeros((8, batch), jnp.float32) for _ in range(draws)),
            unroll=4,
        )
        for s in range(draws):
            red[1, spot, s : s + 1, :] = jnp.sum(dots[s], axis=0, keepdims=True)
        fan_out(dotb, reduce_all(1, lambda parts: tree(jnp.add, parts)))

    def cot_chunk(grain, row):
        def body(b, carry):
            means, scales = [], []
            for part in range(2):
                block = pl.ds(pl.multiple_of(row + b * 16 + part * 8, 8), 8)
                eb, wt = peak[block], weight[block]
                terms = [zbuf[block, lanes(s)] * (eb * dotb[:, lanes(s)] - wt) for s in range(draws)]
                means.append(tree(jnp.add, terms))
                scales.append(
                    tree(jnp.add, [t * low[block, lanes(s)] for s, t in enumerate(terms)]) * gate[block]
                )
            inside = pl.ds(pl.multiple_of(row + b * 16, 16), 16)
            cot[own_q, inside, :batch] = jnp.concatenate(means, axis=0).astype(jnp.bfloat16)
            cot[own_q, inside, batch:] = jnp.concatenate(scales, axis=0).astype(jnp.bfloat16)
            return carry
        lax.fori_loop(0, grain // 16, body, 0)

    side = plan.side

    def gz(e, kind, k, grain, row, target):
        block = cot.at[e * 2 + (y if kind < 2 else 1 - y), pl.ds(row + (side if kind == 1 else 0), grain)]
        return remote(block, block, gzs.at[e, kind], gzr.at[e, kind, k], at(target, y))

    def gy(e, kind, k, grain, row, line):
        block = cot.at[e * 2 + line, pl.ds(row + side * kind, grain)]
        return remote(block, block, gys.at[e, kind], gyr.at[e, kind, k], at(z, 1 - y))

    def relay(e, i, target):
        def pass_on(kind, k, grain, row):
            gz(e, kind, k, grain, row, mid).wait_recv()
            if target is not None:
                gz(e, kind, k, grain, row, target).start()

        def early(grain, row):
            pass_on(1, i, grain, row)
            gy(e, 1, i, grain, row, y).start()

        def late(grain, row):
            pass_on(0, i - steps, grain, row)
            pass_on(2, i - steps, grain, row)

        when((i >= 0) & (i < steps), lambda: plan.step(i, early))
        when((i >= steps) & (i < 2 * steps), lambda: plan.step(i - steps, late))

    def absorb(j, grain, row):
        for e in range(2):
            gy(e, 1, j, grain, row, 1 - y).wait_recv()
        for kind in range(2):
            for h in range(2):
                lhs = jnp.concatenate(
                    [cot[q, pl.ds(row + kind * side, grain), h * batch : (h + 1) * batch] for q in range(4)], axis=0
                )
                rhs = jnp.concatenate(
                    [
                        whole[h, pl.ds(pl.multiple_of(plan.starts[q] + kind * side + row, UNIT), grain)]
                        for q in range(4)
                    ],
                    axis=0,
                )
                acc[...] += lax.dot_general(
                    lhs, rhs, (((0,), (0,)), ((), ())), preferred_element_type=jnp.float32
                )

    for copy in whole_copies:
        copy.wait()

    def gather(i, carry):
        @pl.when(outer)
        def _():
            def early(grain, row):
                cot_chunk(grain, row)
                gy(half, 0, i, grain, row, y).start()
                cot_chunk(grain, row + side)
                gz(half, 1, i, grain, row, mid).start()

            def late(grain, row):
                k = i - steps
                gz(half, 0, k, grain, row, mid).start()
                gy(half, 1, k, grain, row, y).start()
                gy(half, 0, k, grain, row, 1 - y).wait_recv()
                gz(half, 2, k, grain, row, mid).start()

            when(i < steps, lambda: plan.step(i, early))
            when((i >= steps) & (i < 2 * steps), lambda: plan.step(i - steps, late))
            relay(1 - half, i - relay_out, None)

        @pl.when(inner)
        def _():
            relay(half, i, across)
            relay(1 - half, i - relay_in, edge)
        last = i - relay_out - steps
        when(last >= 0, lambda: plan.step(last, functools.partial(absorb, last)))
        return carry

    lax.fori_loop(0, 2 * steps + relay_out, gather, 0)

    twin = remote(acc, acc_in, csend, crecv, sibling)
    twin.start()
    twin.wait_recv()
    part[...] = acc[...] + acc_in[...]

    def relayed(e, kind):
        block = cot.at[e * 2, pl.ds(kind % 2 * side, side)]
        return remote(block, block, gzs.at[e, kind], gzr.at[e, kind, 0], at(mid, y))

    def crossed(e, kind):
        block = cot.at[e * 2, pl.ds(kind * side, side)]
        return remote(block, block, gys.at[e, kind], gyr.at[e, kind, 0], at(z, 1 - y))

    for kind in range(3):
        relayed(half, kind).wait_send()
        when(inner, lambda: relayed(1 - half, kind).wait_send())
    for e in range(2):
        crossed(e, 1).wait_send()
    when(outer, lambda: crossed(half, 0).wait_send())
    def z_sent(e):
        return remote(arrived.at[e], arrived.at[e], zsend.at[e], zrecv.at[e, 0], at(mid, y))

    y_sent().wait_send()
    z_sent(e_first).wait_send()
    when(inner, lambda: z_sent(e_second).wait_send())
    twin.wait_send()
    for e in range(2):
        when(z != 3 * e, lambda: noise_copy(e, z).wait_send())

    @pl.when(outer)
    def _():
        for n in range(2):
            stage(n, False).wait_send()
        for kind in range(2):
            for k in range(1, 16):
                red_copy(kind, spot, k, lax.rem(spot + k, 16)).wait_send()


def head_kernel(plan, cot, feat_in, mean_out, scale_out, cols_in, stage, loads, sems):
    batch, rows = plan.batch, plan.rows
    me = lax.axis_index("draw")
    feat_copy = pltpu.make_async_copy(
        feat_in.at[:, pl.ds(pl.multiple_of(me * rows, rows), rows)], cols_in, loads
    )

    feat_copy.start()
    feat_copy.wait()
    cols = cols_in[...]
    blank = jnp.zeros_like(cols)
    rhs = jnp.concatenate(
        [jnp.concatenate([cols, blank], axis=1), jnp.concatenate([blank, cols], axis=1)], axis=0
    )
    outs = (mean_out, scale_out)
    copies = []
    for q in range(4):
        size, first = plan.sizes[q], plan.starts[q]
        for part in range(2):
            begin = part * plan.side
            count = min(plan.side, size - begin)
            value = jnp.dot(cot[q, begin : begin + count], rhs, preferred_element_type=jnp.float32)
            spot = slice(first + begin, first + begin + count)
            for h in range(2):
                stage[h, spot] = value[:, h * rows : (h + 1) * rows]
                copy = pltpu.make_async_copy(stage.at[h, spot], outs[h].at[spot], sems.at[h, q * 2 + part])
                copy.start()
                copies.append(copy)
    for copy in copies:
        copy.wait()


def in_hbm(x):
    return pltpu.with_memory_space_constraint(x, pltpu.HBM)


def ends_on_device(features, mean_head, scale_head, factor, noise, labels):
    rows, columns = mean_head.shape
    batch = features.shape[0]
    own, rank = noise.shape[0], noise.shape[2]
    draws = own * 8
    plan = Plan(batch, rows, columns, rank)
    width, chunks, steps = plan.width, plan.chunks, plan.steps
    mean_rows, scale_rows = mean_head.T, scale_head.T
    noise_t = noise.transpose(0, 2, 1)
    dma = pltpu.SemaphoreType.DMA
    f32, bf16 = jnp.float32, jnp.bfloat16
    cot, part = pl.pallas_call(
        functools.partial(softmax_kernel, plan, draws, 3, 3, 9, 4, 10),
        out_shape=(
            jax.ShapeDtypeStruct((4, width, 2 * batch), bf16),
            jax.ShapeDtypeStruct((batch, rows), f32),
        ),
        in_specs=[HBM] * 4 + [ANY, HBM],
        out_specs=(VMEM, VMEM),
        scratch_shapes=[
            pltpu.VMEM((2, 2, width, 2 * rows), bf16),
            pltpu.VMEM((2, 2, width, batch), f32),
            pltpu.VMEM((2, 2, width, batch), f32),
            pltpu.VMEM((width, draws * batch), f32),
            pltpu.VMEM((plan.padded, draws * batch), f32),
            pltpu.VMEM((width, batch), f32),
            pltpu.VMEM((width, batch), f32),
            pltpu.VMEM((width, batch), f32),
            pltpu.VMEM((batch, 2 * rows), bf16),
            pltpu.VMEM((2 * rows, batch), bf16),
            pltpu.VMEM((rank, columns), bf16),
            pltpu.VMEM((64, plan.padded), bf16),
            pltpu.VMEM((2, 2, 4, rank, batch), bf16),
            pltpu.VMEM((64, draws * batch), bf16),
            pltpu.VMEM((width, batch), f32),
            pltpu.VMEM((8, draws * batch), f32),
            pltpu.VMEM((8, draws * batch), f32),
            pltpu.VMEM((8, draws * batch), f32),
            pltpu.VMEM((8, draws * batch), f32),
            pltpu.VMEM((2, 16, draws, batch), f32),
            pltpu.VMEM((2, columns, rows), bf16),
            pltpu.VMEM((batch, rows), f32),
            pltpu.VMEM((batch, rows), f32),
            dma((8,)),
            dma,
            dma((chunks,)),
            dma((2,)),
            dma((2, chunks)),
            dma((2,)),
            dma((4,)),
            dma((2,)),
            dma((2,)),
            dma((2, 16)),
            dma((2, 16)),
            dma((2, 3)),
            dma((2, 3, steps)),
            dma((2, 2)),
            dma((2, 2, steps)),
            dma((2,)),
            dma,
            dma,
        ],
        compiler_params=params(0, 50),
    )(in_hbm(features), in_hbm(mean_rows), in_hbm(scale_rows), in_hbm(factor.T), noise_t, in_hbm(labels.T))

    other = lax.ppermute(part, "cls", [(i, i ^ 2) for i in range(4)])
    mean_grad, scale_grad = pl.pallas_call(
        functools.partial(head_kernel, plan),
        out_shape=(jax.ShapeDtypeStruct((columns, rows), f32),) * 2,
        in_specs=[VMEM, HBM],
        out_specs=(HBM, HBM),
        scratch_shapes=[
            pltpu.VMEM((batch, rows), bf16),
            pltpu.VMEM((2, columns, rows), f32),
            dma,
            dma((2, 8)),
        ],
        compiler_params=pltpu.CompilerParams(vmem_limit_bytes=32 * 2**20),
        cost_estimate=pl.CostEstimate(
            flops=8 * columns * batch * rows, bytes_accessed=16 * columns * rows, transcendentals=0
        ),
    )(cot, features)
    return (mean_grad.T, scale_grad.T, part + other)


def solution(mesh):
    ends = dict(mesh.shape) == {"cls": 4, "draw": 8}
    return jax.shard_map(
        ends_on_device if ends else on_device,
        mesh=mesh,
        in_specs=(
            P(),
            P("draw", "cls"),
            P("draw", "cls"),
            P("cls", None),
            P("draw", None, None),
            P(None, "cls"),
        ),
        out_specs=(P("draw", "cls"), P("draw", "cls"), P(None, "draw")),
        check_vma=False,
    )
```

```python
import functools
import jax
import jax.numpy as jnp
from jax import lax
from jax.experimental import pallas as pl
from jax.experimental.pallas import tpu as pltpu
from jax.sharding import PartitionSpec as P

CREAL = 21843
UNIT = 16
MESH = pl.DeviceIdType.MESH
ANY = pl.BlockSpec(memory_space=pl.ANY)
VMEM = pl.BlockSpec(memory_space=pltpu.VMEM)
HBM = pl.BlockSpec(memory_space=pltpu.HBM)


def start_of(owner, n, units):
    return lax.div(owner * units, n)


def at_width(owner, n, units, run):
    base = units // n
    wide = start_of(owner + 1, n, units) - start_of(owner, n, units) > base
    pl.when(wide)(functools.partial(run, (base + 1) * UNIT))
    pl.when(jnp.logical_not(wide))(functools.partial(run, base * UNIT))


def exchange_kernel(
    n, units, feat, mean, scale, noise, logits, noise_out, held, part_out, part_in,
    send, recv, part_send, part_recv, nsend, nrecv, local, nlocal,
):
    me, cls = lax.axis_index("draw"), lax.axis_index("cls")
    half, rows = n // 2, mean.shape[1]
    mirror = lax.rem(me + half, n)
    base, spot = lax.div(me, half) * half, lax.rem(me, half)
    barrier = pltpu.get_barrier_semaphore()
    for k in range(1, n):
        pl.semaphore_signal(barrier, inc=1, device_id=(cls, lax.rem(me + k, n)), device_id_type=MESH)
    pl.semaphore_wait(barrier, n - 1)

    def remote(source, target, send_sem, recv_sem, device):
        return pltpu.make_async_remote_copy(
            source, target, send_sem, recv_sem, device_id=(cls, device), device_id_type=MESH
        )

    def noise_copy(slot, k, device):
        return remote(noise, noise_out.at[slot], nsend.at[k], nrecv.at[slot], device)

    def block(head, owner, width):
        start = pl.multiple_of(start_of(owner, n, units) * UNIT, UNIT)
        return (mean, scale)[head].at[pl.ds(start, width)]

    def block_copy(far, head, owner, k, source, device, act):
        at_width(
            owner, n, units,
            lambda w: act(
                remote(
                    block(head, owner, w), held.at[far, head, source, pl.ds(0, w)],
                    send.at[far, head, k], recv.at[far, head, source], device,
                )
            ),
        )

    def own_copy(far, head, act):
        owner = mirror if far else me
        at_width(
            owner, n, units,
            lambda w: act(
                pltpu.make_async_copy(
                    block(head, owner, w), held.at[far, head, spot, pl.ds(0, w)], local.at[far, head]
                )
            ),
        )

    def sends(far, head, act):
        for k in range(1, half):
            peer = base + lax.rem(spot + k, half)
            block_copy(far, head, lax.rem(peer + half, n) if far else peer, k, spot, peer, act)

    def columns_of(source):
        if rows % 128:
            return feat[source]
        return feat[:, pl.ds(pl.multiple_of(source * rows, rows), rows)]

    def arrive(far, head):
        owner = mirror if far else me
        for k in range(1, half):
            source = lax.rem(spot + half - k, half)
            block_copy(far, head, owner, k, source, base + source, lambda c: c.wait_recv())
        own_copy(far, head, lambda c: c.wait())
        total = None
        for source in range(half):
            term = lax.dot_general(
                held[far, head, source], columns_of(base + source), (((1,), (1,)), ((), ())),
                preferred_element_type=jnp.float32,
            )
            total = term if total is None else total + term
        return total

    def part_copy(head):
        return remote(part_out.at[head], part_in.at[head], part_send.at[head], part_recv.at[head], mirror)

    own_noise = pltpu.make_async_copy(noise, noise_out.at[me], nlocal)
    stages = [(1, 0), (1, 1), (0, 0), (0, 1)]
    sends(1, 0, lambda c: c.start())
    for k in range(1, n):
        noise_copy(me, k, lax.rem(me + k, n)).start()
    for far, head in stages[1:]:
        sends(far, head, lambda c: c.start())
    for far, head in stages:
        own_copy(far, head, lambda c: c.start())
    own_noise.start()
    for head in range(2):
        part_out[head] = arrive(1, head)
        part_copy(head).start()
    for head in range(2):
        logits[head] = arrive(0, head)
    for k in range(1, n):
        source = lax.rem(me + n - k, n)
        noise_copy(source, k, source).wait_recv()
    own_noise.wait()
    for head in range(2):
        part_copy(head).wait_recv()
        logits[head] = logits[head] + part_in[head]
    for far, head in stages:
        sends(far, head, lambda c: c.wait_send())
    for k in range(1, n):
        noise_copy(me, k, lax.rem(me + k, n)).wait_send()
    for head in range(2):
        part_copy(head).wait_send()


def gather_kernel(n, units, cot, out, send, recv, local):
    me, cls = lax.axis_index("draw"), lax.axis_index("cls")
    half = n // 2
    group, side = lax.div(me, 2), lax.rem(me, 2)
    partner = group * 2 + 1 - side
    split = units // n // 2 * UNIT
    pieces = [(head, part) for head in range(2) for part in range(2)]
    barrier = pltpu.get_barrier_semaphore()
    peers = [partner] + [lax.rem(group + k, half) * 2 + side for k in range(1, half)]
    for peer in peers:
        pl.semaphore_signal(barrier, inc=1, device_id=(cls, peer), device_id_type=MESH)
    pl.semaphore_wait(barrier, half)

    def source(piece, width):
        head, part = pieces[piece]
        return cot.at[head, pl.ds(split, width - split) if part else pl.ds(0, split)]

    def place(piece, owner, width):
        head, part = pieces[piece]
        start = start_of(owner, n, units) * UNIT + part * split
        return out.at[head, pl.ds(pl.multiple_of(start, UNIT), width - split if part else split)]

    def send_own(piece, owner, slot, device, act):
        at_width(
            owner, n, units,
            lambda w: act(
                pltpu.make_async_remote_copy(
                    source(piece, w), place(piece, owner, w), send.at[slot, piece], recv.at[owner, piece],
                    device_id=(cls, device), device_id_type=MESH,
                )
            ),
        )

    def forward(piece, owner, slot, act):
        at_width(
            owner, n, units,
            lambda w: act(
                pltpu.make_async_remote_copy(
                    place(piece, owner, w), place(piece, owner, w), send.at[slot, piece], recv.at[owner, piece],
                    device_id=(cls, partner), device_id_type=MESH,
                )
            ),
        )

    def own(piece, act):
        at_width(
            me, n, units,
            lambda w: act(pltpu.make_async_copy(source(piece, w), place(piece, me, w), local.at[piece])),
        )

    count = len(pieces)
    for piece in range(count):
        for k in range(1, half):
            send_own(piece, me, k, peers[k], lambda c: c.start())
        send_own(piece, me, 0, partner, lambda c: c.start())
    for piece in range(count):
        own(piece, lambda c: c.start())
    order = sorted(range(1, half), key=lambda k: min(k, half - k))
    for piece in range(count):
        for k in order:
            send_own(piece, peers[k], k, peers[k], lambda c: c.wait_recv())
            forward(piece, peers[k], half + k, lambda c: c.start())
    for piece in range(count):
        send_own(piece, partner, 0, partner, lambda c: c.wait_recv())
        for k in range(1, half):
            owner = lax.rem(group + k, half) * 2 + 1 - side
            forward(piece, owner, half + k, lambda c: c.wait_recv())
    for piece in range(count):
        for k in range(half):
            send_own(piece, me, k, peers[k], lambda c: c.wait_send())
        for k in range(1, half):
            forward(piece, peers[k], half + k, lambda c: c.wait_send())
        own(piece, lambda c: c.wait())


def merge(slots, count, softmax):
    if not softmax:
        total = slots[0]
        for i in range(1, count):
            total = total + slots[i]
        return total
    top = slots[0, 0]
    for i in range(1, count):
        top = jnp.maximum(top, slots[i, 0])
    total = jnp.zeros_like(top)
    for i in range(count):
        total = total + slots[i, 1] * jnp.exp(slots[i, 0] - top)
    return jnp.stack((top, total))


def reduce_kernel(counts, softmax, x, out, *scratch):
    levels = len(counts)
    slots, sends, recvs = scratch[:levels], scratch[levels : 2 * levels], scratch[2 * levels :]
    cls, draw = lax.axis_index("cls"), lax.axis_index("draw")

    def device(level, index):
        return (index, draw) if level == 0 else (cls, index)

    barrier = pltpu.get_barrier_semaphore()
    for level, n in enumerate(counts):
        me = (cls, draw)[level]
        for k in range(1, n):
            pl.semaphore_signal(
                barrier, inc=1, device_id=device(level, lax.rem(me + k, n)), device_id_type=MESH
            )
    pl.semaphore_wait(barrier, sum(counts) - levels)
    value = x[...]
    for level, n in enumerate(counts):
        me = (cls, draw)[level]
        held = slots[level]
        held[me] = value

        def copy(slot, k, target):
            return pltpu.make_async_remote_copy(
                held.at[slot], held.at[slot], sends[level].at[k], recvs[level].at[slot],
                device_id=device(level, target), device_id_type=MESH,
            )

        for k in range(1, n):
            copy(me, k, lax.rem(me + k, n)).start()
        for k in range(1, n):
            source = lax.rem(me + n - k, n)
            copy(source, k, source).wait_recv()
        for k in range(1, n):
            copy(me, k, lax.rem(me + k, n)).wait_send()
        value = merge(held, n, softmax)
    if softmax:
        out[...] = value[0] + jnp.log(value[1])
    else:
        out[...] = value


def params(collective_id, grant=32):
    return pltpu.CompilerParams(
        collective_id=collective_id, has_side_effects=True, vmem_limit_bytes=grant * 2**20
    )


def reduce_over(x, counts, softmax, collective_id):
    shape = x.shape[1:] if softmax else x.shape
    return pl.pallas_call(
        functools.partial(reduce_kernel, counts, softmax),
        out_shape=jax.ShapeDtypeStruct(shape, jnp.float32),
        in_specs=[VMEM],
        out_specs=VMEM,
        scratch_shapes=[pltpu.VMEM((n,) + x.shape, jnp.float32) for n in counts]
        + [pltpu.SemaphoreType.DMA((n,)) for n in counts]
        + [pltpu.SemaphoreType.DMA((n,)) for n in counts],
        compiler_params=params(collective_id),
    )(x)


def on_device(features, mean_head, scale_head, factor, noise, labels):
    rows, columns = mean_head.shape
    batch = features.shape[0]
    n, ncls = lax.axis_size("draw"), lax.axis_size("cls")
    me = lax.axis_index("draw")
    units = columns // UNIT
    tile = -(-units // n) * UNIT
    own, rank = noise.shape[0], noise.shape[2]
    draws = own * n
    mean_rows, scale_rows = mean_head.T, scale_head.T
    half = n // 2
    feat = features.reshape(batch, n, rows).transpose(1, 0, 2) if rows % 128 else features

    heads, noise_t = pl.pallas_call(
        functools.partial(exchange_kernel, n, units),
        out_shape=(
            jax.ShapeDtypeStruct((2, tile, batch), jnp.float32),
            jax.ShapeDtypeStruct((n, own, rank, batch), jnp.bfloat16),
        ),
        in_specs=[VMEM] + [ANY] * 3,
        out_specs=(VMEM, ANY),
        scratch_shapes=[
            pltpu.VMEM((2, 2, half, tile, rows), jnp.bfloat16),
            pltpu.VMEM((2, tile, batch), jnp.float32),
            pltpu.VMEM((2, tile, batch), jnp.float32),
            pltpu.SemaphoreType.DMA((2, 2, half)),
            pltpu.SemaphoreType.DMA((2, 2, half)),
            pltpu.SemaphoreType.DMA((2,)),
            pltpu.SemaphoreType.DMA((2,)),
            pltpu.SemaphoreType.DMA((n,)),
            pltpu.SemaphoreType.DMA((n,)),
            pltpu.SemaphoreType.DMA((2, 2)),
            pltpu.SemaphoreType.DMA,
        ],
        compiler_params=params(0),
    )(feat, mean_rows, scale_rows, noise.transpose(0, 2, 1))

    first = start_of(me, n, units) * UNIT
    width = start_of(me + 1, n, units) * UNIT - first
    offsets = jnp.arange(tile, dtype=jnp.int32)[:, None]
    valid = offsets < width
    class_ids = lax.axis_index("cls") * columns + first + offsets
    shift = jnp.where(class_ids >= CREAL, 30000.0, 0.0).astype(jnp.float32)
    my_factor = lax.dynamic_slice_in_dim(factor.T, first, tile, 1)
    my_labels = jnp.where(valid, lax.dynamic_slice_in_dim(labels.T, first, tile, 0), 0.0)

    mean_logit, scale_pre = heads[0], heads[1]
    scale_pre = jnp.where(valid, scale_pre, 0.0)
    spread = jax.nn.softplus(scale_pre)
    lowrank = jnp.einsum(
        "rc,srb->scb", my_factor, noise_t.reshape(draws, rank, batch), preferred_element_type=jnp.float32
    )
    logits = mean_logit[None] + spread[None] * lowrank - shift[None]
    logits = jnp.where(valid[None], logits, -1e30)
    local_top = jnp.max(logits, axis=1)
    local_total = jnp.sum(jnp.exp(logits - local_top[:, None]), axis=1)
    lse = reduce_over(jnp.stack((local_top, local_total)), (ncls, n), True, 1)
    log_prob = logits - lse[:, None]
    best = jnp.max(log_prob, axis=0)
    risen = jnp.exp(log_prob - best[None])
    inverse = 1.0 / jnp.sum(risen, axis=0)
    weight = my_labels * inverse
    label_dot = reduce_over(jnp.sum(weight[None] * risen, axis=1), (ncls, n), False, 2)
    logit_cot = risen * ((jnp.exp(best) / batch)[None] * label_dot[:, None] - (weight / batch)[None])
    dmean = jnp.sum(logit_cot, axis=0)
    dspread = jnp.sum(logit_cot * lowrank, axis=0)
    cots = jnp.stack((dmean, dspread * jax.nn.sigmoid(scale_pre))).astype(jnp.bfloat16)

    gathered = pl.pallas_call(
        functools.partial(gather_kernel, n, units),
        out_shape=jax.ShapeDtypeStruct((2, columns, batch), jnp.bfloat16),
        in_specs=[ANY],
        out_specs=ANY,
        scratch_shapes=[
            pltpu.SemaphoreType.DMA((n, 4)),
            pltpu.SemaphoreType.DMA((n, 4)),
            pltpu.SemaphoreType.DMA((4,)),
        ],
        compiler_params=params(3),
    )(cots)
    mean_cot, scale_cot = gathered[0], gathered[1]
    my_columns = lax.dynamic_slice_in_dim(features, me * rows, rows, 1)
    over_classes = (((0,), (0,)), ((), ()))
    feature_part = lax.dot_general(
        mean_cot, mean_rows, over_classes, preferred_element_type=jnp.float32
    ) + lax.dot_general(scale_cot, scale_rows, over_classes, preferred_element_type=jnp.float32)
    mean_grad = jnp.dot(mean_cot, my_columns, preferred_element_type=jnp.float32).T
    scale_grad = jnp.dot(scale_cot, my_columns, preferred_element_type=jnp.float32).T
    feature_grad, step = feature_part, 1
    while step < ncls:
        feature_grad = feature_grad + lax.ppermute(feature_grad, "cls", [(i, i ^ step) for i in range(ncls)])
        step *= 2
    return (mean_grad, scale_grad, feature_grad)


GRAIN = 64
SMALL = 32
FINE = 1
NEG = -1e30
LOG2E = 1.4426950408889634


def when(cond, fn):
    pl.when(cond)(fn)


class Plan:
    def __init__(self, batch, rows, columns, rank):
        self.batch, self.rows, self.columns, self.rank = batch, rows, columns, rank
        units = columns // UNIT
        edges = [q * units // 4 * UNIT for q in range(5)]
        widest = max(b - a for a, b in zip(edges, edges[1:]))
        self.width = -(-widest // SMALL) * SMALL
        self.padded = -(-self.width // 128) * 128
        self.full = self.width // GRAIN - 1
        self.chunks = self.full + (self.width - self.full * GRAIN) // SMALL
        self.side = self.width // 2
        self.side_full = self.side // GRAIN
        self.rest = self.side - self.side_full * GRAIN
        self.steps = self.side_full + (self.rest > 0)
        self.units = units
        self.extra = max(0, edges[3] + self.width - columns)
        self.starts = edges[:3] + [edges[3] - self.extra]
        self.sizes = [b - a for a, b in zip(self.starts, self.starts[1:] + [columns])]

    def start(self, q):
        return pl.multiple_of(lax.div(q * self.units, 4) * UNIT - self.extra * lax.div(q, 3), UNIT)

    def chunk(self, k, run):
        def tail():
            run(SMALL, pl.multiple_of(self.full * GRAIN + (k - self.full) * SMALL, SMALL))
        when(k < self.full, lambda: run(GRAIN, pl.multiple_of(k * GRAIN, GRAIN)))
        when(k >= self.full, tail)

    def step(self, k, run):
        when(k < self.side_full, lambda: run(GRAIN, pl.multiple_of(k * GRAIN, GRAIN)))
        if self.rest:
            when(k >= self.side_full, lambda: run(self.rest, self.side_full * GRAIN))

    def size(self, q):
        after = lax.div((q + 1) * self.units, 4) * UNIT - self.extra * (lax.div(q + 1, 3) - lax.div(q + 1, 4))
        return after - self.start(q)


def tree(fn, items):
    items = list(items)
    while len(items) > 1:
        items = [fn(*items[i : i + 2]) if i + 1 < len(items) else items[i] for i in range(0, len(items), 2)]
    return items[0]


def softmax_kernel(
    plan, draws, ahead, lag_in, lag_out, relay_in, relay_out,
    feat, mean, scale, factor, noise, labels, cot, part,
    wbuf, sums, arrived, zbuf, low, gate, weight, peak, fcols, fturn, fac, fq, nb, nmat, lab, top, total, lseb, dotb,
    red, whole, acc, acc_in,
    lsem, ysend, yrecv, zsend, zrecv, nsend, nrecv, nstage, nstage_r, rsend, rrecv,
    gzs, gzr, gys, gyr, wsem, csend, crecv,
):
    me, cls = lax.axis_index("draw"), lax.axis_index("cls")
    z, y = lax.div(me, 2), lax.rem(me, 2)
    xx, core = lax.div(cls, 2), lax.rem(cls, 2)
    half = lax.div(z, 2)
    outer = (z == 0) | (z == 3)
    inner = jnp.logical_not(outer)
    edge, mid = 3 * half, 1 + half
    across = 2 - half
    batch, rows, chunks, steps = plan.batch, plan.rows, plan.chunks, plan.steps
    own_q = half * 2 + y
    start = plan.start(own_q)
    valid_rows = plan.size(own_q)
    plane = cls * 2 + y
    heads = (mean, scale)

    def at(zi, yi):
        return (cls, zi * 2 + yi)

    def in_plane(p):
        return (lax.div(p, 2), z * 2 + lax.rem(p, 2))

    barrier = pltpu.get_barrier_semaphore()
    for k in range(1, 8):
        pl.semaphore_signal(barrier, inc=1, device_id=in_plane(lax.rem(plane + k, 8)), device_id_type=MESH)
    for k in range(1, 4):
        pl.semaphore_signal(barrier, inc=1, device_id=at(lax.rem(z + k, 4), y), device_id_type=MESH)

    @pl.when(outer)
    def _():
        for k in range(1, 8):
            p = lax.rem(plane + k, 8)
            pl.semaphore_signal(
                barrier, inc=1, device_id=(lax.div(p, 2), (3 - z) * 2 + lax.rem(p, 2)), device_id_type=MESH
            )

    def remote(src, dst, s, r, device):
        return pltpu.make_async_remote_copy(src, dst, s, r, device_id=device, device_id_type=MESH)

    def local_own(e, h):
        return pltpu.make_async_copy(
            heads[h].at[pl.ds(plan.start(e * 2 + y), plan.width)],
            wbuf.at[e, h, :, pl.ds(pl.multiple_of(y * rows, rows), rows)],
            lsem.at[e * 2 + h],
        )

    feat_copy = pltpu.make_async_copy(
        feat.at[:, pl.ds(pl.multiple_of(z * 2 * rows, 2 * rows), 2 * rows)], fcols, lsem.at[4]
    )
    factor_copy = pltpu.make_async_copy(factor, fac, lsem.at[5])
    label_copy = pltpu.make_async_copy(labels.at[pl.ds(start, plan.width)], lab, lsem.at[6])
    noise_own = pltpu.make_async_copy(
        noise.at[core], nb.at[core, y, z], lsem.at[7]
    )

    def y_copy(e, h, k, grain, row):
        return remote(
            heads[h].at[pl.ds(plan.start(e * 2 + 1 - y) + row, grain)],
            wbuf.at[e, h, pl.ds(row, grain), pl.ds(pl.multiple_of(y * rows, rows), rows)],
            ysend, yrecv.at[k], at(z, 1 - y),
        )

    def y_landed(k, grain, row):
        block = wbuf.at[:, :, pl.ds(row, grain), pl.ds(pl.multiple_of((1 - y) * rows, rows), rows)]
        return remote(block, block, ysend, yrecv.at[k], at(z, 1 - y))

    def y_sent():
        block = wbuf.at[:, :, :, pl.ds(pl.multiple_of(y * rows, rows), rows)]
        return remote(block, block, ysend, yrecv.at[0], at(z, 1 - y))

    def y_start(k):
        def run(grain, row):
            for e in range(2):
                for h in range(2):
                    y_copy(e, h, k, grain, row).start()
        plan.chunk(k, run)

    def z_copy(e, k, part, grain, row, target):
        fine = grain // FINE
        block = pl.ds(pl.multiple_of(row + part * fine, fine), fine)
        return remote(
            sums.at[e, :, block], arrived.at[e, :, block], zsend.at[e], zrecv.at[e, k, part], at(target, y)
        )

    def noise_copy(e, source):
        return remote(
            noise.at[core], nb.at[core, y, source], nsend.at[e], nrecv.at[source], at(3 * e, y),
        )

    sibling = (xx * 2 + 1 - core, me)

    def stage(n, far_side):
        if n == 0:
            block = nb.at[core, 1 - y if far_side else y]
            return remote(block, block, nstage.at[0], nstage_r.at[0], at(z, 1 - y))
        block = nb.at[1 - core if far_side else core]
        return remote(block, block, nstage.at[1], nstage_r.at[1], sibling)

    feat_copy.start()
    when(outer, lambda: pl.semaphore_wait(barrier, 17))
    when(inner, lambda: pl.semaphore_wait(barrier, 10))
    y_start(0)
    for e in range(2):
        for h in range(2):
            local_own(e, h).start()
    noise_own.start()
    for k in range(1, ahead):
        y_start(k)
    for e in range(2):
        when(z != 3 * e, lambda: noise_copy(e, z).start())
    factor_copy.start()
    fq[...] = jnp.zeros_like(fq)
    nmat[...] = jnp.zeros_like(nmat)
    top[...] = jnp.full_like(top, NEG)
    total[...] = jnp.zeros_like(total)
    acc[...] = jnp.zeros_like(acc)
    feat_copy.wait()
    fturn[...] = fcols[...].T
    for e in range(2):
        for h in range(2):
            local_own(e, h).wait()

    def lanes(s):
        return slice(s * batch, (s + 1) * batch)

    def first_pass(grain, row):
        @pl.when(lax.rem(row, 128) == 0)
        def _():
            span = pl.ds(pl.multiple_of(row, 128), 128)
            low[span] = lax.dot_general(
                fq[:, span], nmat[...], (((0,), (0,)), ((), ())), preferred_element_type=jnp.float32
            )
        rows_k = pl.ds(row, grain)
        logit, pre = sums[half, 0, rows_k], sums[half, 1, rows_k]
        offset = row + lax.broadcasted_iota(jnp.int32, (grain, batch), 0)
        valid = offset < valid_rows
        ids = cls * plan.columns + start + offset
        shifted = logit - jnp.where(ids >= CREAL, 30000.0, 0.0)
        fade = jnp.exp(-jnp.abs(pre))
        spread = jnp.maximum(pre, 0.0) + jnp.log1p(fade)
        gate[rows_k] = jnp.where(pre >= 0, 1.0, fade) / (1.0 + fade)
        shifted = jnp.where(valid, shifted * LOG2E, NEG)
        spread = jnp.where(valid, spread * LOG2E, 0.0)
        for s in range(draws):
            value = shifted + spread * low[rows_k, lanes(s)]
            zbuf[rows_k, lanes(s)] = value
            blocks = [value[i * 8 : i * 8 + 8] for i in range(grain // 8)]
            old = top[:, lanes(s)]
            new = jnp.maximum(old, tree(jnp.maximum, blocks))
            grown = tree(jnp.add, [jnp.exp2(b - new) for b in blocks])
            total[:, lanes(s)] = total[:, lanes(s)] * jnp.exp2(old - new) + grown
            top[:, lanes(s)] = new

    e_first, e_second = 1 - half, half

    def noise_stage(i):
        @pl.when(i == 2)
        def _():
            for k in range(4):
                when(z != k, lambda: noise_copy(half, k).wait_recv())
            noise_own.wait()
            stage(0, False).start()

        @pl.when(i == 4)
        def _():
            stage(0, True).wait_recv()
            stage(1, False).start()

        when(i == 10, label_copy.start)

        @pl.when(i == 3)
        def _():
            factor_copy.wait()
            for q in range(4):
                def pick(q=q):
                    fq[: plan.rank, : plan.width] = fac[:, plan.starts[q] : plan.starts[q] + plan.width]
                when(own_q == q, pick)

        @pl.when(i == 5)
        def _():
            stage(1, True).wait_recv()
            for j in range(2):
                for yi in range(2):
                    for zi in range(4):
                        nmat[: plan.rank, lanes((j * 2 + yi) * 4 + zi)] = nb[j, yi, zi]

    def own_sums(i, grain, row):
        when(i + ahead < chunks, lambda: y_start(i + ahead))
        y_landed(i, grain, row).wait_recv()
        block = pl.ds(row, grain)
        lhs = jnp.concatenate([wbuf[e, h, block] for e in range(2) for h in range(2)], axis=0)
        value = lax.dot_general(
            lhs, fturn[...], (((1,), (0,)), ((), ())), preferred_element_type=jnp.float32
        )
        sums[:, :, block] = value.reshape(2, 2, grain, batch)

    def add_arrived(e, k, part, grain, row):
        z_copy(e, k, part, grain, row, mid).wait_recv()
        fine = grain // FINE
        block = pl.ds(pl.multiple_of(row + part * fine, fine), fine)
        sums[e, :, block] = sums[e, :, block] + arrived[e, :, block]

    def forward_inner(i, carry):
        def first(grain, row):
            own_sums(i, grain, row)
            for part in range(FINE):
                add_arrived(e_first, i, part, grain, row)
                z_copy(e_first, i, part, grain, row, across).start()

        def second(grain, row):
            for part in range(FINE):
                add_arrived(e_second, i - lag_in, part, grain, row)
                z_copy(e_second, i - lag_in, part, grain, row, edge).start()

        when(i < chunks, lambda: plan.chunk(i, first))
        when(i >= lag_in, lambda: plan.chunk(i - lag_in, second))
        return carry

    def forward_outer(i, carry):
        def first(grain, row):
            own_sums(i, grain, row)
            for part in range(FINE):
                z_copy(e_first, i, part, grain, row, mid).start()

        def second(grain, row):
            for part in range(FINE):
                add_arrived(e_second, i - lag_out, part, grain, row)
            first_pass(grain, row)

        when(i < chunks, lambda: plan.chunk(i, first))
        noise_stage(i)
        when(i >= lag_out, lambda: plan.chunk(i - lag_out, second))
        return carry

    @pl.when(inner)
    def _():
        lax.fori_loop(0, chunks + lag_in, forward_inner, 0)

    @pl.when(outer)
    def _():
        lax.fori_loop(0, chunks + lag_out, forward_outer, 0)

    whole_copies = [pltpu.make_async_copy(heads[h], whole.at[h], wsem.at[h]) for h in range(2)]
    for copy in whole_copies:
        copy.start()
    when(outer, label_copy.wait)

    @pl.when(inner)
    def _():
        factor_copy.wait()
        noise_own.wait()

    spot = half * 8 + plane

    def end_device(p):
        return (lax.div(lax.rem(p, 8), 2), lax.div(p, 8) * 6 + lax.rem(p, 2))

    def red_copy(kind, slot, k, p):
        return remote(red.at[kind, slot], red.at[kind, slot], rsend.at[kind, k], rrecv.at[kind, slot], end_device(p))

    def log_merge(parts):
        best = tree(jnp.maximum, parts)
        return best + LOG2E * jnp.log(tree(jnp.add, [jnp.exp2(p - best) for p in parts]))

    def fan_out(target, value):
        for s in range(draws):
            target[:, lanes(s)] = jnp.broadcast_to(value[s : s + 1], (8, batch))

    def reduce_all(kind, merge):
        for k in range(8, 16):
            red_copy(kind, spot, k, lax.rem(spot + k, 16)).start()
        for k in range(1, 8):
            red_copy(kind, spot, k, lax.rem(spot + k, 16)).start()
        for k in range(1, 16):
            source = lax.rem(spot + 16 - k, 16)
            red_copy(kind, source, k, source).wait_recv()
        return merge([red[kind, p] for p in range(16)])

    @pl.when(outer)
    def _():
        for s in range(draws):
            m = top[:, lanes(s)]
            best = jnp.max(m, axis=0, keepdims=True)
            size = jnp.sum(total[:, lanes(s)] * jnp.exp2(m - best), axis=0, keepdims=True)
            red[0, spot, s : s + 1, :] = best + LOG2E * jnp.log(size)
        fan_out(lseb, reduce_all(0, log_merge))

        def second_pass(r, sums_in):
            block = pl.ds(pl.multiple_of(r * 8, 8), 8)
            logs = [zbuf[block, lanes(s)] - lseb[:, lanes(s)] for s in range(draws)]
            best = tree(jnp.maximum, logs)
            risen = [jnp.exp2(v - best) for v in logs]
            offset = r * 8 + lax.broadcasted_iota(jnp.int32, (8, batch), 0)
            share = jnp.where(offset < valid_rows, lab[block] / tree(jnp.add, risen), 0.0)
            peak[block] = jnp.exp2(best) * (1.0 / batch)
            weight[block] = share * (1.0 / batch)
            for s in range(draws):
                zbuf[block, lanes(s)] = risen[s]
            return tuple(a + share * v for a, v in zip(sums_in, risen))

        dots = lax.fori_loop(
            0, plan.width // 8, second_pass, tuple(jnp.zeros((8, batch), jnp.float32) for _ in range(draws)),
            unroll=4,
        )
        for s in range(draws):
            red[1, spot, s : s + 1, :] = jnp.sum(dots[s], axis=0, keepdims=True)
        fan_out(dotb, reduce_all(1, lambda parts: tree(jnp.add, parts)))

    def cot_chunk(grain, row):
        def body(b, carry):
            means, scales = [], []
            for part in range(2):
                block = pl.ds(pl.multiple_of(row + b * 16 + part * 8, 8), 8)
                eb, wt = peak[block], weight[block]
                terms = [zbuf[block, lanes(s)] * (eb * dotb[:, lanes(s)] - wt) for s in range(draws)]
                means.append(tree(jnp.add, terms))
                scales.append(
                    tree(jnp.add, [t * low[block, lanes(s)] for s, t in enumerate(terms)]) * gate[block]
                )
            inside = pl.ds(pl.multiple_of(row + b * 16, 16), 16)
            cot[own_q, inside, :batch] = jnp.concatenate(means, axis=0).astype(jnp.bfloat16)
            cot[own_q, inside, batch:] = jnp.concatenate(scales, axis=0).astype(jnp.bfloat16)
            return carry
        lax.fori_loop(0, grain // 16, body, 0)

    side = plan.side

    def gz(e, kind, k, grain, row, target):
        block = cot.at[e * 2 + (y if kind < 2 else 1 - y), pl.ds(row + (side if kind == 1 else 0), grain)]
        return remote(block, block, gzs.at[e, kind], gzr.at[e, kind, k], at(target, y))

    def gy(e, kind, k, grain, row, line):
        block = cot.at[e * 2 + line, pl.ds(row + side * kind, grain)]
        return remote(block, block, gys.at[e, kind], gyr.at[e, kind, k], at(z, 1 - y))

    def relay(e, i, target):
        def pass_on(kind, k, grain, row):
            gz(e, kind, k, grain, row, mid).wait_recv()
            if target is not None:
                gz(e, kind, k, grain, row, target).start()

        def early(grain, row):
            pass_on(1, i, grain, row)
            gy(e, 1, i, grain, row, y).start()

        def late(grain, row):
            pass_on(0, i - steps, grain, row)
            pass_on(2, i - steps, grain, row)

        when((i >= 0) & (i < steps), lambda: plan.step(i, early))
        when((i >= steps) & (i < 2 * steps), lambda: plan.step(i - steps, late))

    def absorb(j, grain, row):
        for e in range(2):
            gy(e, 1, j, grain, row, 1 - y).wait_recv()
        for kind in range(2):
            for h in range(2):
                lhs = jnp.concatenate(
                    [cot[q, pl.ds(row + kind * side, grain), h * batch : (h + 1) * batch] for q in range(4)], axis=0
                )
                rhs = jnp.concatenate(
                    [
                        whole[h, pl.ds(pl.multiple_of(plan.starts[q] + kind * side + row, UNIT), grain)]
                        for q in range(4)
                    ],
                    axis=0,
                )
                acc[...] += lax.dot_general(
                    lhs, rhs, (((0,), (0,)), ((), ())), preferred_element_type=jnp.float32
                )

    for copy in whole_copies:
        copy.wait()

    def gather(i, carry):
        @pl.when(outer)
        def _():
            def early(grain, row):
                cot_chunk(grain, row)
                gy(half, 0, i, grain, row, y).start()
                cot_chunk(grain, row + side)
                gz(half, 1, i, grain, row, mid).start()

            def late(grain, row):
                k = i - steps
                gz(half, 0, k, grain, row, mid).start()
                gy(half, 1, k, grain, row, y).start()
                gy(half, 0, k, grain, row, 1 - y).wait_recv()
                gz(half, 2, k, grain, row, mid).start()

            when(i < steps, lambda: plan.step(i, early))
            when((i >= steps) & (i < 2 * steps), lambda: plan.step(i - steps, late))
            relay(1 - half, i - relay_out, None)

        @pl.when(inner)
        def _():
            relay(half, i, across)
            relay(1 - half, i - relay_in, edge)
        last = i - relay_out - steps
        when(last >= 0, lambda: plan.step(last, functools.partial(absorb, last)))
        return carry

    lax.fori_loop(0, 2 * steps + relay_out, gather, 0)

    twin = remote(acc, acc_in, csend, crecv, sibling)
    twin.start()

    def relayed(e, kind):
        block = cot.at[e * 2, pl.ds(kind % 2 * side, side)]
        return remote(block, block, gzs.at[e, kind], gzr.at[e, kind, 0], at(mid, y))

    def crossed(e, kind):
        block = cot.at[e * 2, pl.ds(kind * side, side)]
        return remote(block, block, gys.at[e, kind], gyr.at[e, kind, 0], at(z, 1 - y))

    for kind in range(3):
        relayed(half, kind).wait_send()
        when(inner, lambda: relayed(1 - half, kind).wait_send())
    for e in range(2):
        crossed(e, 1).wait_send()
    when(outer, lambda: crossed(half, 0).wait_send())
    def z_sent(e):
        return remote(arrived.at[e], arrived.at[e], zsend.at[e], zrecv.at[e, 0, 0], at(mid, y))

    y_sent().wait_send()
    z_sent(e_first).wait_send()
    when(inner, lambda: z_sent(e_second).wait_send())
    twin.wait_recv()
    part[...] = acc[...] + acc_in[...]
    twin.wait_send()
    for e in range(2):
        when(z != 3 * e, lambda: noise_copy(e, z).wait_send())

    @pl.when(outer)
    def _():
        for n in range(2):
            stage(n, False).wait_send()
        for kind in range(2):
            for k in range(1, 16):
                red_copy(kind, spot, k, lax.rem(spot + k, 16)).wait_send()


def head_kernel(plan, cot, feat_in, mean_out, scale_out, cols_in, stage, loads, sems):
    batch, rows = plan.batch, plan.rows
    me = lax.axis_index("draw")
    feat_copy = pltpu.make_async_copy(
        feat_in.at[:, pl.ds(pl.multiple_of(me * rows, rows), rows)], cols_in, loads
    )

    feat_copy.start()
    feat_copy.wait()
    cols = cols_in[...]
    blank = jnp.zeros_like(cols)
    rhs = jnp.concatenate(
        [jnp.concatenate([cols, blank], axis=1), jnp.concatenate([blank, cols], axis=1)], axis=0
    )
    outs = (mean_out, scale_out)
    copies = []
    for q in range(4):
        size, first = plan.sizes[q], plan.starts[q]
        for part in range(2):
            begin = part * plan.side
            count = min(plan.side, size - begin)
            value = jnp.dot(cot[q, begin : begin + count], rhs, preferred_element_type=jnp.float32)
            spot = slice(first + begin, first + begin + count)
            for h in range(2):
                stage[h, spot] = value[:, h * rows : (h + 1) * rows]
                copy = pltpu.make_async_copy(stage.at[h, spot], outs[h].at[spot], sems.at[h, q * 2 + part])
                copy.start()
                copies.append(copy)
    for copy in copies:
        copy.wait()


def in_hbm(x):
    return pltpu.with_memory_space_constraint(x, pltpu.HBM)


def ends_on_device(features, mean_head, scale_head, factor, noise, labels):
    rows, columns = mean_head.shape
    batch = features.shape[0]
    own, rank = noise.shape[0], noise.shape[2]
    draws = own * 8
    plan = Plan(batch, rows, columns, rank)
    width, chunks, steps = plan.width, plan.chunks, plan.steps
    mean_rows, scale_rows = mean_head.T, scale_head.T
    noise_t = noise.transpose(0, 2, 1)
    dma = pltpu.SemaphoreType.DMA
    f32, bf16 = jnp.float32, jnp.bfloat16
    cot, part = pl.pallas_call(
        functools.partial(softmax_kernel, plan, draws, 3, 3, 9, 4, 10),
        out_shape=(
            jax.ShapeDtypeStruct((4, width, 2 * batch), bf16),
            jax.ShapeDtypeStruct((batch, rows), f32),
        ),
        in_specs=[HBM] * 4 + [ANY, HBM],
        out_specs=(VMEM, VMEM),
        scratch_shapes=[
            pltpu.VMEM((2, 2, width, 2 * rows), bf16),
            pltpu.VMEM((2, 2, width, batch), f32),
            pltpu.VMEM((2, 2, width, batch), f32),
            pltpu.VMEM((width, draws * batch), f32),
            pltpu.VMEM((plan.padded, draws * batch), f32),
            pltpu.VMEM((width, batch), f32),
            pltpu.VMEM((width, batch), f32),
            pltpu.VMEM((width, batch), f32),
            pltpu.VMEM((batch, 2 * rows), bf16),
            pltpu.VMEM((2 * rows, batch), bf16),
            pltpu.VMEM((rank, columns), bf16),
            pltpu.VMEM((64, plan.padded), bf16),
            pltpu.VMEM((2, 2, 4, rank, batch), bf16),
            pltpu.VMEM((64, draws * batch), bf16),
            pltpu.VMEM((width, batch), f32),
            pltpu.VMEM((8, draws * batch), f32),
            pltpu.VMEM((8, draws * batch), f32),
            pltpu.VMEM((8, draws * batch), f32),
            pltpu.VMEM((8, draws * batch), f32),
            pltpu.VMEM((2, 16, draws, batch), f32),
            pltpu.VMEM((2, columns, rows), bf16),
            pltpu.VMEM((batch, rows), f32),
            pltpu.VMEM((batch, rows), f32),
            dma((8,)),
            dma,
            dma((chunks,)),
            dma((2,)),
            dma((2, chunks, FINE)),
            dma((2,)),
            dma((4,)),
            dma((2,)),
            dma((2,)),
            dma((2, 16)),
            dma((2, 16)),
            dma((2, 3)),
            dma((2, 3, steps)),
            dma((2, 2)),
            dma((2, 2, steps)),
            dma((2,)),
            dma,
            dma,
        ],
        compiler_params=params(0, 50),
    )(in_hbm(features), in_hbm(mean_rows), in_hbm(scale_rows), in_hbm(factor.T), noise_t, in_hbm(labels.T))

    other = lax.ppermute(part, "cls", [(i, i ^ 2) for i in range(4)])
    mean_grad, scale_grad = pl.pallas_call(
        functools.partial(head_kernel, plan),
        out_shape=(jax.ShapeDtypeStruct((columns, rows), f32),) * 2,
        in_specs=[VMEM, HBM],
        out_specs=(HBM, HBM),
        scratch_shapes=[
            pltpu.VMEM((batch, rows), bf16),
            pltpu.VMEM((2, columns, rows), f32),
            dma,
            dma((2, 8)),
        ],
        compiler_params=pltpu.CompilerParams(vmem_limit_bytes=32 * 2**20),
        cost_estimate=pl.CostEstimate(
            flops=8 * columns * batch * rows, bytes_accessed=16 * columns * rows, transcendentals=0
        ),
    )(cot, features)
    return (mean_grad.T, scale_grad.T, part + other)


def solution(mesh):
    ends = dict(mesh.shape) == {"cls": 4, "draw": 8}
    return jax.shard_map(
        ends_on_device if ends else on_device,
        mesh=mesh,
        in_specs=(
            P(),
            P("draw", "cls"),
            P("draw", "cls"),
            P("cls", None),
            P("draw", None, None),
            P(None, "cls"),
        ),
        out_specs=(P("draw", "cls"), P("draw", "cls"), P(None, "draw")),
        check_vma=False,
    )
```

```python
import functools
import jax
import jax.numpy as jnp
from jax import lax
from jax.experimental import pallas as pl
from jax.experimental.pallas import tpu as pltpu
from jax.sharding import PartitionSpec as P

CREAL = 21843
UNIT = 16
MESH = pl.DeviceIdType.MESH
ANY = pl.BlockSpec(memory_space=pl.ANY)
VMEM = pl.BlockSpec(memory_space=pltpu.VMEM)
HBM = pl.BlockSpec(memory_space=pltpu.HBM)


def start_of(owner, n, units):
    return lax.div(owner * units, n)


def at_width(owner, n, units, run):
    base = units // n
    wide = start_of(owner + 1, n, units) - start_of(owner, n, units) > base
    pl.when(wide)(functools.partial(run, (base + 1) * UNIT))
    pl.when(jnp.logical_not(wide))(functools.partial(run, base * UNIT))


def exchange_kernel(
    n, units, feat, mean, scale, noise, logits, noise_out, held, part_out, part_in,
    send, recv, part_send, part_recv, nsend, nrecv, local, nlocal,
):
    me, cls = lax.axis_index("draw"), lax.axis_index("cls")
    half, rows = n // 2, mean.shape[1]
    mirror = lax.rem(me + half, n)
    base, spot = lax.div(me, half) * half, lax.rem(me, half)
    barrier = pltpu.get_barrier_semaphore()
    for k in range(1, n):
        pl.semaphore_signal(barrier, inc=1, device_id=(cls, lax.rem(me + k, n)), device_id_type=MESH)
    pl.semaphore_wait(barrier, n - 1)

    def remote(source, target, send_sem, recv_sem, device):
        return pltpu.make_async_remote_copy(
            source, target, send_sem, recv_sem, device_id=(cls, device), device_id_type=MESH
        )

    def noise_copy(slot, k, device):
        return remote(noise, noise_out.at[slot], nsend.at[k], nrecv.at[slot], device)

    def block(head, owner, width):
        start = pl.multiple_of(start_of(owner, n, units) * UNIT, UNIT)
        return (mean, scale)[head].at[pl.ds(start, width)]

    def block_copy(far, head, owner, k, source, device, act):
        at_width(
            owner, n, units,
            lambda w: act(
                remote(
                    block(head, owner, w), held.at[far, head, source, pl.ds(0, w)],
                    send.at[far, head, k], recv.at[far, head, source], device,
                )
            ),
        )

    def own_copy(far, head, act):
        owner = mirror if far else me
        at_width(
            owner, n, units,
            lambda w: act(
                pltpu.make_async_copy(
                    block(head, owner, w), held.at[far, head, spot, pl.ds(0, w)], local.at[far, head]
                )
            ),
        )

    def sends(far, head, act):
        for k in range(1, half):
            peer = base + lax.rem(spot + k, half)
            block_copy(far, head, lax.rem(peer + half, n) if far else peer, k, spot, peer, act)

    def columns_of(source):
        if rows % 128:
            return feat[source]
        return feat[:, pl.ds(pl.multiple_of(source * rows, rows), rows)]

    def arrive(far, head):
        owner = mirror if far else me
        for k in range(1, half):
            source = lax.rem(spot + half - k, half)
            block_copy(far, head, owner, k, source, base + source, lambda c: c.wait_recv())
        own_copy(far, head, lambda c: c.wait())
        total = None
        for source in range(half):
            term = lax.dot_general(
                held[far, head, source], columns_of(base + source), (((1,), (1,)), ((), ())),
                preferred_element_type=jnp.float32,
            )
            total = term if total is None else total + term
        return total

    def part_copy(head):
        return remote(part_out.at[head], part_in.at[head], part_send.at[head], part_recv.at[head], mirror)

    own_noise = pltpu.make_async_copy(noise, noise_out.at[me], nlocal)
    stages = [(1, 0), (1, 1), (0, 0), (0, 1)]
    sends(1, 0, lambda c: c.start())
    for k in range(1, n):
        noise_copy(me, k, lax.rem(me + k, n)).start()
    for far, head in stages[1:]:
        sends(far, head, lambda c: c.start())
    for far, head in stages:
        own_copy(far, head, lambda c: c.start())
    own_noise.start()
    for head in range(2):
        part_out[head] = arrive(1, head)
        part_copy(head).start()
    for head in range(2):
        logits[head] = arrive(0, head)
    for k in range(1, n):
        source = lax.rem(me + n - k, n)
        noise_copy(source, k, source).wait_recv()
    own_noise.wait()
    for head in range(2):
        part_copy(head).wait_recv()
        logits[head] = logits[head] + part_in[head]
    for far, head in stages:
        sends(far, head, lambda c: c.wait_send())
    for k in range(1, n):
        noise_copy(me, k, lax.rem(me + k, n)).wait_send()
    for head in range(2):
        part_copy(head).wait_send()


def gather_kernel(n, units, cot, out, send, recv, local):
    me, cls = lax.axis_index("draw"), lax.axis_index("cls")
    half = n // 2
    group, side = lax.div(me, 2), lax.rem(me, 2)
    partner = group * 2 + 1 - side
    split = units // n // 2 * UNIT
    pieces = [(head, part) for head in range(2) for part in range(2)]
    barrier = pltpu.get_barrier_semaphore()
    peers = [partner] + [lax.rem(group + k, half) * 2 + side for k in range(1, half)]
    for peer in peers:
        pl.semaphore_signal(barrier, inc=1, device_id=(cls, peer), device_id_type=MESH)
    pl.semaphore_wait(barrier, half)

    def source(piece, width):
        head, part = pieces[piece]
        return cot.at[head, pl.ds(split, width - split) if part else pl.ds(0, split)]

    def place(piece, owner, width):
        head, part = pieces[piece]
        start = start_of(owner, n, units) * UNIT + part * split
        return out.at[head, pl.ds(pl.multiple_of(start, UNIT), width - split if part else split)]

    def send_own(piece, owner, slot, device, act):
        at_width(
            owner, n, units,
            lambda w: act(
                pltpu.make_async_remote_copy(
                    source(piece, w), place(piece, owner, w), send.at[slot, piece], recv.at[owner, piece],
                    device_id=(cls, device), device_id_type=MESH,
                )
            ),
        )

    def forward(piece, owner, slot, act):
        at_width(
            owner, n, units,
            lambda w: act(
                pltpu.make_async_remote_copy(
                    place(piece, owner, w), place(piece, owner, w), send.at[slot, piece], recv.at[owner, piece],
                    device_id=(cls, partner), device_id_type=MESH,
                )
            ),
        )

    def own(piece, act):
        at_width(
            me, n, units,
            lambda w: act(pltpu.make_async_copy(source(piece, w), place(piece, me, w), local.at[piece])),
        )

    count = len(pieces)
    for piece in range(count):
        for k in range(1, half):
            send_own(piece, me, k, peers[k], lambda c: c.start())
        send_own(piece, me, 0, partner, lambda c: c.start())
    for piece in range(count):
        own(piece, lambda c: c.start())
    order = sorted(range(1, half), key=lambda k: min(k, half - k))
    for piece in range(count):
        for k in order:
            send_own(piece, peers[k], k, peers[k], lambda c: c.wait_recv())
            forward(piece, peers[k], half + k, lambda c: c.start())
    for piece in range(count):
        send_own(piece, partner, 0, partner, lambda c: c.wait_recv())
        for k in range(1, half):
            owner = lax.rem(group + k, half) * 2 + 1 - side
            forward(piece, owner, half + k, lambda c: c.wait_recv())
    for piece in range(count):
        for k in range(half):
            send_own(piece, me, k, peers[k], lambda c: c.wait_send())
        for k in range(1, half):
            forward(piece, peers[k], half + k, lambda c: c.wait_send())
        own(piece, lambda c: c.wait())


def merge(slots, count, softmax):
    if not softmax:
        total = slots[0]
        for i in range(1, count):
            total = total + slots[i]
        return total
    top = slots[0, 0]
    for i in range(1, count):
        top = jnp.maximum(top, slots[i, 0])
    total = jnp.zeros_like(top)
    for i in range(count):
        total = total + slots[i, 1] * jnp.exp(slots[i, 0] - top)
    return jnp.stack((top, total))


def reduce_kernel(counts, softmax, x, out, *scratch):
    levels = len(counts)
    slots, sends, recvs = scratch[:levels], scratch[levels : 2 * levels], scratch[2 * levels :]
    cls, draw = lax.axis_index("cls"), lax.axis_index("draw")

    def device(level, index):
        return (index, draw) if level == 0 else (cls, index)

    barrier = pltpu.get_barrier_semaphore()
    for level, n in enumerate(counts):
        me = (cls, draw)[level]
        for k in range(1, n):
            pl.semaphore_signal(
                barrier, inc=1, device_id=device(level, lax.rem(me + k, n)), device_id_type=MESH
            )
    pl.semaphore_wait(barrier, sum(counts) - levels)
    value = x[...]
    for level, n in enumerate(counts):
        me = (cls, draw)[level]
        held = slots[level]
        held[me] = value

        def copy(slot, k, target):
            return pltpu.make_async_remote_copy(
                held.at[slot], held.at[slot], sends[level].at[k], recvs[level].at[slot],
                device_id=device(level, target), device_id_type=MESH,
            )

        for k in range(1, n):
            copy(me, k, lax.rem(me + k, n)).start()
        for k in range(1, n):
            source = lax.rem(me + n - k, n)
            copy(source, k, source).wait_recv()
        for k in range(1, n):
            copy(me, k, lax.rem(me + k, n)).wait_send()
        value = merge(held, n, softmax)
    if softmax:
        out[...] = value[0] + jnp.log(value[1])
    else:
        out[...] = value


def params(collective_id, grant=32):
    return pltpu.CompilerParams(
        collective_id=collective_id, has_side_effects=True, vmem_limit_bytes=grant * 2**20
    )


def reduce_over(x, counts, softmax, collective_id):
    shape = x.shape[1:] if softmax else x.shape
    return pl.pallas_call(
        functools.partial(reduce_kernel, counts, softmax),
        out_shape=jax.ShapeDtypeStruct(shape, jnp.float32),
        in_specs=[VMEM],
        out_specs=VMEM,
        scratch_shapes=[pltpu.VMEM((n,) + x.shape, jnp.float32) for n in counts]
        + [pltpu.SemaphoreType.DMA((n,)) for n in counts]
        + [pltpu.SemaphoreType.DMA((n,)) for n in counts],
        compiler_params=params(collective_id),
    )(x)


def on_device(features, mean_head, scale_head, factor, noise, labels):
    rows, columns = mean_head.shape
    batch = features.shape[0]
    n, ncls = lax.axis_size("draw"), lax.axis_size("cls")
    me = lax.axis_index("draw")
    units = columns // UNIT
    tile = -(-units // n) * UNIT
    own, rank = noise.shape[0], noise.shape[2]
    draws = own * n
    mean_rows, scale_rows = mean_head.T, scale_head.T
    half = n // 2
    feat = features.reshape(batch, n, rows).transpose(1, 0, 2) if rows % 128 else features

    heads, noise_t = pl.pallas_call(
        functools.partial(exchange_kernel, n, units),
        out_shape=(
            jax.ShapeDtypeStruct((2, tile, batch), jnp.float32),
            jax.ShapeDtypeStruct((n, own, rank, batch), jnp.bfloat16),
        ),
        in_specs=[VMEM] + [ANY] * 3,
        out_specs=(VMEM, ANY),
        scratch_shapes=[
            pltpu.VMEM((2, 2, half, tile, rows), jnp.bfloat16),
            pltpu.VMEM((2, tile, batch), jnp.float32),
            pltpu.VMEM((2, tile, batch), jnp.float32),
            pltpu.SemaphoreType.DMA((2, 2, half)),
            pltpu.SemaphoreType.DMA((2, 2, half)),
            pltpu.SemaphoreType.DMA((2,)),
            pltpu.SemaphoreType.DMA((2,)),
            pltpu.SemaphoreType.DMA((n,)),
            pltpu.SemaphoreType.DMA((n,)),
            pltpu.SemaphoreType.DMA((2, 2)),
            pltpu.SemaphoreType.DMA,
        ],
        compiler_params=params(0),
    )(feat, mean_rows, scale_rows, noise.transpose(0, 2, 1))

    first = start_of(me, n, units) * UNIT
    width = start_of(me + 1, n, units) * UNIT - first
    offsets = jnp.arange(tile, dtype=jnp.int32)[:, None]
    valid = offsets < width
    class_ids = lax.axis_index("cls") * columns + first + offsets
    shift = jnp.where(class_ids >= CREAL, 30000.0, 0.0).astype(jnp.float32)
    my_factor = lax.dynamic_slice_in_dim(factor.T, first, tile, 1)
    my_labels = jnp.where(valid, lax.dynamic_slice_in_dim(labels.T, first, tile, 0), 0.0)

    mean_logit, scale_pre = heads[0], heads[1]
    scale_pre = jnp.where(valid, scale_pre, 0.0)
    spread = jax.nn.softplus(scale_pre)
    lowrank = jnp.einsum(
        "rc,srb->scb", my_factor, noise_t.reshape(draws, rank, batch), preferred_element_type=jnp.float32
    )
    logits = mean_logit[None] + spread[None] * lowrank - shift[None]
    logits = jnp.where(valid[None], logits, -1e30)
    local_top = jnp.max(logits, axis=1)
    local_total = jnp.sum(jnp.exp(logits - local_top[:, None]), axis=1)
    lse = reduce_over(jnp.stack((local_top, local_total)), (ncls, n), True, 1)
    log_prob = logits - lse[:, None]
    best = jnp.max(log_prob, axis=0)
    risen = jnp.exp(log_prob - best[None])
    inverse = 1.0 / jnp.sum(risen, axis=0)
    weight = my_labels * inverse
    label_dot = reduce_over(jnp.sum(weight[None] * risen, axis=1), (ncls, n), False, 2)
    logit_cot = risen * ((jnp.exp(best) / batch)[None] * label_dot[:, None] - (weight / batch)[None])
    dmean = jnp.sum(logit_cot, axis=0)
    dspread = jnp.sum(logit_cot * lowrank, axis=0)
    cots = jnp.stack((dmean, dspread * jax.nn.sigmoid(scale_pre))).astype(jnp.bfloat16)

    gathered = pl.pallas_call(
        functools.partial(gather_kernel, n, units),
        out_shape=jax.ShapeDtypeStruct((2, columns, batch), jnp.bfloat16),
        in_specs=[ANY],
        out_specs=ANY,
        scratch_shapes=[
            pltpu.SemaphoreType.DMA((n, 4)),
            pltpu.SemaphoreType.DMA((n, 4)),
            pltpu.SemaphoreType.DMA((4,)),
        ],
        compiler_params=params(3),
    )(cots)
    mean_cot, scale_cot = gathered[0], gathered[1]
    my_columns = lax.dynamic_slice_in_dim(features, me * rows, rows, 1)
    over_classes = (((0,), (0,)), ((), ()))
    feature_part = lax.dot_general(
        mean_cot, mean_rows, over_classes, preferred_element_type=jnp.float32
    ) + lax.dot_general(scale_cot, scale_rows, over_classes, preferred_element_type=jnp.float32)
    mean_grad = jnp.dot(mean_cot, my_columns, preferred_element_type=jnp.float32).T
    scale_grad = jnp.dot(scale_cot, my_columns, preferred_element_type=jnp.float32).T
    feature_grad, step = feature_part, 1
    while step < ncls:
        feature_grad = feature_grad + lax.ppermute(feature_grad, "cls", [(i, i ^ step) for i in range(ncls)])
        step *= 2
    return (mean_grad, scale_grad, feature_grad)


GRAIN = 64
SMALL = 32
FINE = 1
NEG = -1e30
LOG2E = 1.4426950408889634


def when(cond, fn):
    pl.when(cond)(fn)


class Plan:
    def __init__(self, batch, rows, columns, rank):
        self.batch, self.rows, self.columns, self.rank = batch, rows, columns, rank
        units = columns // UNIT
        edges = [q * units // 4 * UNIT for q in range(5)]
        widest = max(b - a for a, b in zip(edges, edges[1:]))
        self.width = -(-widest // SMALL) * SMALL
        self.padded = -(-self.width // 128) * 128
        self.full = self.width // GRAIN - 1
        self.chunks = self.full + (self.width - self.full * GRAIN) // SMALL
        self.side = self.width // 2
        self.side_full = self.side // GRAIN
        self.rest = self.side - self.side_full * GRAIN
        self.steps = self.side_full + (self.rest > 0)
        self.units = units
        self.extra = max(0, edges[3] + self.width - columns)
        self.starts = edges[:3] + [edges[3] - self.extra]
        self.sizes = [b - a for a, b in zip(self.starts, self.starts[1:] + [columns])]

    def start(self, q):
        return pl.multiple_of(lax.div(q * self.units, 4) * UNIT - self.extra * lax.div(q, 3), UNIT)

    def chunk(self, k, run):
        def tail():
            run(SMALL, pl.multiple_of(self.full * GRAIN + (k - self.full) * SMALL, SMALL))
        when(k < self.full, lambda: run(GRAIN, pl.multiple_of(k * GRAIN, GRAIN)))
        when(k >= self.full, tail)

    def step(self, k, run):
        when(k < self.side_full, lambda: run(GRAIN, pl.multiple_of(k * GRAIN, GRAIN)))
        if self.rest:
            when(k >= self.side_full, lambda: run(self.rest, self.side_full * GRAIN))

    def size(self, q):
        after = lax.div((q + 1) * self.units, 4) * UNIT - self.extra * (lax.div(q + 1, 3) - lax.div(q + 1, 4))
        return after - self.start(q)


def tree(fn, items):
    items = list(items)
    while len(items) > 1:
        items = [fn(*items[i : i + 2]) if i + 1 < len(items) else items[i] for i in range(0, len(items), 2)]
    return items[0]


def softmax_kernel(
    plan, draws, ahead, lag_in, lag_out, relay_in, relay_out,
    feat, mean, scale, factor, noise, labels, cot, part,
    wbuf, sums, arrived, zbuf, low, gate, weight, peak, fcols, fturn, fac, fq, nb, nmat, lab, top, total, lseb, dotb,
    red, whole, acc, acc_in,
    lsem, ysend, yrecv, zsend, zrecv, nsend, nrecv, nstage, nstage_r, rsend, rrecv,
    gzs, gzr, gys, gyr, wsem, csend, crecv,
):
    me, cls = lax.axis_index("draw"), lax.axis_index("cls")
    z, y = lax.div(me, 2), lax.rem(me, 2)
    xx, core = lax.div(cls, 2), lax.rem(cls, 2)
    half = lax.div(z, 2)
    outer = (z == 0) | (z == 3)
    inner = jnp.logical_not(outer)
    edge, mid = 3 * half, 1 + half
    across = 2 - half
    batch, rows, chunks, steps = plan.batch, plan.rows, plan.chunks, plan.steps
    own_q = half * 2 + y
    start = plan.start(own_q)
    valid_rows = plan.size(own_q)
    plane = cls * 2 + y
    heads = (mean, scale)

    def at(zi, yi):
        return (cls, zi * 2 + yi)

    def in_plane(p):
        return (lax.div(p, 2), z * 2 + lax.rem(p, 2))

    barrier = pltpu.get_barrier_semaphore()
    for k in range(1, 8):
        pl.semaphore_signal(barrier, inc=1, device_id=in_plane(lax.rem(plane + k, 8)), device_id_type=MESH)
    for k in range(1, 4):
        pl.semaphore_signal(barrier, inc=1, device_id=at(lax.rem(z + k, 4), y), device_id_type=MESH)

    @pl.when(outer)
    def _():
        for k in range(1, 8):
            p = lax.rem(plane + k, 8)
            pl.semaphore_signal(
                barrier, inc=1, device_id=(lax.div(p, 2), (3 - z) * 2 + lax.rem(p, 2)), device_id_type=MESH
            )

    def remote(src, dst, s, r, device):
        return pltpu.make_async_remote_copy(src, dst, s, r, device_id=device, device_id_type=MESH)

    def local_own(e, h):
        return pltpu.make_async_copy(
            heads[h].at[pl.ds(plan.start(e * 2 + y), plan.width)],
            wbuf.at[e, h, :, pl.ds(pl.multiple_of(y * rows, rows), rows)],
            lsem.at[e * 2 + h],
        )

    feat_copy = pltpu.make_async_copy(
        feat.at[:, pl.ds(pl.multiple_of(z * 2 * rows, 2 * rows), 2 * rows)], fcols, lsem.at[4]
    )
    factor_copy = pltpu.make_async_copy(factor, fac, lsem.at[5])
    label_copy = pltpu.make_async_copy(labels.at[pl.ds(start, plan.width)], lab, lsem.at[6])
    noise_own = pltpu.make_async_copy(
        noise.at[core], nb.at[core, y, z], lsem.at[7]
    )

    def y_copy(e, h, k, grain, row):
        return remote(
            heads[h].at[pl.ds(plan.start(e * 2 + 1 - y) + row, grain)],
            wbuf.at[e, h, pl.ds(row, grain), pl.ds(pl.multiple_of(y * rows, rows), rows)],
            ysend, yrecv.at[k], at(z, 1 - y),
        )

    def y_landed(k, grain, row):
        block = wbuf.at[:, :, pl.ds(row, grain), pl.ds(pl.multiple_of((1 - y) * rows, rows), rows)]
        return remote(block, block, ysend, yrecv.at[k], at(z, 1 - y))

    def y_sent():
        block = wbuf.at[:, :, :, pl.ds(pl.multiple_of(y * rows, rows), rows)]
        return remote(block, block, ysend, yrecv.at[0], at(z, 1 - y))

    def y_start(k):
        def run(grain, row):
            for e in range(2):
                for h in range(2):
                    y_copy(e, h, k, grain, row).start()
        plan.chunk(k, run)

    def z_copy(e, k, part, grain, row, target):
        fine = grain // FINE
        block = pl.ds(pl.multiple_of(row + part * fine, fine), fine)
        return remote(
            sums.at[e, :, block], arrived.at[e, :, block], zsend.at[e], zrecv.at[e, k, part], at(target, y)
        )

    def noise_copy(e, source):
        return remote(
            noise.at[core], nb.at[core, y, source], nsend.at[e], nrecv.at[source], at(3 * e, y),
        )

    sibling = (xx * 2 + 1 - core, me)

    def stage(n, far_side):
        if n == 0:
            block = nb.at[core, 1 - y if far_side else y]
            return remote(block, block, nstage.at[0], nstage_r.at[0], at(z, 1 - y))
        block = nb.at[1 - core if far_side else core]
        return remote(block, block, nstage.at[1], nstage_r.at[1], sibling)

    feat_copy.start()
    when(outer, lambda: pl.semaphore_wait(barrier, 17))
    when(inner, lambda: pl.semaphore_wait(barrier, 10))
    y_start(0)
    for e in range(2):
        for h in range(2):
            local_own(e, h).start()
    noise_own.start()
    for k in range(1, ahead):
        y_start(k)
    for e in range(2):
        when(z != 3 * e, lambda: noise_copy(e, z).start())
    factor_copy.start()
    fq[...] = jnp.zeros_like(fq)
    nmat[...] = jnp.zeros_like(nmat)
    top[...] = jnp.full_like(top, NEG)
    total[...] = jnp.zeros_like(total)
    acc[...] = jnp.zeros_like(acc)
    feat_copy.wait()
    fturn[...] = fcols[...].T
    for e in range(2):
        for h in range(2):
            local_own(e, h).wait()

    def lanes(s):
        return slice(s * batch, (s + 1) * batch)

    def first_pass(grain, row):
        @pl.when(lax.rem(row, 128) == 0)
        def _():
            span = pl.ds(pl.multiple_of(row, 128), 128)
            low[span] = lax.dot_general(
                fq[:, span], nmat[...], (((0,), (0,)), ((), ())), preferred_element_type=jnp.float32
            )
        rows_k = pl.ds(row, grain)
        logit, pre = sums[half, 0, rows_k], sums[half, 1, rows_k]
        offset = row + lax.broadcasted_iota(jnp.int32, (grain, batch), 0)
        valid = offset < valid_rows
        ids = cls * plan.columns + start + offset
        shifted = logit - jnp.where(ids >= CREAL, 30000.0, 0.0)
        fade = jnp.exp(-jnp.abs(pre))
        spread = jnp.maximum(pre, 0.0) + jnp.log1p(fade)
        gate[rows_k] = jnp.where(pre >= 0, 1.0, fade) / (1.0 + fade)
        shifted = jnp.where(valid, shifted * LOG2E, NEG)
        spread = jnp.where(valid, spread * LOG2E, 0.0)
        for s in range(draws):
            value = shifted + spread * low[rows_k, lanes(s)]
            zbuf[rows_k, lanes(s)] = value
            blocks = [value[i * 8 : i * 8 + 8] for i in range(grain // 8)]
            old = top[:, lanes(s)]
            new = jnp.maximum(old, tree(jnp.maximum, blocks))
            grown = tree(jnp.add, [jnp.exp2(b - new) for b in blocks])
            total[:, lanes(s)] = total[:, lanes(s)] * jnp.exp2(old - new) + grown
            top[:, lanes(s)] = new

    e_first, e_second = 1 - half, half

    def noise_stage(i):
        @pl.when(i == 2)
        def _():
            for k in range(4):
                when(z != k, lambda: noise_copy(half, k).wait_recv())
            noise_own.wait()
            stage(0, False).start()

        @pl.when(i == 4)
        def _():
            stage(0, True).wait_recv()
            stage(1, False).start()

        when(i == 10, label_copy.start)

        @pl.when(i == 3)
        def _():
            factor_copy.wait()
            for q in range(4):
                def pick(q=q):
                    fq[: plan.rank, : plan.width] = fac[:, plan.starts[q] : plan.starts[q] + plan.width]
                when(own_q == q, pick)

        @pl.when(i == 5)
        def _():
            stage(1, True).wait_recv()
            for j in range(2):
                for yi in range(2):
                    for zi in range(4):
                        nmat[: plan.rank, lanes((j * 2 + yi) * 4 + zi)] = nb[j, yi, zi]

    def own_sums(i, grain, row):
        when(i + ahead < chunks, lambda: y_start(i + ahead))
        y_landed(i, grain, row).wait_recv()
        block = pl.ds(row, grain)
        lhs = jnp.concatenate([wbuf[e, h, block] for e in range(2) for h in range(2)], axis=0)
        value = lax.dot_general(
            lhs, fturn[...], (((1,), (0,)), ((), ())), preferred_element_type=jnp.float32
        )
        sums[:, :, block] = value.reshape(2, 2, grain, batch)

    def add_arrived(e, k, part, grain, row):
        z_copy(e, k, part, grain, row, mid).wait_recv()
        fine = grain // FINE
        block = pl.ds(pl.multiple_of(row + part * fine, fine), fine)
        sums[e, :, block] = sums[e, :, block] + arrived[e, :, block]

    def forward_inner(i, carry):
        def first(grain, row):
            own_sums(i, grain, row)
            for part in range(FINE):
                add_arrived(e_first, i, part, grain, row)
                z_copy(e_first, i, part, grain, row, across).start()

        def second(grain, row):
            for part in range(FINE):
                add_arrived(e_second, i - lag_in, part, grain, row)
                z_copy(e_second, i - lag_in, part, grain, row, edge).start()

        when(i < chunks, lambda: plan.chunk(i, first))
        when(i >= lag_in, lambda: plan.chunk(i - lag_in, second))
        return carry

    def forward_outer(i, carry):
        def first(grain, row):
            own_sums(i, grain, row)
            for part in range(FINE):
                z_copy(e_first, i, part, grain, row, mid).start()

        def second(grain, row):
            for part in range(FINE):
                add_arrived(e_second, i - lag_out, part, grain, row)
            first_pass(grain, row)

        when(i < chunks, lambda: plan.chunk(i, first))
        noise_stage(i)
        when(i >= lag_out, lambda: plan.chunk(i - lag_out, second))
        return carry

    @pl.when(inner)
    def _():
        lax.fori_loop(0, chunks + lag_in, forward_inner, 0)

    @pl.when(outer)
    def _():
        lax.fori_loop(0, chunks + lag_out, forward_outer, 0)

    whole_copies = [pltpu.make_async_copy(heads[h], whole.at[h], wsem.at[h]) for h in range(2)]
    for copy in whole_copies:
        copy.start()
    when(outer, label_copy.wait)

    @pl.when(inner)
    def _():
        factor_copy.wait()
        noise_own.wait()

    spot = half * 8 + plane

    def end_device(p):
        return (lax.div(lax.rem(p, 8), 2), lax.div(p, 8) * 6 + lax.rem(p, 2))

    def red_copy(kind, slot, k, p):
        return remote(red.at[kind, slot], red.at[kind, slot], rsend.at[kind, k], rrecv.at[kind, slot], end_device(p))

    def log_merge(parts):
        best = tree(jnp.maximum, parts)
        return best + LOG2E * jnp.log(tree(jnp.add, [jnp.exp2(p - best) for p in parts]))

    def fan_out(target, value):
        for s in range(draws):
            target[:, lanes(s)] = jnp.broadcast_to(value[s : s + 1], (8, batch))

    def reduce_all(kind, merge):
        for k in range(8, 16):
            red_copy(kind, spot, k, lax.rem(spot + k, 16)).start()
        for k in range(1, 8):
            red_copy(kind, spot, k, lax.rem(spot + k, 16)).start()
        for k in range(1, 16):
            source = lax.rem(spot + 16 - k, 16)
            red_copy(kind, source, k, source).wait_recv()
        return merge([red[kind, p] for p in range(16)])

    @pl.when(outer)
    def _():
        for s in range(draws):
            m = top[:, lanes(s)]
            best = jnp.max(m, axis=0, keepdims=True)
            size = jnp.sum(total[:, lanes(s)] * jnp.exp2(m - best), axis=0, keepdims=True)
            red[0, spot, s : s + 1, :] = best + LOG2E * jnp.log(size)
        fan_out(lseb, reduce_all(0, log_merge))

        def second_pass(r, sums_in):
            block = pl.ds(pl.multiple_of(r * 8, 8), 8)
            logs = [zbuf[block, lanes(s)] - lseb[:, lanes(s)] for s in range(draws)]
            best = tree(jnp.maximum, logs)
            risen = [jnp.exp2(v - best) for v in logs]
            offset = r * 8 + lax.broadcasted_iota(jnp.int32, (8, batch), 0)
            share = jnp.where(offset < valid_rows, lab[block] / tree(jnp.add, risen), 0.0)
            peak[block] = jnp.exp2(best) * (1.0 / batch)
            weight[block] = share * (1.0 / batch)
            for s in range(draws):
                zbuf[block, lanes(s)] = risen[s]
            return tuple(a + share * v for a, v in zip(sums_in, risen))

        dots = lax.fori_loop(
            0, plan.width // 8, second_pass, tuple(jnp.zeros((8, batch), jnp.float32) for _ in range(draws)),
            unroll=4,
        )
        for s in range(draws):
            red[1, spot, s : s + 1, :] = jnp.sum(dots[s], axis=0, keepdims=True)
        fan_out(dotb, reduce_all(1, lambda parts: tree(jnp.add, parts)))

    def cot_chunk(grain, row):
        def body(b, carry):
            means, scales = [], []
            for part in range(2):
                block = pl.ds(pl.multiple_of(row + b * 16 + part * 8, 8), 8)
                eb, wt = peak[block], weight[block]
                terms = [zbuf[block, lanes(s)] * (eb * dotb[:, lanes(s)] - wt) for s in range(draws)]
                means.append(tree(jnp.add, terms))
                scales.append(
                    tree(jnp.add, [t * low[block, lanes(s)] for s, t in enumerate(terms)]) * gate[block]
                )
            inside = pl.ds(pl.multiple_of(row + b * 16, 16), 16)
            cot[own_q, inside, :batch] = jnp.concatenate(means, axis=0).astype(jnp.bfloat16)
            cot[own_q, inside, batch:] = jnp.concatenate(scales, axis=0).astype(jnp.bfloat16)
            return carry
        lax.fori_loop(0, grain // 16, body, 0)

    side = plan.side

    def gz(e, kind, k, grain, row, target):
        block = cot.at[e * 2 + (y if kind < 2 else 1 - y), pl.ds(row + (side if kind == 1 else 0), grain)]
        return remote(block, block, gzs.at[e, kind], gzr.at[e, kind, k], at(target, y))

    def gy(e, kind, k, grain, row, line):
        block = cot.at[e * 2 + line, pl.ds(row + side * kind, grain)]
        return remote(block, block, gys.at[e, kind], gyr.at[e, kind, k], at(z, 1 - y))

    def relay(e, i, target):
        def pass_on(kind, k, grain, row):
            gz(e, kind, k, grain, row, mid).wait_recv()
            if target is not None:
                gz(e, kind, k, grain, row, target).start()

        def early(grain, row):
            pass_on(1, i, grain, row)
            gy(e, 1, i, grain, row, y).start()

        def late(grain, row):
            pass_on(0, i - steps, grain, row)
            pass_on(2, i - steps, grain, row)

        when((i >= 0) & (i < steps), lambda: plan.step(i, early))
        when((i >= steps) & (i < 2 * steps), lambda: plan.step(i - steps, late))

    def absorb(j, grain, row):
        for e in range(2):
            gy(e, 1, j, grain, row, 1 - y).wait_recv()
        for kind in range(2):
            for h in range(2):
                lhs = jnp.concatenate(
                    [cot[q, pl.ds(row + kind * side, grain), h * batch : (h + 1) * batch] for q in range(4)], axis=0
                )
                rhs = jnp.concatenate(
                    [
                        whole[h, pl.ds(pl.multiple_of(plan.starts[q] + kind * side + row, UNIT), grain)]
                        for q in range(4)
                    ],
                    axis=0,
                )
                acc[...] += lax.dot_general(
                    lhs, rhs, (((0,), (0,)), ((), ())), preferred_element_type=jnp.float32
                )

    for copy in whole_copies:
        copy.wait()

    def gather(i, carry):
        @pl.when(outer)
        def _():
            def early(grain, row):
                cot_chunk(grain, row)
                gy(half, 0, i, grain, row, y).start()
                cot_chunk(grain, row + side)
                gz(half, 1, i, grain, row, mid).start()

            def late(grain, row):
                k = i - steps
                gz(half, 0, k, grain, row, mid).start()
                gy(half, 1, k, grain, row, y).start()
                gy(half, 0, k, grain, row, 1 - y).wait_recv()
                gz(half, 2, k, grain, row, mid).start()

            when(i < steps, lambda: plan.step(i, early))
            when((i >= steps) & (i < 2 * steps), lambda: plan.step(i - steps, late))
            relay(1 - half, i - relay_out, None)

        @pl.when(inner)
        def _():
            relay(half, i, across)
            relay(1 - half, i - relay_in, edge)
        last = i - relay_out - steps
        when(last >= 0, lambda: plan.step(last, functools.partial(absorb, last)))
        return carry

    lax.fori_loop(0, 2 * steps + relay_out, gather, 0)

    twin = remote(acc, acc_in, csend, crecv, sibling)
    twin.start()

    def relayed(e, kind):
        block = cot.at[e * 2, pl.ds(kind % 2 * side, side)]
        return remote(block, block, gzs.at[e, kind], gzr.at[e, kind, 0], at(mid, y))

    def crossed(e, kind):
        block = cot.at[e * 2, pl.ds(kind * side, side)]
        return remote(block, block, gys.at[e, kind], gyr.at[e, kind, 0], at(z, 1 - y))

    for kind in range(3):
        relayed(half, kind).wait_send()
        when(inner, lambda: relayed(1 - half, kind).wait_send())
    for e in range(2):
        crossed(e, 1).wait_send()
    when(outer, lambda: crossed(half, 0).wait_send())
    def z_sent(e):
        return remote(arrived.at[e], arrived.at[e], zsend.at[e], zrecv.at[e, 0, 0], at(mid, y))

    y_sent().wait_send()
    z_sent(e_first).wait_send()
    when(inner, lambda: z_sent(e_second).wait_send())
    twin.wait_recv()
    part[...] = acc[...] + acc_in[...]
    twin.wait_send()
    for e in range(2):
        when(z != 3 * e, lambda: noise_copy(e, z).wait_send())

    @pl.when(outer)
    def _():
        for n in range(2):
            stage(n, False).wait_send()
        for kind in range(2):
            for k in range(1, 16):
                red_copy(kind, spot, k, lax.rem(spot + k, 16)).wait_send()


def head_kernel(plan, cot, feat_in, mean_out, scale_out, cols_in, stage, loads, sems):
    batch, rows = plan.batch, plan.rows
    me = lax.axis_index("draw")
    feat_copy = pltpu.make_async_copy(
        feat_in.at[:, pl.ds(pl.multiple_of(me * rows, rows), rows)], cols_in, loads
    )

    feat_copy.start()
    feat_copy.wait()
    cols = cols_in[...]
    blank = jnp.zeros_like(cols)
    rhs = jnp.concatenate(
        [jnp.concatenate([cols, blank], axis=1), jnp.concatenate([blank, cols], axis=1)], axis=0
    )
    outs = (mean_out, scale_out)
    copies = []
    for q in range(4):
        size, first = plan.sizes[q], plan.starts[q]
        for part in range(2):
            begin = part * plan.side
            count = min(plan.side, size - begin)
            value = jnp.dot(cot[q, begin : begin + count], rhs, preferred_element_type=jnp.float32)
            spot = slice(first + begin, first + begin + count)
            for h in range(2):
                stage[h, spot] = value[:, h * rows : (h + 1) * rows]
                copy = pltpu.make_async_copy(stage.at[h, spot], outs[h].at[spot], sems.at[h, q * 2 + part])
                copy.start()
                copies.append(copy)
    for copy in copies:
        copy.wait()


def in_hbm(x):
    return pltpu.with_memory_space_constraint(x, pltpu.HBM)


def ends_on_device(features, mean_head, scale_head, factor, noise, labels):
    rows, columns = mean_head.shape
    batch = features.shape[0]
    own, rank = noise.shape[0], noise.shape[2]
    draws = own * 8
    plan = Plan(batch, rows, columns, rank)
    width, chunks, steps = plan.width, plan.chunks, plan.steps
    mean_rows, scale_rows = mean_head.T, scale_head.T
    noise_t = noise.transpose(0, 2, 1)
    dma = pltpu.SemaphoreType.DMA
    f32, bf16 = jnp.float32, jnp.bfloat16
    cot, part = pl.pallas_call(
        functools.partial(softmax_kernel, plan, draws, 3, 3, 9, 3, 10),
        out_shape=(
            jax.ShapeDtypeStruct((4, width, 2 * batch), bf16),
            jax.ShapeDtypeStruct((batch, rows), f32),
        ),
        in_specs=[HBM] * 4 + [ANY, HBM],
        out_specs=(VMEM, VMEM),
        scratch_shapes=[
            pltpu.VMEM((2, 2, width, 2 * rows), bf16),
            pltpu.VMEM((2, 2, width, batch), f32),
            pltpu.VMEM((2, 2, width, batch), f32),
            pltpu.VMEM((width, draws * batch), f32),
            pltpu.VMEM((plan.padded, draws * batch), f32),
            pltpu.VMEM((width, batch), f32),
            pltpu.VMEM((width, batch), f32),
            pltpu.VMEM((width, batch), f32),
            pltpu.VMEM((batch, 2 * rows), bf16),
            pltpu.VMEM((2 * rows, batch), bf16),
            pltpu.VMEM((rank, columns), bf16),
            pltpu.VMEM((64, plan.padded), bf16),
            pltpu.VMEM((2, 2, 4, rank, batch), bf16),
            pltpu.VMEM((64, draws * batch), bf16),
            pltpu.VMEM((width, batch), f32),
            pltpu.VMEM((8, draws * batch), f32),
            pltpu.VMEM((8, draws * batch), f32),
            pltpu.VMEM((8, draws * batch), f32),
            pltpu.VMEM((8, draws * batch), f32),
            pltpu.VMEM((2, 16, draws, batch), f32),
            pltpu.VMEM((2, columns, rows), bf16),
            pltpu.VMEM((batch, rows), f32),
            pltpu.VMEM((batch, rows), f32),
            dma((8,)),
            dma,
            dma((chunks,)),
            dma((2,)),
            dma((2, chunks, FINE)),
            dma((2,)),
            dma((4,)),
            dma((2,)),
            dma((2,)),
            dma((2, 16)),
            dma((2, 16)),
            dma((2, 3)),
            dma((2, 3, steps)),
            dma((2, 2)),
            dma((2, 2, steps)),
            dma((2,)),
            dma,
            dma,
        ],
        compiler_params=params(0, 50),
    )(in_hbm(features), in_hbm(mean_rows), in_hbm(scale_rows), in_hbm(factor.T), noise_t, in_hbm(labels.T))

    other = lax.ppermute(part, "cls", [(i, i ^ 2) for i in range(4)])
    mean_grad, scale_grad = pl.pallas_call(
        functools.partial(head_kernel, plan),
        out_shape=(jax.ShapeDtypeStruct((columns, rows), f32),) * 2,
        in_specs=[VMEM, HBM],
        out_specs=(HBM, HBM),
        scratch_shapes=[
            pltpu.VMEM((batch, rows), bf16),
            pltpu.VMEM((2, columns, rows), f32),
            dma,
            dma((2, 8)),
        ],
        compiler_params=pltpu.CompilerParams(vmem_limit_bytes=32 * 2**20),
        cost_estimate=pl.CostEstimate(
            flops=8 * columns * batch * rows, bytes_accessed=16 * columns * rows, transcendentals=0
        ),
    )(cot, features)
    return (mean_grad.T, scale_grad.T, part + other)


def solution(mesh):
    ends = dict(mesh.shape) == {"cls": 4, "draw": 8}
    return jax.shard_map(
        ends_on_device if ends else on_device,
        mesh=mesh,
        in_specs=(
            P(),
            P("draw", "cls"),
            P("draw", "cls"),
            P("cls", None),
            P("draw", None, None),
            P(None, "cls"),
        ),
        out_specs=(P("draw", "cls"), P("draw", "cls"), P(None, "draw")),
        check_vma=False,
    )
```

```python
import functools
import jax
import jax.numpy as jnp
from jax import lax
from jax.experimental import pallas as pl
from jax.experimental.pallas import tpu as pltpu
from jax.sharding import PartitionSpec as P

CREAL = 21843
UNIT = 16
MESH = pl.DeviceIdType.MESH
ANY = pl.BlockSpec(memory_space=pl.ANY)
VMEM = pl.BlockSpec(memory_space=pltpu.VMEM)
HBM = pl.BlockSpec(memory_space=pltpu.HBM)


def start_of(owner, n, units):
    return lax.div(owner * units, n)


def at_width(owner, n, units, run):
    base = units // n
    wide = start_of(owner + 1, n, units) - start_of(owner, n, units) > base
    pl.when(wide)(functools.partial(run, (base + 1) * UNIT))
    pl.when(jnp.logical_not(wide))(functools.partial(run, base * UNIT))


def exchange_kernel(
    n, units, feat, mean, scale, noise, logits, noise_out, held, part_out, part_in,
    send, recv, part_send, part_recv, nsend, nrecv, local, nlocal,
):
    me, cls = lax.axis_index("draw"), lax.axis_index("cls")
    half, rows = n // 2, mean.shape[1]
    mirror = lax.rem(me + half, n)
    base, spot = lax.div(me, half) * half, lax.rem(me, half)
    barrier = pltpu.get_barrier_semaphore()
    for k in range(1, n):
        pl.semaphore_signal(barrier, inc=1, device_id=(cls, lax.rem(me + k, n)), device_id_type=MESH)
    pl.semaphore_wait(barrier, n - 1)

    def remote(source, target, send_sem, recv_sem, device):
        return pltpu.make_async_remote_copy(
            source, target, send_sem, recv_sem, device_id=(cls, device), device_id_type=MESH
        )

    def noise_copy(slot, k, device):
        return remote(noise, noise_out.at[slot], nsend.at[k], nrecv.at[slot], device)

    def block(head, owner, width):
        start = pl.multiple_of(start_of(owner, n, units) * UNIT, UNIT)
        return (mean, scale)[head].at[pl.ds(start, width)]

    def block_copy(far, head, owner, k, source, device, act):
        at_width(
            owner, n, units,
            lambda w: act(
                remote(
                    block(head, owner, w), held.at[far, head, source, pl.ds(0, w)],
                    send.at[far, head, k], recv.at[far, head, source], device,
                )
            ),
        )

    def own_copy(far, head, act):
        owner = mirror if far else me
        at_width(
            owner, n, units,
            lambda w: act(
                pltpu.make_async_copy(
                    block(head, owner, w), held.at[far, head, spot, pl.ds(0, w)], local.at[far, head]
                )
            ),
        )

    def sends(far, head, act):
        for k in range(1, half):
            peer = base + lax.rem(spot + k, half)
            block_copy(far, head, lax.rem(peer + half, n) if far else peer, k, spot, peer, act)

    def columns_of(source):
        if rows % 128:
            return feat[source]
        return feat[:, pl.ds(pl.multiple_of(source * rows, rows), rows)]

    def arrive(far, head):
        owner = mirror if far else me
        for k in range(1, half):
            source = lax.rem(spot + half - k, half)
            block_copy(far, head, owner, k, source, base + source, lambda c: c.wait_recv())
        own_copy(far, head, lambda c: c.wait())
        total = None
        for source in range(half):
            term = lax.dot_general(
                held[far, head, source], columns_of(base + source), (((1,), (1,)), ((), ())),
                preferred_element_type=jnp.float32,
            )
            total = term if total is None else total + term
        return total

    def part_copy(head):
        return remote(part_out.at[head], part_in.at[head], part_send.at[head], part_recv.at[head], mirror)

    own_noise = pltpu.make_async_copy(noise, noise_out.at[me], nlocal)
    stages = [(1, 0), (1, 1), (0, 0), (0, 1)]
    sends(1, 0, lambda c: c.start())
    for k in range(1, n):
        noise_copy(me, k, lax.rem(me + k, n)).start()
    for far, head in stages[1:]:
        sends(far, head, lambda c: c.start())
    for far, head in stages:
        own_copy(far, head, lambda c: c.start())
    own_noise.start()
    for head in range(2):
        part_out[head] = arrive(1, head)
        part_copy(head).start()
    for head in range(2):
        logits[head] = arrive(0, head)
    for k in range(1, n):
        source = lax.rem(me + n - k, n)
        noise_copy(source, k, source).wait_recv()
    own_noise.wait()
    for head in range(2):
        part_copy(head).wait_recv()
        logits[head] = logits[head] + part_in[head]
    for far, head in stages:
        sends(far, head, lambda c: c.wait_send())
    for k in range(1, n):
        noise_copy(me, k, lax.rem(me + k, n)).wait_send()
    for head in range(2):
        part_copy(head).wait_send()


def gather_kernel(n, units, cot, out, send, recv, local):
    me, cls = lax.axis_index("draw"), lax.axis_index("cls")
    half = n // 2
    group, side = lax.div(me, 2), lax.rem(me, 2)
    partner = group * 2 + 1 - side
    split = units // n // 2 * UNIT
    pieces = [(head, part) for head in range(2) for part in range(2)]
    barrier = pltpu.get_barrier_semaphore()
    peers = [partner] + [lax.rem(group + k, half) * 2 + side for k in range(1, half)]
    for peer in peers:
        pl.semaphore_signal(barrier, inc=1, device_id=(cls, peer), device_id_type=MESH)
    pl.semaphore_wait(barrier, half)

    def source(piece, width):
        head, part = pieces[piece]
        return cot.at[head, pl.ds(split, width - split) if part else pl.ds(0, split)]

    def place(piece, owner, width):
        head, part = pieces[piece]
        start = start_of(owner, n, units) * UNIT + part * split
        return out.at[head, pl.ds(pl.multiple_of(start, UNIT), width - split if part else split)]

    def send_own(piece, owner, slot, device, act):
        at_width(
            owner, n, units,
            lambda w: act(
                pltpu.make_async_remote_copy(
                    source(piece, w), place(piece, owner, w), send.at[slot, piece], recv.at[owner, piece],
                    device_id=(cls, device), device_id_type=MESH,
                )
            ),
        )

    def forward(piece, owner, slot, act):
        at_width(
            owner, n, units,
            lambda w: act(
                pltpu.make_async_remote_copy(
                    place(piece, owner, w), place(piece, owner, w), send.at[slot, piece], recv.at[owner, piece],
                    device_id=(cls, partner), device_id_type=MESH,
                )
            ),
        )

    def own(piece, act):
        at_width(
            me, n, units,
            lambda w: act(pltpu.make_async_copy(source(piece, w), place(piece, me, w), local.at[piece])),
        )

    count = len(pieces)
    for piece in range(count):
        for k in range(1, half):
            send_own(piece, me, k, peers[k], lambda c: c.start())
        send_own(piece, me, 0, partner, lambda c: c.start())
    for piece in range(count):
        own(piece, lambda c: c.start())
    order = sorted(range(1, half), key=lambda k: min(k, half - k))
    for piece in range(count):
        for k in order:
            send_own(piece, peers[k], k, peers[k], lambda c: c.wait_recv())
            forward(piece, peers[k], half + k, lambda c: c.start())
    for piece in range(count):
        send_own(piece, partner, 0, partner, lambda c: c.wait_recv())
        for k in range(1, half):
            owner = lax.rem(group + k, half) * 2 + 1 - side
            forward(piece, owner, half + k, lambda c: c.wait_recv())
    for piece in range(count):
        for k in range(half):
            send_own(piece, me, k, peers[k], lambda c: c.wait_send())
        for k in range(1, half):
            forward(piece, peers[k], half + k, lambda c: c.wait_send())
        own(piece, lambda c: c.wait())


def merge(slots, count, softmax):
    if not softmax:
        total = slots[0]
        for i in range(1, count):
            total = total + slots[i]
        return total
    top = slots[0, 0]
    for i in range(1, count):
        top = jnp.maximum(top, slots[i, 0])
    total = jnp.zeros_like(top)
    for i in range(count):
        total = total + slots[i, 1] * jnp.exp(slots[i, 0] - top)
    return jnp.stack((top, total))


def reduce_kernel(counts, softmax, x, out, *scratch):
    levels = len(counts)
    slots, sends, recvs = scratch[:levels], scratch[levels : 2 * levels], scratch[2 * levels :]
    cls, draw = lax.axis_index("cls"), lax.axis_index("draw")

    def device(level, index):
        return (index, draw) if level == 0 else (cls, index)

    barrier = pltpu.get_barrier_semaphore()
    for level, n in enumerate(counts):
        me = (cls, draw)[level]
        for k in range(1, n):
            pl.semaphore_signal(
                barrier, inc=1, device_id=device(level, lax.rem(me + k, n)), device_id_type=MESH
            )
    pl.semaphore_wait(barrier, sum(counts) - levels)
    value = x[...]
    for level, n in enumerate(counts):
        me = (cls, draw)[level]
        held = slots[level]
        held[me] = value

        def copy(slot, k, target):
            return pltpu.make_async_remote_copy(
                held.at[slot], held.at[slot], sends[level].at[k], recvs[level].at[slot],
                device_id=device(level, target), device_id_type=MESH,
            )

        for k in range(1, n):
            copy(me, k, lax.rem(me + k, n)).start()
        for k in range(1, n):
            source = lax.rem(me + n - k, n)
            copy(source, k, source).wait_recv()
        for k in range(1, n):
            copy(me, k, lax.rem(me + k, n)).wait_send()
        value = merge(held, n, softmax)
    if softmax:
        out[...] = value[0] + jnp.log(value[1])
    else:
        out[...] = value


def params(collective_id, grant=32):
    return pltpu.CompilerParams(
        collective_id=collective_id, has_side_effects=True, vmem_limit_bytes=grant * 2**20
    )


def reduce_over(x, counts, softmax, collective_id):
    shape = x.shape[1:] if softmax else x.shape
    return pl.pallas_call(
        functools.partial(reduce_kernel, counts, softmax),
        out_shape=jax.ShapeDtypeStruct(shape, jnp.float32),
        in_specs=[VMEM],
        out_specs=VMEM,
        scratch_shapes=[pltpu.VMEM((n,) + x.shape, jnp.float32) for n in counts]
        + [pltpu.SemaphoreType.DMA((n,)) for n in counts]
        + [pltpu.SemaphoreType.DMA((n,)) for n in counts],
        compiler_params=params(collective_id),
    )(x)


def on_device(features, mean_head, scale_head, factor, noise, labels):
    rows, columns = mean_head.shape
    batch = features.shape[0]
    n, ncls = lax.axis_size("draw"), lax.axis_size("cls")
    me = lax.axis_index("draw")
    units = columns // UNIT
    tile = -(-units // n) * UNIT
    own, rank = noise.shape[0], noise.shape[2]
    draws = own * n
    mean_rows, scale_rows = mean_head.T, scale_head.T
    half = n // 2
    feat = features.reshape(batch, n, rows).transpose(1, 0, 2) if rows % 128 else features

    heads, noise_t = pl.pallas_call(
        functools.partial(exchange_kernel, n, units),
        out_shape=(
            jax.ShapeDtypeStruct((2, tile, batch), jnp.float32),
            jax.ShapeDtypeStruct((n, own, rank, batch), jnp.bfloat16),
        ),
        in_specs=[VMEM] + [ANY] * 3,
        out_specs=(VMEM, ANY),
        scratch_shapes=[
            pltpu.VMEM((2, 2, half, tile, rows), jnp.bfloat16),
            pltpu.VMEM((2, tile, batch), jnp.float32),
            pltpu.VMEM((2, tile, batch), jnp.float32),
            pltpu.SemaphoreType.DMA((2, 2, half)),
            pltpu.SemaphoreType.DMA((2, 2, half)),
            pltpu.SemaphoreType.DMA((2,)),
            pltpu.SemaphoreType.DMA((2,)),
            pltpu.SemaphoreType.DMA((n,)),
            pltpu.SemaphoreType.DMA((n,)),
            pltpu.SemaphoreType.DMA((2, 2)),
            pltpu.SemaphoreType.DMA,
        ],
        compiler_params=params(0),
    )(feat, mean_rows, scale_rows, noise.transpose(0, 2, 1))

    first = start_of(me, n, units) * UNIT
    width = start_of(me + 1, n, units) * UNIT - first
    offsets = jnp.arange(tile, dtype=jnp.int32)[:, None]
    valid = offsets < width
    class_ids = lax.axis_index("cls") * columns + first + offsets
    shift = jnp.where(class_ids >= CREAL, 30000.0, 0.0).astype(jnp.float32)
    my_factor = lax.dynamic_slice_in_dim(factor.T, first, tile, 1)
    my_labels = jnp.where(valid, lax.dynamic_slice_in_dim(labels.T, first, tile, 0), 0.0)

    mean_logit, scale_pre = heads[0], heads[1]
    scale_pre = jnp.where(valid, scale_pre, 0.0)
    spread = jax.nn.softplus(scale_pre)
    lowrank = jnp.einsum(
        "rc,srb->scb", my_factor, noise_t.reshape(draws, rank, batch), preferred_element_type=jnp.float32
    )
    logits = mean_logit[None] + spread[None] * lowrank - shift[None]
    logits = jnp.where(valid[None], logits, -1e30)
    local_top = jnp.max(logits, axis=1)
    local_total = jnp.sum(jnp.exp(logits - local_top[:, None]), axis=1)
    lse = reduce_over(jnp.stack((local_top, local_total)), (ncls, n), True, 1)
    log_prob = logits - lse[:, None]
    best = jnp.max(log_prob, axis=0)
    risen = jnp.exp(log_prob - best[None])
    inverse = 1.0 / jnp.sum(risen, axis=0)
    weight = my_labels * inverse
    label_dot = reduce_over(jnp.sum(weight[None] * risen, axis=1), (ncls, n), False, 2)
    logit_cot = risen * ((jnp.exp(best) / batch)[None] * label_dot[:, None] - (weight / batch)[None])
    dmean = jnp.sum(logit_cot, axis=0)
    dspread = jnp.sum(logit_cot * lowrank, axis=0)
    cots = jnp.stack((dmean, dspread * jax.nn.sigmoid(scale_pre))).astype(jnp.bfloat16)

    gathered = pl.pallas_call(
        functools.partial(gather_kernel, n, units),
        out_shape=jax.ShapeDtypeStruct((2, columns, batch), jnp.bfloat16),
        in_specs=[ANY],
        out_specs=ANY,
        scratch_shapes=[
            pltpu.SemaphoreType.DMA((n, 4)),
            pltpu.SemaphoreType.DMA((n, 4)),
            pltpu.SemaphoreType.DMA((4,)),
        ],
        compiler_params=params(3),
    )(cots)
    mean_cot, scale_cot = gathered[0], gathered[1]
    my_columns = lax.dynamic_slice_in_dim(features, me * rows, rows, 1)
    over_classes = (((0,), (0,)), ((), ()))
    feature_part = lax.dot_general(
        mean_cot, mean_rows, over_classes, preferred_element_type=jnp.float32
    ) + lax.dot_general(scale_cot, scale_rows, over_classes, preferred_element_type=jnp.float32)
    mean_grad = jnp.dot(mean_cot, my_columns, preferred_element_type=jnp.float32).T
    scale_grad = jnp.dot(scale_cot, my_columns, preferred_element_type=jnp.float32).T
    feature_grad, step = feature_part, 1
    while step < ncls:
        feature_grad = feature_grad + lax.ppermute(feature_grad, "cls", [(i, i ^ step) for i in range(ncls)])
        step *= 2
    return (mean_grad, scale_grad, feature_grad)


GRAIN = 64
SMALL = 32
FINE = 1
NEG = -1e30
LOG2E = 1.4426950408889634


def when(cond, fn):
    pl.when(cond)(fn)


class Plan:
    def __init__(self, batch, rows, columns, rank):
        self.batch, self.rows, self.columns, self.rank = batch, rows, columns, rank
        units = columns // UNIT
        edges = [q * units // 4 * UNIT for q in range(5)]
        widest = max(b - a for a, b in zip(edges, edges[1:]))
        self.width = -(-widest // SMALL) * SMALL
        self.padded = -(-self.width // 128) * 128
        self.full = self.width // GRAIN - 1
        self.chunks = self.full + (self.width - self.full * GRAIN) // SMALL
        self.side = self.width // 2
        self.side_full = self.side // GRAIN
        self.rest = self.side - self.side_full * GRAIN
        self.steps = self.side_full + (self.rest > 0)
        self.units = units
        self.extra = max(0, edges[3] + self.width - columns)
        self.starts = edges[:3] + [edges[3] - self.extra]
        self.sizes = [b - a for a, b in zip(self.starts, self.starts[1:] + [columns])]

    def start(self, q):
        return pl.multiple_of(lax.div(q * self.units, 4) * UNIT - self.extra * lax.div(q, 3), UNIT)

    def chunk(self, k, run):
        def tail():
            run(SMALL, pl.multiple_of(self.full * GRAIN + (k - self.full) * SMALL, SMALL))
        when(k < self.full, lambda: run(GRAIN, pl.multiple_of(k * GRAIN, GRAIN)))
        when(k >= self.full, tail)

    def step(self, k, run):
        when(k < self.side_full, lambda: run(GRAIN, pl.multiple_of(k * GRAIN, GRAIN)))
        if self.rest:
            when(k >= self.side_full, lambda: run(self.rest, self.side_full * GRAIN))

    def size(self, q):
        after = lax.div((q + 1) * self.units, 4) * UNIT - self.extra * (lax.div(q + 1, 3) - lax.div(q + 1, 4))
        return after - self.start(q)


def tree(fn, items):
    items = list(items)
    while len(items) > 1:
        items = [fn(*items[i : i + 2]) if i + 1 < len(items) else items[i] for i in range(0, len(items), 2)]
    return items[0]


def softmax_kernel(
    plan, draws, ahead, lag_in, lag_out, relay_in, relay_out,
    feat, mean, scale, factor, noise, labels, cot, part,
    wbuf, sums, arrived, zbuf, low, gate, weight, peak, fcols, fturn, fac, fq, nb, nmat, lab, top, total, lseb, dotb,
    red, whole, acc, acc_in,
    lsem, ysend, yrecv, zsend, zrecv, nsend, nrecv, nstage, nstage_r, rsend, rrecv,
    gzs, gzr, gys, gyr, wsem, csend, crecv,
):
    me, cls = lax.axis_index("draw"), lax.axis_index("cls")
    z, y = lax.div(me, 2), lax.rem(me, 2)
    xx, core = lax.div(cls, 2), lax.rem(cls, 2)
    half = lax.div(z, 2)
    outer = (z == 0) | (z == 3)
    inner = jnp.logical_not(outer)
    edge, mid = 3 * half, 1 + half
    across = 2 - half
    batch, rows, chunks, steps = plan.batch, plan.rows, plan.chunks, plan.steps
    own_q = half * 2 + y
    start = plan.start(own_q)
    valid_rows = plan.size(own_q)
    plane = cls * 2 + y
    heads = (mean, scale)

    def at(zi, yi):
        return (cls, zi * 2 + yi)

    def in_plane(p):
        return (lax.div(p, 2), z * 2 + lax.rem(p, 2))

    barrier = pltpu.get_barrier_semaphore()
    for k in range(1, 8):
        pl.semaphore_signal(barrier, inc=1, device_id=in_plane(lax.rem(plane + k, 8)), device_id_type=MESH)
    for k in range(1, 4):
        pl.semaphore_signal(barrier, inc=1, device_id=at(lax.rem(z + k, 4), y), device_id_type=MESH)

    @pl.when(outer)
    def _():
        for k in range(1, 8):
            p = lax.rem(plane + k, 8)
            pl.semaphore_signal(
                barrier, inc=1, device_id=(lax.div(p, 2), (3 - z) * 2 + lax.rem(p, 2)), device_id_type=MESH
            )

    def remote(src, dst, s, r, device):
        return pltpu.make_async_remote_copy(src, dst, s, r, device_id=device, device_id_type=MESH)

    def local_own(e, h):
        return pltpu.make_async_copy(
            heads[h].at[pl.ds(plan.start(e * 2 + y), plan.width)],
            wbuf.at[e, h, :, pl.ds(pl.multiple_of(y * rows, rows), rows)],
            lsem.at[e * 2 + h],
        )

    feat_copy = pltpu.make_async_copy(
        feat.at[:, pl.ds(pl.multiple_of(z * 2 * rows, 2 * rows), 2 * rows)], fcols, lsem.at[4]
    )
    factor_copy = pltpu.make_async_copy(factor, fac, lsem.at[5])
    label_copy = pltpu.make_async_copy(labels.at[pl.ds(start, plan.width)], lab, lsem.at[6])
    noise_own = pltpu.make_async_copy(
        noise.at[core], nb.at[core, y, z], lsem.at[7]
    )

    def y_copy(e, h, k, grain, row):
        return remote(
            heads[h].at[pl.ds(plan.start(e * 2 + 1 - y) + row, grain)],
            wbuf.at[e, h, pl.ds(row, grain), pl.ds(pl.multiple_of(y * rows, rows), rows)],
            ysend, yrecv.at[k], at(z, 1 - y),
        )

    def y_landed(k, grain, row):
        block = wbuf.at[:, :, pl.ds(row, grain), pl.ds(pl.multiple_of((1 - y) * rows, rows), rows)]
        return remote(block, block, ysend, yrecv.at[k], at(z, 1 - y))

    def y_sent():
        block = wbuf.at[:, :, :, pl.ds(pl.multiple_of(y * rows, rows), rows)]
        return remote(block, block, ysend, yrecv.at[0], at(z, 1 - y))

    def y_start(k):
        def run(grain, row):
            for e in range(2):
                for h in range(2):
                    y_copy(e, h, k, grain, row).start()
        plan.chunk(k, run)

    def z_copy(e, k, part, grain, row, target):
        fine = grain // FINE
        block = pl.ds(pl.multiple_of(row + part * fine, fine), fine)
        return remote(
            sums.at[e, :, block], arrived.at[e, :, block], zsend.at[e], zrecv.at[e, k, part], at(target, y)
        )

    def noise_copy(e, source):
        return remote(
            noise.at[core], nb.at[core, y, source], nsend.at[e], nrecv.at[source], at(3 * e, y),
        )

    sibling = (xx * 2 + 1 - core, me)

    def stage(n, far_side):
        if n == 0:
            block = nb.at[core, 1 - y if far_side else y]
            return remote(block, block, nstage.at[0], nstage_r.at[0], at(z, 1 - y))
        block = nb.at[1 - core if far_side else core]
        return remote(block, block, nstage.at[1], nstage_r.at[1], sibling)

    feat_copy.start()
    when(outer, lambda: pl.semaphore_wait(barrier, 17))
    when(inner, lambda: pl.semaphore_wait(barrier, 10))
    y_start(0)
    for e in range(2):
        for h in range(2):
            local_own(e, h).start()
    noise_own.start()
    for k in range(1, ahead):
        y_start(k)
    for e in range(2):
        when(z != 3 * e, lambda: noise_copy(e, z).start())
    factor_copy.start()
    fq[...] = jnp.zeros_like(fq)
    nmat[...] = jnp.zeros_like(nmat)
    top[...] = jnp.full_like(top, NEG)
    total[...] = jnp.zeros_like(total)
    acc[...] = jnp.zeros_like(acc)
    feat_copy.wait()
    fturn[...] = fcols[...].T
    for e in range(2):
        for h in range(2):
            local_own(e, h).wait()

    def lanes(s):
        return slice(s * batch, (s + 1) * batch)

    def first_pass(grain, row):
        @pl.when(lax.rem(row, 128) == 0)
        def _():
            span = pl.ds(pl.multiple_of(row, 128), 128)
            low[span] = lax.dot_general(
                fq[:, span], nmat[...], (((0,), (0,)), ((), ())), preferred_element_type=jnp.float32
            )
        rows_k = pl.ds(row, grain)
        logit, pre = sums[half, 0, rows_k], sums[half, 1, rows_k]
        offset = row + lax.broadcasted_iota(jnp.int32, (grain, batch), 0)
        valid = offset < valid_rows
        ids = cls * plan.columns + start + offset
        shifted = logit - jnp.where(ids >= CREAL, 30000.0, 0.0)
        fade = jnp.exp(-jnp.abs(pre))
        spread = jnp.maximum(pre, 0.0) + jnp.log1p(fade)
        gate[rows_k] = jnp.where(pre >= 0, 1.0, fade) / (1.0 + fade)
        shifted = jnp.where(valid, shifted * LOG2E, NEG)
        spread = jnp.where(valid, spread * LOG2E, 0.0)
        for s in range(draws):
            value = shifted + spread * low[rows_k, lanes(s)]
            zbuf[rows_k, lanes(s)] = value
            blocks = [value[i * 8 : i * 8 + 8] for i in range(grain // 8)]
            old = top[:, lanes(s)]
            new = jnp.maximum(old, tree(jnp.maximum, blocks))
            grown = tree(jnp.add, [jnp.exp2(b - new) for b in blocks])
            total[:, lanes(s)] = total[:, lanes(s)] * jnp.exp2(old - new) + grown
            top[:, lanes(s)] = new

    e_first, e_second = 1 - half, half

    def noise_stage(i):
        @pl.when(i == 2)
        def _():
            for k in range(4):
                when(z != k, lambda: noise_copy(half, k).wait_recv())
            noise_own.wait()
            stage(0, False).start()

        @pl.when(i == 4)
        def _():
            stage(0, True).wait_recv()
            stage(1, False).start()

        when(i == 10, label_copy.start)

        @pl.when(i == 3)
        def _():
            factor_copy.wait()
            for q in range(4):
                def pick(q=q):
                    fq[: plan.rank, : plan.width] = fac[:, plan.starts[q] : plan.starts[q] + plan.width]
                when(own_q == q, pick)

        @pl.when(i == 5)
        def _():
            stage(1, True).wait_recv()
            for j in range(2):
                for yi in range(2):
                    for zi in range(4):
                        nmat[: plan.rank, lanes((j * 2 + yi) * 4 + zi)] = nb[j, yi, zi]

    def own_sums(i, grain, row):
        when(i + ahead < chunks, lambda: y_start(i + ahead))
        y_landed(i, grain, row).wait_recv()
        block = pl.ds(row, grain)
        lhs = jnp.concatenate([wbuf[e, h, block] for e in range(2) for h in range(2)], axis=0)
        value = lax.dot_general(
            lhs, fturn[...], (((1,), (0,)), ((), ())), preferred_element_type=jnp.float32
        )
        sums[:, :, block] = value.reshape(2, 2, grain, batch)

    def add_arrived(e, k, part, grain, row):
        z_copy(e, k, part, grain, row, mid).wait_recv()
        fine = grain // FINE
        block = pl.ds(pl.multiple_of(row + part * fine, fine), fine)
        sums[e, :, block] = sums[e, :, block] + arrived[e, :, block]

    def forward_inner(i, carry):
        def first(grain, row):
            own_sums(i, grain, row)
            for part in range(FINE):
                add_arrived(e_first, i, part, grain, row)
                z_copy(e_first, i, part, grain, row, across).start()

        def second(grain, row):
            for part in range(FINE):
                add_arrived(e_second, i - lag_in, part, grain, row)
                z_copy(e_second, i - lag_in, part, grain, row, edge).start()

        when(i < chunks, lambda: plan.chunk(i, first))
        when(i >= lag_in, lambda: plan.chunk(i - lag_in, second))
        return carry

    def forward_outer(i, carry):
        def first(grain, row):
            own_sums(i, grain, row)
            for part in range(FINE):
                z_copy(e_first, i, part, grain, row, mid).start()

        def second(grain, row):
            for part in range(FINE):
                add_arrived(e_second, i - lag_out, part, grain, row)
            first_pass(grain, row)

        when(i < chunks, lambda: plan.chunk(i, first))
        noise_stage(i)
        when(i >= lag_out, lambda: plan.chunk(i - lag_out, second))
        return carry

    @pl.when(inner)
    def _():
        lax.fori_loop(0, chunks + lag_in, forward_inner, 0)

    @pl.when(outer)
    def _():
        lax.fori_loop(0, chunks + lag_out, forward_outer, 0)

    whole_copies = [pltpu.make_async_copy(heads[h], whole.at[h], wsem.at[h]) for h in range(2)]
    for copy in whole_copies:
        copy.start()
    when(outer, label_copy.wait)

    @pl.when(inner)
    def _():
        factor_copy.wait()
        noise_own.wait()

    spot = half * 8 + plane

    def end_device(p):
        return (lax.div(lax.rem(p, 8), 2), lax.div(p, 8) * 6 + lax.rem(p, 2))

    def red_copy(kind, slot, k, p):
        return remote(red.at[kind, slot], red.at[kind, slot], rsend.at[kind, k], rrecv.at[kind, slot], end_device(p))

    def log_merge(parts):
        best = tree(jnp.maximum, parts)
        return best + LOG2E * jnp.log(tree(jnp.add, [jnp.exp2(p - best) for p in parts]))

    def fan_out(target, value):
        for s in range(draws):
            target[:, lanes(s)] = jnp.broadcast_to(value[s : s + 1], (8, batch))

    def reduce_all(kind, merge):
        for k in range(8, 16):
            red_copy(kind, spot, k, lax.rem(spot + k, 16)).start()
        for k in range(1, 8):
            red_copy(kind, spot, k, lax.rem(spot + k, 16)).start()
        for k in range(1, 16):
            source = lax.rem(spot + 16 - k, 16)
            red_copy(kind, source, k, source).wait_recv()
        return merge([red[kind, p] for p in range(16)])

    @pl.when(outer)
    def _():
        for s in range(draws):
            m = top[:, lanes(s)]
            best = jnp.max(m, axis=0, keepdims=True)
            size = jnp.sum(total[:, lanes(s)] * jnp.exp2(m - best), axis=0, keepdims=True)
            red[0, spot, s : s + 1, :] = best + LOG2E * jnp.log(size)
        fan_out(lseb, reduce_all(0, log_merge))

        def second_pass(r, sums_in):
            block = pl.ds(pl.multiple_of(r * 8, 8), 8)
            logs = [zbuf[block, lanes(s)] - lseb[:, lanes(s)] for s in range(draws)]
            best = tree(jnp.maximum, logs)
            risen = [jnp.exp2(v - best) for v in logs]
            offset = r * 8 + lax.broadcasted_iota(jnp.int32, (8, batch), 0)
            share = jnp.where(offset < valid_rows, lab[block] / tree(jnp.add, risen), 0.0)
            peak[block] = jnp.exp2(best) * (1.0 / batch)
            weight[block] = share * (1.0 / batch)
            for s in range(draws):
                zbuf[block, lanes(s)] = risen[s]
            return tuple(a + share * v for a, v in zip(sums_in, risen))

        dots = lax.fori_loop(
            0, plan.width // 8, second_pass, tuple(jnp.zeros((8, batch), jnp.float32) for _ in range(draws)),
            unroll=4,
        )
        for s in range(draws):
            red[1, spot, s : s + 1, :] = jnp.sum(dots[s], axis=0, keepdims=True)
        fan_out(dotb, reduce_all(1, lambda parts: tree(jnp.add, parts)))

    def cot_chunk(grain, row):
        def body(b, carry):
            means, scales = [], []
            for part in range(2):
                block = pl.ds(pl.multiple_of(row + b * 16 + part * 8, 8), 8)
                eb, wt = peak[block], weight[block]
                terms = [zbuf[block, lanes(s)] * (eb * dotb[:, lanes(s)] - wt) for s in range(draws)]
                means.append(tree(jnp.add, terms))
                scales.append(
                    tree(jnp.add, [t * low[block, lanes(s)] for s, t in enumerate(terms)]) * gate[block]
                )
            inside = pl.ds(pl.multiple_of(row + b * 16, 16), 16)
            cot[own_q, inside, :batch] = jnp.concatenate(means, axis=0).astype(jnp.bfloat16)
            cot[own_q, inside, batch:] = jnp.concatenate(scales, axis=0).astype(jnp.bfloat16)
            return carry
        lax.fori_loop(0, grain // 16, body, 0)

    side = plan.side

    def gz(e, kind, k, grain, row, target):
        block = cot.at[e * 2 + (y if kind < 2 else 1 - y), pl.ds(row + (side if kind == 1 else 0), grain)]
        return remote(block, block, gzs.at[e, kind], gzr.at[e, kind, k], at(target, y))

    def gy(e, kind, k, grain, row, line):
        block = cot.at[e * 2 + line, pl.ds(row + side * kind, grain)]
        return remote(block, block, gys.at[e, kind], gyr.at[e, kind, k], at(z, 1 - y))

    def relay(e, i, target):
        def pass_on(kind, k, grain, row):
            gz(e, kind, k, grain, row, mid).wait_recv()
            if target is not None:
                gz(e, kind, k, grain, row, target).start()

        def early(grain, row):
            pass_on(1, i, grain, row)
            gy(e, 1, i, grain, row, y).start()

        def late(grain, row):
            pass_on(0, i - steps, grain, row)
            pass_on(2, i - steps, grain, row)

        when((i >= 0) & (i < steps), lambda: plan.step(i, early))
        when((i >= steps) & (i < 2 * steps), lambda: plan.step(i - steps, late))

    def absorb(j, grain, row):
        for e in range(2):
            gy(e, 1, j, grain, row, 1 - y).wait_recv()
        for kind in range(2):
            for h in range(2):
                lhs = jnp.concatenate(
                    [cot[q, pl.ds(row + kind * side, grain), h * batch : (h + 1) * batch] for q in range(4)], axis=0
                )
                rhs = jnp.concatenate(
                    [
                        whole[h, pl.ds(pl.multiple_of(plan.starts[q] + kind * side + row, UNIT), grain)]
                        for q in range(4)
                    ],
                    axis=0,
                )
                acc[...] += lax.dot_general(
                    lhs, rhs, (((0,), (0,)), ((), ())), preferred_element_type=jnp.float32
                )

    for copy in whole_copies:
        copy.wait()

    def gather(i, carry):
        @pl.when(outer)
        def _():
            def early(grain, row):
                cot_chunk(grain, row + side)
                gz(half, 1, i, grain, row, mid).start()
                cot_chunk(grain, row)
                gy(half, 0, i, grain, row, y).start()

            def late(grain, row):
                k = i - steps
                gz(half, 0, k, grain, row, mid).start()
                gy(half, 0, k, grain, row, 1 - y).wait_recv()
                gz(half, 2, k, grain, row, mid).start()
                gy(half, 1, k, grain, row, y).start()

            when(i < steps, lambda: plan.step(i, early))
            when((i >= steps) & (i < 2 * steps), lambda: plan.step(i - steps, late))
            relay(1 - half, i - relay_out, None)

        @pl.when(inner)
        def _():
            relay(half, i, across)
            relay(1 - half, i - relay_in, edge)
        last = i - relay_out - steps
        when(last >= 0, lambda: plan.step(last, functools.partial(absorb, last)))
        return carry

    lax.fori_loop(0, 2 * steps + relay_out, gather, 0)

    twin = remote(acc, acc_in, csend, crecv, sibling)
    twin.start()

    def relayed(e, kind):
        block = cot.at[e * 2, pl.ds(kind % 2 * side, side)]
        return remote(block, block, gzs.at[e, kind], gzr.at[e, kind, 0], at(mid, y))

    def crossed(e, kind):
        block = cot.at[e * 2, pl.ds(kind * side, side)]
        return remote(block, block, gys.at[e, kind], gyr.at[e, kind, 0], at(z, 1 - y))

    for kind in range(3):
        relayed(half, kind).wait_send()
        when(inner, lambda: relayed(1 - half, kind).wait_send())
    for e in range(2):
        crossed(e, 1).wait_send()
    when(outer, lambda: crossed(half, 0).wait_send())
    def z_sent(e):
        return remote(arrived.at[e], arrived.at[e], zsend.at[e], zrecv.at[e, 0, 0], at(mid, y))

    y_sent().wait_send()
    z_sent(e_first).wait_send()
    when(inner, lambda: z_sent(e_second).wait_send())
    twin.wait_recv()
    part[...] = acc[...] + acc_in[...]
    twin.wait_send()
    for e in range(2):
        when(z != 3 * e, lambda: noise_copy(e, z).wait_send())

    @pl.when(outer)
    def _():
        for n in range(2):
            stage(n, False).wait_send()
        for kind in range(2):
            for k in range(1, 16):
                red_copy(kind, spot, k, lax.rem(spot + k, 16)).wait_send()


def head_kernel(plan, cot, feat_in, mean_out, scale_out, cols_in, stage, loads, sems):
    batch, rows = plan.batch, plan.rows
    me = lax.axis_index("draw")
    feat_copy = pltpu.make_async_copy(
        feat_in.at[:, pl.ds(pl.multiple_of(me * rows, rows), rows)], cols_in, loads
    )

    feat_copy.start()
    feat_copy.wait()
    cols = cols_in[...]
    blank = jnp.zeros_like(cols)
    rhs = jnp.concatenate(
        [jnp.concatenate([cols, blank], axis=1), jnp.concatenate([blank, cols], axis=1)], axis=0
    )
    outs = (mean_out, scale_out)
    copies = []
    for q in range(4):
        size, first = plan.sizes[q], plan.starts[q]
        for part in range(2):
            begin = part * plan.side
            count = min(plan.side, size - begin)
            value = jnp.dot(cot[q, begin : begin + count], rhs, preferred_element_type=jnp.float32)
            spot = slice(first + begin, first + begin + count)
            for h in range(2):
                stage[h, spot] = value[:, h * rows : (h + 1) * rows]
                copy = pltpu.make_async_copy(stage.at[h, spot], outs[h].at[spot], sems.at[h, q * 2 + part])
                copy.start()
                copies.append(copy)
    for copy in copies:
        copy.wait()


def in_hbm(x):
    return pltpu.with_memory_space_constraint(x, pltpu.HBM)


def ends_on_device(features, mean_head, scale_head, factor, noise, labels):
    rows, columns = mean_head.shape
    batch = features.shape[0]
    own, rank = noise.shape[0], noise.shape[2]
    draws = own * 8
    plan = Plan(batch, rows, columns, rank)
    width, chunks, steps = plan.width, plan.chunks, plan.steps
    mean_rows, scale_rows = mean_head.T, scale_head.T
    noise_t = noise.transpose(0, 2, 1)
    dma = pltpu.SemaphoreType.DMA
    f32, bf16 = jnp.float32, jnp.bfloat16
    cot, part = pl.pallas_call(
        functools.partial(softmax_kernel, plan, draws, 3, 3, 9, 3, 10),
        out_shape=(
            jax.ShapeDtypeStruct((4, width, 2 * batch), bf16),
            jax.ShapeDtypeStruct((batch, rows), f32),
        ),
        in_specs=[HBM] * 4 + [ANY, HBM],
        out_specs=(VMEM, VMEM),
        scratch_shapes=[
            pltpu.VMEM((2, 2, width, 2 * rows), bf16),
            pltpu.VMEM((2, 2, width, batch), f32),
            pltpu.VMEM((2, 2, width, batch), f32),
            pltpu.VMEM((width, draws * batch), f32),
            pltpu.VMEM((plan.padded, draws * batch), f32),
            pltpu.VMEM((width, batch), f32),
            pltpu.VMEM((width, batch), f32),
            pltpu.VMEM((width, batch), f32),
            pltpu.VMEM((batch, 2 * rows), bf16),
            pltpu.VMEM((2 * rows, batch), bf16),
            pltpu.VMEM((rank, columns), bf16),
            pltpu.VMEM((64, plan.padded), bf16),
            pltpu.VMEM((2, 2, 4, rank, batch), bf16),
            pltpu.VMEM((64, draws * batch), bf16),
            pltpu.VMEM((width, batch), f32),
            pltpu.VMEM((8, draws * batch), f32),
            pltpu.VMEM((8, draws * batch), f32),
            pltpu.VMEM((8, draws * batch), f32),
            pltpu.VMEM((8, draws * batch), f32),
            pltpu.VMEM((2, 16, draws, batch), f32),
            pltpu.VMEM((2, columns, rows), bf16),
            pltpu.VMEM((batch, rows), f32),
            pltpu.VMEM((batch, rows), f32),
            dma((8,)),
            dma,
            dma((chunks,)),
            dma((2,)),
            dma((2, chunks, FINE)),
            dma((2,)),
            dma((4,)),
            dma((2,)),
            dma((2,)),
            dma((2, 16)),
            dma((2, 16)),
            dma((2, 3)),
            dma((2, 3, steps)),
            dma((2, 2)),
            dma((2, 2, steps)),
            dma((2,)),
            dma,
            dma,
        ],
        compiler_params=params(0, 50),
    )(in_hbm(features), in_hbm(mean_rows), in_hbm(scale_rows), in_hbm(factor.T), noise_t, in_hbm(labels.T))

    other = lax.ppermute(part, "cls", [(i, i ^ 2) for i in range(4)])
    mean_grad, scale_grad = pl.pallas_call(
        functools.partial(head_kernel, plan),
        out_shape=(jax.ShapeDtypeStruct((columns, rows), f32),) * 2,
        in_specs=[VMEM, HBM],
        out_specs=(HBM, HBM),
        scratch_shapes=[
            pltpu.VMEM((batch, rows), bf16),
            pltpu.VMEM((2, columns, rows), f32),
            dma,
            dma((2, 8)),
        ],
        compiler_params=pltpu.CompilerParams(vmem_limit_bytes=32 * 2**20),
        cost_estimate=pl.CostEstimate(
            flops=8 * columns * batch * rows, bytes_accessed=16 * columns * rows, transcendentals=0
        ),
    )(cot, features)
    return (mean_grad.T, scale_grad.T, part + other)


def solution(mesh):
    ends = dict(mesh.shape) == {"cls": 4, "draw": 8}
    return jax.shard_map(
        ends_on_device if ends else on_device,
        mesh=mesh,
        in_specs=(
            P(),
            P("draw", "cls"),
            P("draw", "cls"),
            P("cls", None),
            P("draw", None, None),
            P(None, "cls"),
        ),
        out_specs=(P("draw", "cls"), P("draw", "cls"), P(None, "draw")),
        check_vma=False,
    )
```
